512 devices in a mesh: branch: 4 (over y_hi, core), segment: 8 (over y_lo, x), tp: 16 (over z).
Axes of the slice: x: 4, y: 4 (y_hi: 2, y_lo: 2; y = y_hi * 2 + y_lo), z: 16, core: 2. Of those that a mesh axis runs over, the one named last changes fastest.
Arguments:
- rollout: bfloat16 [2304, 8192], P(('branch', 'segment')), may hold values from -6 to 6
- send_rows: int32 [2304], P(('branch', 'segment')), may hold values from 0 to 71, as said below
- seq_lengths: int32 [8, 6], P('segment'), may hold values from 1 to 144, 288 in all within a row
- attn_gain: bfloat16 [4, 8192], P('branch'), may hold values from 0.099609375 to 1.8984375
- w_query: bfloat16 [4, 8192, 8192], P('branch', 'segment', 'tp'), may hold values from -1 to 1
- w_keyval: bfloat16 [4, 8192, 2048], P('branch', 'segment', 'tp'), may hold values from -1 to 1
- head_weight: bfloat16 [4, 8192], P('branch', 'tp'), may hold values from -0.0625 to 0.0625
- head_attn: bfloat16 [4, 8192], P('branch', 'tp'), may hold values from -0.25 to 0.25
Outputs:
- scores: float32 [4, 2304], P(None, ('branch', 'segment'))
The draws below stay inside these ranges and needn't reach their ends.
Inputs may be any that keep to these rules, and one draw needn't show every extreme that they name: `send_rows`: each aligned block of 72 entries holds every number of 0 to 71 once.
All inputs are finite; a program needn't handle non-finite values.
Results may differ from the reference program's by a relative error of at most 0.006.
Values may be sent and summed in bfloat16 or wider, within the bound.
A program may use at most 128 MiB of HBM per device.

```python
import math
import jax
import jax.numpy as jnp
import numpy as np
from jax import lax

D = 8192
HEAD = 128
HEADS = 64
KV_HEADS = 8
PACK = 288
SEQ_PACK = 6
MAXLEN = 144
SECTIONS = 4
PACKS = 8
TOKENS = 2304
GEN_DEV = 72
PIECE = 9


def draw_send_rows(key, part):
    block_keys = jax.random.split(key, TOKENS // GEN_DEV)
    shuffled = jax.vmap(lambda one_key: jax.random.permutation(one_key, GEN_DEV))(block_keys)
    return shuffled.reshape(TOKENS).astype(jnp.int32)


def noise_weights(key, columns):
    scale = D ** (-0.5)
    values = jax.random.normal(key, (SECTIONS, D, columns), jnp.float32) * scale
    return jnp.clip(values, -6.0 * scale, 6.0 * scale)


def draw_rollout(key, part):
    noise_key = jax.random.fold_in(key, 1)
    rows = jax.random.normal(noise_key, (TOKENS, D), jnp.float32)
    return jnp.clip(rows, -6.0, 6.0).astype(jnp.bfloat16)


def draw_w_query(key, part):
    columns = HEADS * HEAD
    values = noise_weights(jax.random.fold_in(key, 5), columns)
    return jnp.clip(values, -1.0, 1.0).astype(jnp.bfloat16)


def draw_w_keyval(key, part):
    columns = 2 * KV_HEADS * HEAD
    values = noise_weights(jax.random.fold_in(key, 6), columns)
    return jnp.clip(values, -1.0, 1.0).astype(jnp.bfloat16)


def levels(own_key, shape, cuts, smallest, high):
    factor_of, own = 1.0, jax.random.fold_in(own_key, 6)
    for position, parts in cuts:
        draws = jnp.exp(jax.random.uniform(jax.random.fold_in(own, position), (parts,), jnp.float32, smallest / len(cuts), high / len(cuts)))
        factor_of = factor_of * jnp.repeat(draws, shape[position] // parts).reshape([-1 if axis == position else 1 for axis in range(len(shape))])
    return factor_of


def length_profile(number_of, total, bound, lean):
    portions = [(1 << 20) // math.isqrt(rank ** lean) + 1 for rank in range(2, number_of + 1)]
    surplus, holding = total - bound - (number_of - 1), [1] * (number_of - 1)
    while surplus > 0:
        movable = [i for i in range(number_of - 1) if holding[i] < bound]
        pool, left = sum([portions[i] for i in movable]), surplus
        for i in movable:
            extra = min(bound - holding[i], max(1, left * portions[i] // pool), surplus)
            holding[i] = holding[i] + extra
            surplus = surplus - extra
    return np.array([bound] + holding)


def ragged_sizes(rng, amount, total, reach, lean):
    if amount == 2:
        one = jax.random.randint(rng, (), max(1, total - reach), min(reach, total - 1) + 1)
        return jnp.stack([one, total - one])
    tallies = jnp.asarray(length_profile(amount, total, reach, lean), jnp.int32)
    twos = (amount - 1) // 2
    donor, taker = tallies[1:1 + 2 * twos:2], tallies[2:2 + 2 * twos:2]
    margin = jnp.minimum(donor - 1, reach - taker)
    shifted = jax.random.randint(jax.random.fold_in(rng, 1), (twos,), 0, 1 << 20) % (margin + 1)
    tallies = tallies.at[1:1 + 2 * twos:2].set(donor - shifted).at[2:2 + 2 * twos:2].set(taker + shifted)
    return tallies[jax.random.permutation(jax.random.fold_in(rng, 2), amount)]


def scatter_about(key, extent, deviation, bound, cuts=(), kind=jnp.bfloat16):
    factor_of = levels(key, extent, cuts, -0.22, 0.18) if cuts else 1.0
    result = jax.random.normal(key, extent, jnp.float32) * deviation * factor_of
    return jnp.minimum(jnp.maximum(result, -bound), bound).astype(kind)


def setup_inputs(seed: int = 0) -> dict:
    splits = jax.random.split(jax.random.key(seed), 9)
    rollout = draw_rollout(jax.random.fold_in(splits[8], 71), 0)
    send_rows = draw_send_rows(jax.random.fold_in(splits[8], 71), 0)
    seq_lengths = jax.vmap(lambda own: ragged_sizes(own, SEQ_PACK, PACK, MAXLEN, 2))(jax.random.split(splits[2], PACKS)).reshape((PACKS, SEQ_PACK)).astype(jnp.int32)
    attn_gain = jnp.clip(1.0 + 0.18 * jax.random.normal(splits[3], (SECTIONS, D), jnp.float32), 0.099609375, 1.8984375).astype(jnp.bfloat16)
    w_query = draw_w_query(jax.random.fold_in(splits[8], 71), 0)
    w_keyval = draw_w_keyval(jax.random.fold_in(splits[8], 71), 0)
    head_weight = scatter_about(splits[6], (SECTIONS, D), D ** -0.5, 0.0625, ((0, 4), (1, 16)))
    head_attn = scatter_about(splits[7], (SECTIONS, HEADS * HEAD), (HEADS * HEAD // 16) ** -0.5, 0.25, ((0, 4), (1, 16)))
    return {"rollout": rollout, "send_rows": send_rows, "seq_lengths": seq_lengths, "attn_gain": attn_gain, "w_query": w_query, "w_keyval": w_keyval, "head_weight": head_weight, "head_attn": head_attn}


epsilon = 1e-05

def score_pack(rows_in, lengths, norm_gain, query_weight, keyval_weight, head_rows, head_heads):
    rows_float = rows_in.astype(jnp.float32)
    mean_square = lax.optimization_barrier(jnp.mean(rows_float * rows_float, axis=-1, keepdims=True))
    normed = (rows_float * lax.rsqrt(mean_square + epsilon) * norm_gain.astype(jnp.float32)).astype(jnp.bfloat16)
    queries = jnp.dot(normed, query_weight, preferred_element_type=jnp.float32).astype(jnp.bfloat16)
    keyval = jnp.dot(normed, keyval_weight, preferred_element_type=jnp.float32).astype(jnp.bfloat16)
    queries = queries.reshape(PACK, HEADS, HEAD)
    key_rows = keyval[:, :KV_HEADS * HEAD].reshape(PACK, KV_HEADS, HEAD)
    value_rows = keyval[:, KV_HEADS * HEAD:].reshape(PACK, KV_HEADS, HEAD)
    group_size = HEADS // KV_HEADS
    key_rows = jnp.repeat(key_rows, group_size, axis=1)
    value_rows = jnp.repeat(value_rows, group_size, axis=1)
    positions = jnp.arange(PACK, dtype=jnp.int32)
    doc_ends = jnp.cumsum(lengths).astype(jnp.int32)
    doc_ids = lax.optimization_barrier(jnp.sum((positions[:, None] >= doc_ends[None, :]).astype(jnp.int32), axis=-1))
    visible = (doc_ids[:, None] == doc_ids[None, :]) & (positions[None, :] <= positions[:, None])
    logits = jnp.einsum('qhc,khc->hqk', queries.astype(jnp.float32), key_rows.astype(jnp.float32)) / math.sqrt(HEAD)
    logits = jnp.where(visible[None], logits, -1e+30)
    row_max = lax.optimization_barrier(jnp.max(logits, axis=-1, keepdims=True))
    expo = jnp.exp(logits - row_max)
    probabilities = (expo / lax.optimization_barrier(jnp.sum(expo, axis=-1, keepdims=True))).astype(jnp.bfloat16)
    attended = jnp.einsum('hqk,khc->qhc', probabilities.astype(jnp.float32), value_rows.astype(jnp.float32))
    attended = attended.reshape(PACK, HEADS * HEAD)
    direct = jnp.dot(rows_in, head_rows, preferred_element_type=jnp.float32)
    through = jnp.dot(attended, head_heads.astype(jnp.float32), precision=lax.Precision.HIGHEST)
    return direct + through

def reference(rollout, send_rows, seq_lengths, attn_gain, w_query, w_keyval, head_weight, head_attn):
    rank_rows = jnp.arange(PACK, dtype=jnp.int32)
    shard_ids = rank_rows // PIECE
    within = rank_rows % PIECE
    segment_ids = jnp.arange(PACKS, dtype=jnp.int32)
    flat_pos = (shard_ids[None, :] * GEN_DEV + segment_ids[:, None] * PIECE + within[None, :]).astype(jnp.int32)
    source = (shard_ids[None, :] * GEN_DEV + send_rows[flat_pos]).astype(jnp.int32)
    packed = rollout[source]

    def one_section(section_item):
        norm_gain, query_weight, keyval_weight, head_rows, head_heads = section_item

        def one_pack(pack_item):
            return score_pack(pack_item[0], pack_item[1], norm_gain, query_weight, keyval_weight, head_rows, head_heads)
        return lax.map(one_pack, (packed, seq_lengths))
    scores_packed = lax.map(one_section, (attn_gain, w_query, w_keyval, head_weight, head_attn))
    scores = jnp.zeros((SECTIONS, TOKENS), jnp.float32)
    scores = scores.at[:, source.reshape(-1)].set(scores_packed.reshape(SECTIONS, TOKENS))
    return scores
```

```python
import math

import jax
import jax.numpy as jnp
from jax import lax
from jax.experimental import pallas as pl
from jax.experimental.pallas import tpu as pltpu
from jax.sharding import PartitionSpec as P

HEAD = 128
EPS = 1e-05
MESH = pl.DeviceIdType.MESH

BR, SEG, TP = 4, 8, 16
ROWS = 72
PIECE = 9
PACK = 288
D = 8192
KS = D // SEG
HK = KS // 2
QC = 512
KC = 128
CC = QC + KC
MSG = 80
LANES = 128


def kernel(order_ref, orow_ref, len_ref, roll_hbm, gain_hbm, wq_hbm, wkv_hbm, hw_hbm, ha_hbm, out_ref,
           roll, gain_v, wq, wkv, hw_v, ha_v,
           y, X, pf, pbuf, rbuf, lbuf, fbuf, qbuf, kvown, kvb, hwf, hwb, bias, tb, rb, zo, zb,
           ld, xr, ds, fs, rs, sf, ps, pr, hs, hr, kvs, kvr, ts, tr, zs, zr):
    br = lax.axis_index("branch")
    seg = lax.axis_index("segment")
    z = lax.axis_index("tp")
    core = lax.rem(br, 2)
    sib = br + 1 - 2 * core
    step_z = 1 - 2 * core
    nxt = lax.rem(z + step_z + TP, TP)
    a0 = z // 2
    half = lax.rem(z, 2)
    source = seg == a0
    f32, bf = jnp.float32, jnp.bfloat16

    ld_roll = pltpu.make_async_copy(roll_hbm, roll, ld.at[0])
    ld_wq = pltpu.make_async_copy(wq_hbm, wq, ld.at[1])
    ld_wkv = pltpu.make_async_copy(wkv_hbm, wkv, ld.at[2])
    ld_gain = pltpu.make_async_copy(gain_hbm, gain_v, ld.at[3])
    ld_hw = pltpu.make_async_copy(hw_hbm, hw_v, ld.at[4])
    ld_ha = pltpu.make_async_copy(ha_hbm, ha_v, ld.at[5])
    for c in (ld_roll, ld_hw, ld_gain, ld_wq, ld_wkv, ld_ha):
        c.start()

    barrier = pltpu.get_barrier_semaphore()

    def greet(dev):
        pl.semaphore_signal(barrier, inc=1, device_id=dev, device_id_type=MESH)

    for o in range(BR):
        for d in range(SEG):
            if o or d:
                greet((lax.rem(br + o, BR), lax.rem(seg + d, SEG), z))
    for d in range(1, TP):
        greet((br, seg, lax.rem(z + d, TP)))

    ld_roll.wait()

    @pl.when(source)
    def _():
        xf = roll[...].astype(f32)
        ms = jnp.sum(xf * xf, axis=-1, keepdims=True) * (1.0 / D)
        r = lax.rsqrt(ms + EPS)
        sub = lax.broadcasted_iota(jnp.int32, (ROWS, LANES), 0)
        r_row = jnp.sum(jnp.where(orow_ref[...] == sub, r, 0.0), axis=0, keepdims=True)
        hi = r_row.astype(bf).astype(f32)
        mid = (r_row - hi).astype(bf).astype(f32)
        lo = r_row - hi - mid
        s8 = lax.broadcasted_iota(jnp.int32, (8, LANES), 0)
        tail = jnp.where(s8 == 0, hi, jnp.where(s8 == 1, mid, jnp.where(s8 == 2, lo, 0.0)))
        tail = jnp.concatenate([tail] + [jnp.zeros((8, LANES), f32)] * (HK // LANES - 1), axis=1)
        lane = lax.broadcasted_iota(jnp.int32, (ROWS, ROWS), 1)
        perm = (order_ref[...] == lane).astype(f32).astype(bf)
        for c in range(2 * SEG):
            yc = jnp.dot(perm, roll[:, c * HK:(c + 1) * HK], preferred_element_type=f32)
            y[c] = jnp.concatenate([yc, tail], axis=0).astype(bf)

    ld_hw.wait()
    hwf[...] = hw_v[...].astype(f32)

    pl.semaphore_wait(barrier, BR * SEG - 1 + TP - 1)

    def dist(d, o):
        s = lax.rem(seg + d, SEG)
        return pltpu.make_async_remote_copy(
            src_ref=y.at[2 * s + half], dst_ref=X.at[z, br], send_sem=ds.at[2 * d + o], recv_sem=xr.at[z, br],
            device_id=(lax.rem(br + 2 * o, 4), s, z), device_id_type=MESH)

    own = pltpu.make_async_copy(y.at[2 * seg + half], X.at[z, br], xr.at[z, br])

    @pl.when(source)
    def _():
        own.start()
        for d in range(SEG):
            for o in range(2):
                if d or o:
                    dist(d, o).start()

    def hw_send(o):
        return pltpu.make_async_remote_copy(
            src_ref=hwf, dst_ref=hwb.at[br], send_sem=hs.at[o - 1], recv_sem=hr.at[br],
            device_id=(lax.rem(br + o, BR), seg, z), device_id_type=MESH)

    for o in range(1, BR):
        hw_send(o).start()

    def piece(b):
        return pltpu.make_async_copy(X.at[z, b], X.at[z, b], xr.at[z, b])

    def to_sib(b, k):
        return pltpu.make_async_remote_copy(
            src_ref=X.at[z, b], dst_ref=X.at[z, b], send_sem=fs.at[k], recv_sem=xr.at[z, b],
            device_id=(sib, seg, z), device_id_type=MESH)

    for c in (ld_gain, ld_wq, ld_wkv, ld_ha):
        c.wait()

    rq = lax.broadcasted_iota(jnp.int32, (PACK, PACK), 0)
    rk = lax.broadcasted_iota(jnp.int32, (PACK, PACK), 1)

    def position(r):
        main = (((r >> 3) & 3) * SEG + (r >> 5)) * PIECE + (r & 7)
        left = ((r & 3) * SEG + ((r - 256) >> 2)) * PIECE + 8
        return jnp.where(r < 256, main, left)

    pq, pk = position(rq), position(rk)
    start = jnp.zeros((PACK, PACK), jnp.int32)
    end = jnp.int32(0)
    for e in range(len_ref.shape[1]):
        end = end + len_ref[0, e]
        start = jnp.where(pq >= end, end, start)
    bias[...] = jnp.where((pk >= start) & (pk <= pq), 0.0, -1e30)

    for k in range(2):
        b = core + 2 * k
        piece(b).wait()
        to_sib(b, k).start()
    for k in range(2):
        piece(1 - core + 2 * k).wait()

    def ring(blk, t, h):
        return pltpu.make_async_remote_copy(
            src_ref=X.at[blk, pl.ds(2 * h, 2)], dst_ref=X.at[blk, pl.ds(2 * h, 2)], send_sem=rs.at[t, h],
            recv_sem=xr.at[blk, 2 * h], device_id=(br, seg, nxt), device_id_type=MESH)

    def side(blk, t, h):
        return pltpu.make_async_remote_copy(
            src_ref=X.at[blk, pl.ds(2 * h, 2)], dst_ref=X.at[blk, pl.ds(2 * h, 2)], send_sem=sf.at[t, h],
            recv_sem=xr.at[blk, 2 * h], device_id=(sib, seg, z), device_id_type=MESH)

    for h in range(2):
        ring(z, 0, h).start()

    def psend(t, d, a):
        s = lax.rem(seg + d, SEG)
        return pltpu.make_async_remote_copy(
            src_ref=pbuf.at[t, d - 1], dst_ref=rbuf.at[d - 1, a], send_sem=ps.at[t, d - 1], recv_sem=pr.at[d - 1, a],
            device_id=(br, s, z), device_id_type=MESH)

    odd = 2 * half - 1
    dj = lax.broadcasted_iota(jnp.int32, (ROWS, LANES), 0) == lax.broadcasted_iota(jnp.int32, (ROWS, LANES), 1)

    def step(t, _):
        mine = lax.rem(z - step_z * t + TP, TP)
        their = lax.rem(z + step_z * t + TP, TP)
        has = jnp.logical_or(t < 8, core == 0)
        fwd = jnp.logical_or(t < 7, jnp.logical_and(t < 8, core == 0))
        has_side = jnp.logical_or(t < 8, core == 1)
        for h in range(2):
            @pl.when(has)
            def _():
                ring(mine, t, h).wait_recv()

            @pl.when(fwd)
            def _():
                ring(mine, t, h).start()

            @pl.when(has)
            def _():
                side(mine, t, h).start()

        @pl.when(has_side)
        def _():
            for h in range(2):
                side(their, t, h).wait_recv()

        off = t // 2
        sign = jnp.where(lax.rem(t, 2) == 0, odd, -odd)
        a = lax.rem(a0 + sign * off + SEG, SEG)
        scale = []
        for r in range(BR):
            row = jnp.sum(X[2 * a, r][ROWS:, :LANES].astype(f32), axis=0, keepdims=True)
            scale.append(jnp.sum(jnp.where(dj, row, 0.0), axis=-1, keepdims=True))
        acc = None
        for b in range(2):
            g0 = pl.multiple_of(seg * KS + b * HK, HK)
            gain = gain_v[:, pl.ds(g0, HK)].astype(f32)
            xf = jnp.concatenate([X[2 * a + b, r].astype(f32)[:ROWS] * scale[r] for r in range(BR)], axis=0)
            lhs = (xf * gain).astype(bf)
            dq = jnp.dot(lhs, wq[b * HK:(b + 1) * HK, :], preferred_element_type=f32)
            dk = jnp.dot(lhs, wkv[b * HK:(b + 1) * HK, :], preferred_element_type=f32)
            acc = (dq, dk) if acc is None else (acc[0] + dq, acc[1] + dk)
        pf[:, :, :, :QC] = acc[0].reshape(BR, PIECE, 8, QC)
        pf[:, :, :, QC:] = acc[1].reshape(BR, PIECE, 8, KC)
        for d in range(1, SEG):
            s = lax.rem(seg + d, SEG)
            pbuf[t - 1, d - 1] = pf[:, s].reshape(32, CC).astype(bf)
            psend(t - 1, d, a).start()
        fbuf[a] = pf[:, seg].reshape(32, CC)
        for c in range(CC // LANES):
            lbuf[c, pl.ds(pl.multiple_of(a * 32, 32), 32), :] = pf[:, 8, :, c * LANES:(c + 1) * LANES].reshape(32, LANES)
        return 0

    lax.fori_loop(1, 9, step, 0)

    for s in range(SEG):
        v = jnp.concatenate([lbuf[c, pl.ds(s, 32, stride=8), :] for c in range(CC // LANES)], axis=1)
        at = lax.rem(s - seg + SEG, SEG)

        @pl.when(at == 0)
        def _():
            fbuf[8] = v

        @pl.when(at > 0)
        def _():
            pbuf[8, at - 1] = v.astype(bf)
    for d in range(1, SEG):
        psend(8, d, 8).start()

    for o in range(1, BR):
        frm = lax.rem(br + o, BR)
        pltpu.make_async_copy(hwb.at[frm], hwb.at[frm], hr.at[frm]).wait()
    hwb[br] = hwf[...]
    hw4 = jnp.concatenate([hwb[m] for m in range(BR)] + [jnp.zeros((4, QC), f32)], axis=0).astype(bf)
    c0 = pl.multiple_of(z * QC, QC)
    direct = lax.dot_general(hw4, roll[:, pl.ds(c0, QC)], (((1,), (1,)), ((), ())), preferred_element_type=f32)
    lanes16 = lax.broadcasted_iota(jnp.int32, (16, LANES), 1)
    left_ord = order_ref[64:72, :]
    table = jnp.concatenate(
        [jnp.concatenate([order_ref[s * 8:(s + 1) * 8, :], left_ord], axis=0) == lanes16 for s in range(SEG)], axis=1)
    table = table.astype(f32).astype(bf)

    def kv_sum(c, _):
        tot = fbuf[c, :, QC:]
        for d in range(1, SEG):
            psend(8, d, c).wait_recv()
            tot = tot + rbuf[d - 1, c, :, QC:].astype(f32)
        kvown[pl.ds(pl.multiple_of(c * 32, 32), 32), :] = tot.astype(bf)
        return 0

    lax.fori_loop(0, 9, kv_sum, 0)
    slot = z // 8

    def kv_send(e):
        return pltpu.make_async_remote_copy(
            src_ref=kvown, dst_ref=kvb.at[slot], send_sem=kvs.at[e], recv_sem=kvr.at[slot],
            device_id=(br, seg, 2 * lax.rem(z, 8) + e), device_id_type=MESH)

    keep = pltpu.make_async_copy(kvown, kvb.at[slot], kvr.at[slot])
    for e in range(2):
        here = 2 * lax.rem(z, 8) + e == z

        @pl.when(here)
        def _():
            keep.start()

        @pl.when(jnp.logical_not(here))
        def _():
            kv_send(e).start()

    def q_sum(c, _):
        tot = fbuf[c, :, :QC]
        for d in range(1, SEG):
            tot = tot + rbuf[d - 1, c, :, :QC].astype(f32)
        qbuf[pl.ds(pl.multiple_of(c * 32, 32), 32), :] = tot.astype(bf)
        return 0

    lax.fori_loop(0, 9, q_sum, 0)

    for k in range(2):
        pltpu.make_async_copy(kvb.at[k], kvb.at[k], kvr.at[k]).wait()
    keys, values = kvb[0], kvb[1]
    acc = jnp.zeros((PACK, HEAD), f32)
    for h in range(QC // HEAD):
        logits = lax.dot_general(qbuf[:, h * HEAD:(h + 1) * HEAD], keys, (((1,), (1,)), ((), ())),
                                 preferred_element_type=f32)
        logits = logits * (1.0 / math.sqrt(HEAD)) + bias[...]
        expo = jnp.exp(logits - jnp.max(logits, axis=-1, keepdims=True))
        probs = (expo * (1.0 / jnp.sum(expo, axis=-1, keepdims=True))).astype(bf)
        att = jnp.dot(probs, values, preferred_element_type=f32)
        acc = acc + att * ha_v[:, h * HEAD:(h + 1) * HEAD].astype(f32)
    through = jnp.sum(acc, axis=-1, keepdims=True)
    sub = lax.broadcasted_iota(jnp.int32, (256, LANES), 0)
    lane = lax.broadcasted_iota(jnp.int32, (256, LANES), 1)
    main = jnp.where((sub & 7) == lane, through[:256], 0.0).reshape(32, 8, LANES).sum(axis=1)
    main = main + jnp.where(lane[:32] == 8 + seg, through[256:], 0.0)
    tb[...] = main.reshape(32, 1, LANES)

    def tsend(o, d):
        b2, s2 = lax.rem(br + o, BR), lax.rem(seg + d, SEG)
        return pltpu.make_async_remote_copy(
            src_ref=tb.at[s2 * BR + b2], dst_ref=rb.at[br * SEG + seg], send_sem=ts, recv_sem=tr,
            device_id=(b2, s2, z), device_id_type=MESH)

    for o in range(BR):
        for d in range(SEG):
            if o or d:
                tsend(o, d).start()
    pltpu.make_async_copy(tb.at[seg * BR + br], rb.at[br * SEG + seg], tr).start()
    pltpu.make_async_copy(rb, rb, tr).wait()
    got = rb[...].reshape(32, LANES)[:, :16]
    g_hi = got.astype(bf)
    rest = got - g_hi.astype(f32)
    g_mid = rest.astype(bf)
    g_lo = (rest - g_mid.astype(f32)).astype(bf)
    routed = jnp.dot(g_hi, table, preferred_element_type=f32)
    routed = routed + jnp.dot(g_mid, table, preferred_element_type=f32)
    routed = routed + jnp.dot(g_lo, table, preferred_element_type=f32)
    pack_of = lax.broadcasted_iota(jnp.int32, (32, LANES), 0) & 7
    part = jnp.zeros((32, LANES), f32)
    for s in range(SEG):
        part = part + jnp.where(pack_of == s, routed[:, s * LANES:(s + 1) * LANES], 0.0)
    part = part.reshape(BR, SEG, LANES).sum(axis=1)
    zo[...] = jnp.zeros((8, LANES), f32)
    zo[:BR, :ROWS] = part[:, :ROWS] + direct[:BR]

    def zsend(d):
        return pltpu.make_async_remote_copy(
            src_ref=zo, dst_ref=zb.at[z], send_sem=zs, recv_sem=zr,
            device_id=(br, seg, lax.rem(z + d, TP)), device_id_type=MESH)

    for d in range(1, TP):
        zsend(d).start()
    pltpu.make_async_copy(zo, zb.at[z], zr).start()
    pltpu.make_async_copy(zb, zb, zr).wait()
    total = zb[0, :BR, :ROWS]
    for k in range(1, TP):
        total = total + zb[k, :BR, :ROWS]
    out_ref[...] = total

    pltpu.make_async_copy(tb.at[pl.ds(0, 31)], tb.at[pl.ds(0, 31)], ts).wait()
    pltpu.make_async_copy(zb.at[pl.ds(0, 15)], zb.at[pl.ds(0, 15)], zs).wait()

    @pl.when(source)
    def _():
        for d in range(SEG):
            for o in range(2):
                if d or o:
                    dist(d, o).wait_send()
    for o in range(1, BR):
        hw_send(o).wait_send()
    for k in range(2):
        to_sib(core + 2 * k, k).wait_send()
    for e in range(2):
        @pl.when(2 * lax.rem(z, 8) + e != z)
        def _():
            kv_send(e).wait_send()

    def drain(t, _):
        for h in range(2):
            @pl.when(jnp.logical_or(t < 7, jnp.logical_and(t < 8, core == 0)))
            def _():
                ring(z, t, h).wait_send()

            @pl.when(jnp.logical_and(t > 0, jnp.logical_or(t < 8, core == 0)))
            def _():
                side(z, t, h).wait_send()
        for d in range(1, SEG):
            psend(t, d, 0).wait_send()
        return 0

    lax.fori_loop(0, 9, drain, 0)


def local(rollout, send_rows, seq_lengths, attn_gain, w_query, w_keyval, head_weight, head_attn):
    sr = send_rows.reshape(SEG, PIECE)
    order = jnp.concatenate([sr[:, :8].reshape(64), sr[:, 8]])
    orow = jnp.pad(order, (0, LANES - ROWS), constant_values=-1).reshape(1, LANES)
    vm = pl.BlockSpec(memory_space=pltpu.VMEM)
    sm = pl.BlockSpec(memory_space=pltpu.SMEM)
    hbm = pl.BlockSpec(memory_space=pltpu.HBM)
    bf, f32, dma = jnp.bfloat16, jnp.float32, pltpu.SemaphoreType.DMA
    return pl.pallas_call(
        kernel,
        name="scores",
        out_shape=jax.ShapeDtypeStruct((BR, ROWS), f32),
        in_specs=[vm, vm, sm] + [hbm] * 6,
        out_specs=vm,
        scratch_shapes=[
            pltpu.VMEM((ROWS, D), bf), pltpu.VMEM((1, D), bf), pltpu.VMEM((KS, QC), bf), pltpu.VMEM((KS, KC), bf),
            pltpu.VMEM((1, QC), bf), pltpu.VMEM((1, QC), bf),
            pltpu.VMEM((2 * SEG, MSG, HK), bf),
            pltpu.VMEM((TP, BR, MSG, HK), bf),
            pltpu.VMEM((BR, PIECE, 8, CC), f32),
            pltpu.VMEM((9, 7, 32, CC), bf),
            pltpu.VMEM((7, 9, 32, CC), bf),
            pltpu.VMEM((CC // LANES, 256, LANES), f32),
            pltpu.VMEM((9, 32, CC), f32),
            pltpu.VMEM((PACK, QC), bf), pltpu.VMEM((PACK, KC), bf), pltpu.VMEM((2, PACK, KC), bf),
            pltpu.VMEM((1, QC), f32), pltpu.VMEM((BR, 1, QC), f32),
            pltpu.VMEM((PACK, PACK), f32),
            pltpu.VMEM((32, 1, LANES), f32), pltpu.VMEM((32, 1, LANES), f32),
            pltpu.VMEM((8, LANES), f32), pltpu.VMEM((TP, 8, LANES), f32),
            dma((6,)), dma((TP, BR)), dma((16,)), dma((2,)), dma((9, 2)), dma((9, 2)), dma((9, 7)), dma((7, 9)),
            dma((3,)), dma((BR,)), dma((2,)), dma((2,)), dma, dma, dma, dma,
        ],
        compiler_params=pltpu.CompilerParams(
            collective_id=0, has_side_effects=True, vmem_limit_bytes=56 << 20),
    )(order.reshape(ROWS, 1), orow, seq_lengths, rollout, attn_gain, w_query[0], w_keyval[0], head_weight, head_attn)


def solution(mesh):
    return jax.shard_map(
        local,
        mesh=mesh,
        in_specs=(
            P(("branch", "segment"), None),
            P(("branch", "segment")),
            P("segment", None),
            P("branch", None),
            P("branch", "segment", "tp"),
            P("branch", "segment", "tp"),
            P("branch", "tp"),
            P("branch", "tp"),
        ),
        out_specs=P(None, ("branch", "segment")),
        check_vma=False,
    )
```

```python
import math

import jax
import jax.numpy as jnp
from jax import lax
from jax.experimental import pallas as pl
from jax.experimental.pallas import tpu as pltpu
from jax.sharding import PartitionSpec as P

EPS = 1e-05
MESH = pl.DeviceIdType.MESH

BR, SEG, TP = 4, 8, 16
NX = 4
ROWS = 72
PIECE = 9
PACK = 288
HALF = PACK // 2
D = 8192
KS = D // SEG
HK = KS // 2
LANES = 128
HEADS_HERE = 4
CHUNKS = HEADS_HERE + 1
MSG = 80
WIDTH = HEADS_HERE * LANES


def kernel(send_ref, len_ref, roll_hbm, gain_hbm, wq_hbm, wkv_hbm, hw_hbm, ha_hbm, out_ref,
           roll, gain_v, wA, hw_v, ha_v, y, X, N, pf, pbuf, rbuf, fown, ybuf, qf, kvb, hwf, hwb, bias, tb, rb, zo, zb,
           ld, lw, xo, xz, so, sd, sl, fo, fz, rs, sf, ws, wr, ps, pr, ys, yr, hs, hr, kvs, kvr, ts, tr, zs, zr):
    f32, bf, i32 = jnp.float32, jnp.bfloat16, jnp.int32
    br = lax.axis_index("branch")
    seg = lax.axis_index("segment")
    z = lax.axis_index("tp")
    core, yh = lax.rem(br, 2), br // 2
    x, yl = lax.rem(seg, NX), seg // NX
    sib = br + 1 - 2 * core
    far = lax.rem(br + 2, BR)
    part_seg = lax.rem(seg + NX, SEG)
    step_z = 1 - 2 * core
    nxt = lax.rem(z + step_z + TP, TP)
    source = x == z // NX

    def xpeer(d):
        return yl * NX + lax.rem(x + d, NX)

    ld_roll = pltpu.make_async_copy(roll_hbm, roll, ld.at[0])
    ld_gain = pltpu.make_async_copy(gain_hbm, gain_v, ld.at[1])
    ld_hw = pltpu.make_async_copy(hw_hbm, hw_v, ld.at[2])
    ld_ha = pltpu.make_async_copy(ha_hbm, ha_v, ld.at[3])
    ld_w = [pltpu.make_async_copy(wkv_hbm, wA.at[yl, 0], lw.at[0])]
    for c in range(HEADS_HERE):
        ld_w.append(pltpu.make_async_copy(wq_hbm.at[:, pl.ds(c * LANES, LANES)], wA.at[yl, c + 1], lw.at[c + 1]))
    for c in [ld_roll, ld_hw, ld_gain] + ld_w + [ld_ha]:
        c.start()

    barrier = pltpu.get_barrier_semaphore()

    def greet(dev):
        pl.semaphore_signal(barrier, inc=1, device_id=dev, device_id_type=MESH)

    for d in range(1, NX):
        greet((br, xpeer(d), z))
    for d in range(NX):
        greet((far, xpeer(d), z))
    greet((br, part_seg, z))
    greet((sib, seg, z))
    greet((lax.rem(sib + 2, BR), seg, z))
    greet((br, seg, lax.rem(z + 1, TP)))
    greet((br, seg, lax.rem(z + TP - 1, TP)))

    drains = []

    def finish():
        for f in drains:
            f()

    sub = lax.broadcasted_iota(i32, (ROWS, LANES), 0)
    lane = lax.broadcasted_iota(i32, (ROWS, LANES), 1)
    diag = sub == lane
    src = jnp.where(sub < 64, (sub >> 3) * PIECE + (sub & 7), (sub - 64) * PIECE + 8)
    send = jnp.concatenate([send_ref[...].astype(f32), jnp.zeros((1, LANES - ROWS), f32)], axis=1)
    order = jnp.sum(jnp.where(lane == src, send, 0.0), axis=1, keepdims=True)
    order_i = order.astype(i32)
    order_row = jnp.sum(jnp.where(diag, order, 0.0), axis=0, keepdims=True).astype(i32)

    ld_roll.wait()
    xf = roll[...].astype(f32)
    r = lax.rsqrt(jnp.sum(xf * xf, axis=-1, keepdims=True) * (1.0 / D) + EPS)
    r_row = jnp.sum(jnp.where((order_row == sub) & (lane < ROWS), r, 0.0), axis=0, keepdims=True)
    hi = r_row.astype(bf).astype(f32)
    mid = (r_row - hi).astype(bf).astype(f32)
    lo = r_row - hi - mid
    s8 = lax.broadcasted_iota(i32, (8, LANES), 0)
    tail = jnp.where(s8 == 0, hi, jnp.where(s8 == 1, mid, jnp.where(s8 == 2, lo, 0.0)))
    tail = jnp.concatenate([tail] + [jnp.zeros((8, LANES), f32)] * (HK // LANES - 1), axis=1)
    perm = (order_i == lane[:, :ROWS]).astype(f32).astype(bf)
    for c in range(2 * SEG):
        yc = jnp.dot(perm, roll[:, c * HK:(c + 1) * HK], preferred_element_type=f32)
        y[c] = jnp.concatenate([yc, tail], axis=0).astype(bf)
    ld_hw.wait()
    hwf[...] = hw_v[...].astype(f32)
    for c in ld_w:
        c.wait()
    ld_gain.wait()
    ld_ha.wait()

    pl.semaphore_wait(barrier, 12)

    quarter = lax.rem(z, NX)

    def dist(d):
        xd = lax.rem(x + d, NX)
        return pltpu.make_async_remote_copy(
            src_ref=y.at[(quarter // 2) * SEG + 2 * xd + lax.rem(quarter, 2)], dst_ref=X.at[yh, z, core],
            send_sem=sd.at[d], recv_sem=xz.at[z, core], device_id=(far, yl * NX + xd, z), device_id_type=MESH)

    @pl.when(source)
    def _():
        for d in range(NX):
            dist(d).start()

    def wsend(c):
        return pltpu.make_async_remote_copy(
            src_ref=wA.at[yl, c], dst_ref=wA.at[yl, c], send_sem=ws.at[c], recv_sem=wr.at[c],
            device_id=(br, part_seg, z), device_id_type=MESH)

    for c in range(CHUNKS):
        wsend(c).start()

    def row_send(d, q):
        xd = lax.rem(x + d, NX)
        return pltpu.make_async_remote_copy(
            src_ref=y.at[pl.ds(q * SEG + 2 * xd, 2)], dst_ref=X.at[yh, pl.ds(x * NX + 2 * q, 2), core],
            send_sem=so.at[d, q], recv_sem=xo.at[x, core, q], device_id=(br, yl * NX + xd, z), device_id_type=MESH)

    def row_keep(q):
        return pltpu.make_async_copy(
            y.at[pl.ds(q * SEG + 2 * x, 2)], X.at[yh, pl.ds(x * NX + 2 * q, 2), core], xo.at[x, core, q])

    def row_side(d, q, src_ref):
        xs = lax.rem(x + d, NX)
        dst = X.at[yh, pl.ds(xs * NX + 2 * q, 2), core]
        return pltpu.make_async_remote_copy(
            src_ref=dst if src_ref is None else src_ref, dst_ref=dst, send_sem=fo.at[d, q],
            recv_sem=xo.at[xs, core, q], device_id=(sib, seg, z), device_id_type=MESH)

    def row_wait(d, q, c):
        xs = lax.rem(x + d, NX)
        ref = X.at[yh, pl.ds(xs * NX + 2 * q, 2), c]
        pltpu.make_async_copy(ref, ref, xo.at[xs, c, q]).wait()

    for d in (1, 3, 2):
        for q in range(2):
            row_send(d, q).start()
    for q in range(2):
        row_keep(q).start()
        row_side(0, q, y.at[pl.ds(q * SEG + 2 * x, 2)]).start()

    def hw_send(o):
        return pltpu.make_async_remote_copy(
            src_ref=hwf, dst_ref=hwb.at[br], send_sem=hs.at[o - 1], recv_sem=hr.at[br],
            device_id=(lax.rem(br + o, BR), seg, z), device_id_type=MESH)

    for o in range(1, BR):
        hw_send(o).start()

    @drains.append
    def _():
        @pl.when(source)
        def _():
            for d in range(NX):
                dist(d).wait_send()
        for c in range(CHUNKS):
            wsend(c).wait_send()
        for d in range(1, NX):
            for q in range(2):
                row_send(d, q).wait_send()
        for q in range(2):
            row_side(0, q, y.at[pl.ds(q * SEG + 2 * x, 2)]).wait_send()
        for o in range(1, BR):
            hw_send(o).wait_send()

    rq = lax.broadcasted_iota(i32, (PACK, PACK), 0)
    rk = lax.broadcasted_iota(i32, (PACK, PACK), 1)

    def position(p):
        low = (p >= HALF).astype(i32)
        u = p - low * HALF
        left = u >= 2 * BR * 16
        sh = jnp.where(left, u - 128, u >> 3)
        i = jnp.where(left, 8, u & 7)
        g = ((sh >> 3) * 2 + (sh & 1)) * SEG + low * NX + ((sh >> 1) & 3)
        return g * PIECE + i

    pq, pk = position(rq), position(rk)
    start = jnp.zeros((PACK, PACK), i32)
    end = jnp.int32(0)
    for e in range(len_ref.shape[1]):
        end = end + len_ref[0, e]
        start = jnp.where(pq >= end, end, start)
    bias[...] = jnp.where((pk >= start) & (pk <= pq), 0.0, -1e30)

    other = 1 - yh

    def zpiece(c):
        ref = X.at[other, z, c]
        return pltpu.make_async_copy(ref, ref, xz.at[z, c])

    def to_sib():
        return pltpu.make_async_remote_copy(
            src_ref=X.at[other, z, core], dst_ref=X.at[other, z, core], send_sem=fz, recv_sem=xz.at[z, core],
            device_id=(sib, seg, z), device_id_type=MESH)

    def ring(blk, t, h):
        return pltpu.make_async_remote_copy(
            src_ref=X.at[other, blk, h], dst_ref=X.at[other, blk, h], send_sem=rs.at[t, h],
            recv_sem=xz.at[blk, h], device_id=(br, seg, nxt), device_id_type=MESH)

    def side(blk, t, h):
        return pltpu.make_async_remote_copy(
            src_ref=X.at[other, blk, h], dst_ref=X.at[other, blk, h], send_sem=sf.at[t, h],
            recv_sem=xz.at[blk, h], device_id=(sib, seg, z), device_id_type=MESH)

    zpiece(core).wait()
    to_sib().start()
    ring(z, 0, core).start()
    zpiece(1 - core).wait()
    ring(z, 0, 1 - core).start()

    def step(t, _):
        mine = lax.rem(z - step_z * t + TP, TP)
        has = jnp.logical_or(t < 8, core == 0)
        fwd = jnp.logical_or(t < 7, jnp.logical_and(t < 8, core == 0))
        for k in range(2):
            h = lax.rem(core + k + TP, 2)

            @pl.when(has)
            def _():
                ring(mine, t, h).wait_recv()

            @pl.when(fwd)
            def _():
                ring(mine, t, h).start()

            @pl.when(has)
            def _():
                side(mine, t, h).start()
        return 0

    lax.fori_loop(1, 6, step, 0)
    for d in (1, 3):
        for q in range(2):
            row_wait(d, q, core)
            row_side(d, q, None).start()
    lax.fori_loop(6, 9, step, 0)
    for q in range(2):
        row_wait(2, q, core)
        row_side(2, q, None).start()

    @drains.append
    def _():
        to_sib().wait_send()
        for d in range(1, NX):
            for q in range(2):
                row_side(d, q, None).wait_send()

        def drain(t, _):
            for h in range(2):
                @pl.when(jnp.logical_or(t < 7, jnp.logical_and(t < 8, core == 0)))
                def _():
                    ring(z, t, h).wait_send()

                @pl.when(jnp.logical_and(t > 0, jnp.logical_or(t < 8, core == 0)))
                def _():
                    side(z, t, h).wait_send()
            return 0

        lax.fori_loop(0, 9, drain, 0)

    for d in range(NX):
        for q in range(2):
            row_wait(d, q, 1 - core)
    for q in range(2):
        row_wait(0, q, core)

    def side_wait(t, _):
        their = lax.rem(z + step_z * t + TP, TP)

        @pl.when(jnp.logical_or(t < 8, core == 1))
        def _():
            for h in range(2):
                side(their, t, h).wait_recv()
        return 0

    lax.fori_loop(1, 9, side_wait, 0)

    def norm(g, _):
        gy, gx = g // NX, lax.rem(g, NX)
        scale = []
        for c in range(2):
            row = jnp.sum(X[gy, gx * NX, c][ROWS:, :LANES].astype(f32), axis=0, keepdims=True)
            scale.append(jnp.sum(jnp.where(diag, row, 0.0), axis=-1, keepdims=True))
        for q in range(4):
            g0 = pl.multiple_of(((q // 2) * NX + x) * KS + (q % 2) * HK, HK)
            gain = gain_v[:, pl.ds(g0, HK)].astype(f32)
            v = jnp.concatenate([X[gy, gx * NX + q, c].astype(f32)[:ROWS] * scale[c] for c in range(2)], axis=0)
            N[g, :, q * HK:(q + 1) * HK] = (v * gain).astype(bf)
        return 0

    lax.fori_loop(0, 2 * NX, norm, 0)

    def psend(c, d):
        return pltpu.make_async_remote_copy(
            src_ref=pbuf.at[c, d - 1], dst_ref=rbuf.at[c, d - 1], send_sem=ps.at[c, d - 1], recv_sem=pr.at[c, d - 1],
            device_id=(br, xpeer(d), z), device_id_type=MESH)

    def ysend(c):
        return pltpu.make_async_remote_copy(
            src_ref=ybuf.at[c], dst_ref=qf.at[c, yl], send_sem=ys.at[c], recv_sem=yr.at[c],
            device_id=(br, part_seg, z), device_id_type=MESH)

    def produce(c):
        wsend(c).wait_recv()
        lhs = N[...].reshape(8 * HALF, 2 * KS)
        acc = jnp.dot(lhs[:, :KS], wA[0, c], preferred_element_type=f32)
        acc = acc + jnp.dot(lhs[:, KS:], wA[1, c], preferred_element_type=f32)
        pf[...] = acc.reshape(16, PIECE, 8, LANES)
        left = pf[:, 8].reshape(128, LANES)
        lx = lax.broadcasted_iota(i32, (16, 8, LANES), 1)
        left = left.reshape(16, 8, LANES)
        for d in range(NX):
            xd = lax.rem(x + d, NX)
            for k in range(2):
                s = k * NX + xd
                main = pf[:, s].reshape(128, LANES)
                tail = jnp.sum(jnp.where(lx == s, left, 0.0), axis=1)
                v = jnp.concatenate([main, tail], axis=0)
                if d == 0:
                    fown[c, k] = v
                else:
                    pbuf[c, d - 1, k] = v.astype(bf)
            if d:
                psend(c, d).start()

    def consume(c):
        tot = fown[c]
        for d in range(1, NX):
            psend(c, d).wait_recv()
            tot = tot + rbuf[c, d - 1].astype(f32)
        fown[c] = tot
        ybuf[c] = fown[c, 1 - yl].astype(bf)
        ysend(c).start()
        qf[c, yl] = fown[c, yl].astype(bf)

    slot = z // 8

    def kv_send(e):
        return pltpu.make_async_remote_copy(
            src_ref=qf.at[0], dst_ref=kvb.at[slot], send_sem=kvs.at[e], recv_sem=kvr.at[slot],
            device_id=(br, seg, 2 * lax.rem(z, 8) + e), device_id_type=MESH)

    keep = pltpu.make_async_copy(qf.at[0], kvb.at[slot], kvr.at[slot])

    def kv_start():
        ysend(0).wait_recv()
        for e in range(2):
            here = 2 * lax.rem(z, 8) + e == z

            @pl.when(here)
            def _():
                keep.start()

            @pl.when(jnp.logical_not(here))
            def _():
                kv_send(e).start()

    def chunk(c, _):
        produce(c)

        @pl.when(c > 0)
        def _():
            consume(c - 1)

        @pl.when(c == 2)
        def _():
            kv_start()
        return 0

    lax.fori_loop(0, CHUNKS, chunk, 0)

    @drains.append
    def _():
        def drain(c, _):
            for d in range(1, NX):
                psend(c, d).wait_send()
            ysend(c).wait_send()
            return 0

        lax.fori_loop(0, CHUNKS, drain, 0)
        for e in range(2):
            @pl.when(2 * lax.rem(z, 8) + e != z)
            def _():
                kv_send(e).wait_send()

    for o in range(1, BR):
        frm = lax.rem(br + o, BR)
        pltpu.make_async_copy(hwb.at[frm], hwb.at[frm], hr.at[frm]).wait()
    hwb[br] = hwf[...]
    hw4 = jnp.concatenate([hwb[m] for m in range(BR)] + [jnp.zeros((4, WIDTH), f32)], axis=0).astype(bf)
    c0 = pl.multiple_of(z * WIDTH, WIDTH)
    direct = lax.dot_general(hw4, roll[:, pl.ds(c0, WIDTH)], (((1,), (1,)), ((), ())), preferred_element_type=f32)
    lanes16 = lax.broadcasted_iota(i32, (16, LANES), 1)
    table = jnp.concatenate(
        [jnp.concatenate([order_i[s * 8:(s + 1) * 8], order_i[64:72]], axis=0) == lanes16 for s in range(SEG)], axis=1)
    table = table.astype(f32).astype(bf)

    consume(CHUNKS - 1)
    for k in range(2):
        pltpu.make_async_copy(kvb.at[k], kvb.at[k], kvr.at[k]).wait()
    keys, values = kvb[0].reshape(PACK, LANES), kvb[1].reshape(PACK, LANES)
    acc = jnp.zeros((PACK, LANES), f32)
    for h in range(HEADS_HERE):
        ysend(h + 1).wait_recv()
        logits = lax.dot_general(qf[h + 1].reshape(PACK, LANES), keys, (((1,), (1,)), ((), ())),
                                 preferred_element_type=f32)
        logits = logits * (1.0 / math.sqrt(LANES)) + bias[...]
        expo = jnp.exp(logits - jnp.max(logits, axis=-1, keepdims=True))
        probs = (expo * (1.0 / jnp.sum(expo, axis=-1, keepdims=True))).astype(bf)
        att = jnp.dot(probs, values, preferred_element_type=f32)
        acc = acc + att * ha_v[:, h * LANES:(h + 1) * LANES].astype(f32)
    through = jnp.sum(acc, axis=-1, keepdims=True)
    sub = lax.broadcasted_iota(i32, (128, LANES), 0)
    lane = lax.broadcasted_iota(i32, (128, LANES), 1)
    for k in range(2):
        rows = through[k * HALF:(k + 1) * HALF]
        main = jnp.where((sub & 7) == lane, rows[:128], 0.0).reshape(16, 8, LANES).sum(axis=1)
        main = main + jnp.where(lane[:16] == 8 + seg, rows[128:], 0.0)
        tb[k * 16:(k + 1) * 16] = main.reshape(16, 1, LANES)

    def at(b2, s2):
        return (s2 // NX) * 16 + ((b2 // 2) * NX + lax.rem(s2, NX)) * 2 + lax.rem(b2, 2)

    def tsend(o, d):
        b2, s2 = lax.rem(br + o, BR), lax.rem(seg + d, SEG)
        return pltpu.make_async_remote_copy(
            src_ref=tb.at[at(b2, s2)], dst_ref=rb.at[br * SEG + seg], send_sem=ts, recv_sem=tr,
            device_id=(b2, s2, z), device_id_type=MESH)

    for o in range(BR):
        for d in range(SEG):
            if o or d:
                tsend(o, d).start()
    pltpu.make_async_copy(tb.at[at(br, seg)], rb.at[br * SEG + seg], tr).start()
    pltpu.make_async_copy(rb, rb, tr).wait()

    @drains.append
    def _():
        pltpu.make_async_copy(tb.at[pl.ds(0, 31)], tb.at[pl.ds(0, 31)], ts).wait()

    got = rb[...].reshape(32, LANES)[:, :16]
    g_hi = got.astype(bf)
    rest = got - g_hi.astype(f32)
    g_mid = rest.astype(bf)
    g_lo = (rest - g_mid.astype(f32)).astype(bf)
    routed = jnp.dot(g_hi, table, preferred_element_type=f32)
    routed = routed + jnp.dot(g_mid, table, preferred_element_type=f32)
    routed = routed + jnp.dot(g_lo, table, preferred_element_type=f32)
    pack_of = lax.broadcasted_iota(i32, (32, LANES), 0) & 7
    part = jnp.zeros((32, LANES), f32)
    for s in range(SEG):
        part = part + jnp.where(pack_of == s, routed[:, s * LANES:(s + 1) * LANES], 0.0)
    part = part.reshape(BR, SEG, LANES).sum(axis=1)
    zo[...] = jnp.zeros((BR, LANES), f32)
    zo[:, :ROWS] = part[:, :ROWS] + direct[:BR]

    def zsend(d):
        return pltpu.make_async_remote_copy(
            src_ref=zo, dst_ref=zb.at[z], send_sem=zs, recv_sem=zr,
            device_id=(br, seg, lax.rem(z + d, TP)), device_id_type=MESH)

    for d in range(1, TP):
        zsend(d).start()
    pltpu.make_async_copy(zo, zb.at[z], zr).start()
    pltpu.make_async_copy(zb, zb, zr).wait()

    @drains.append
    def _():
        pltpu.make_async_copy(zb.at[pl.ds(0, 15)], zb.at[pl.ds(0, 15)], zs).wait()

    total = zb[0, :, :ROWS]
    for k in range(1, TP):
        total = total + zb[k, :, :ROWS]
    out_ref[...] = total
    finish()


def local(rollout, send_rows, seq_lengths, attn_gain, w_query, w_keyval, head_weight, head_attn):
    vm = pl.BlockSpec(memory_space=pltpu.VMEM)
    sm = pl.BlockSpec(memory_space=pltpu.SMEM)
    hbm = pl.BlockSpec(memory_space=pltpu.HBM)
    bf, f32, dma = jnp.bfloat16, jnp.float32, pltpu.SemaphoreType.DMA
    return pl.pallas_call(
        kernel,
        name="scores",
        out_shape=jax.ShapeDtypeStruct((BR, ROWS), f32),
        in_specs=[vm, sm] + [hbm] * 6,
        out_specs=vm,
        scratch_shapes=[
            pltpu.VMEM((ROWS, D), bf), pltpu.VMEM((1, D), bf), pltpu.VMEM((2, CHUNKS, KS, LANES), bf),
            pltpu.VMEM((1, WIDTH), bf), pltpu.VMEM((1, WIDTH), bf),
            pltpu.VMEM((2 * SEG, MSG, HK), bf),
            pltpu.VMEM((2, TP, 2, MSG, HK), bf),
            pltpu.VMEM((8, HALF, 2 * KS), bf),
            pltpu.VMEM((16, PIECE, 8, LANES), f32),
            pltpu.VMEM((CHUNKS, 3, 2, HALF, LANES), bf),
            pltpu.VMEM((CHUNKS, 3, 2, HALF, LANES), bf),
            pltpu.VMEM((CHUNKS, 2, HALF, LANES), f32),
            pltpu.VMEM((CHUNKS, HALF, LANES), bf),
            pltpu.VMEM((CHUNKS, 2, HALF, LANES), bf),
            pltpu.VMEM((2, 2, HALF, LANES), bf),
            pltpu.VMEM((1, WIDTH), f32), pltpu.VMEM((BR, 1, WIDTH), f32),
            pltpu.VMEM((PACK, PACK), f32),
            pltpu.VMEM((32, 1, LANES), f32), pltpu.VMEM((32, 1, LANES), f32),
            pltpu.VMEM((BR, LANES), f32), pltpu.VMEM((TP, BR, LANES), f32),
            dma((4,)), dma((CHUNKS,)), dma((NX, 2, 2)), dma((TP, 2)), dma((NX, 2)), dma((NX,)), dma((2,)),
            dma((NX, 2)), dma, dma((9, 2)), dma((9, 2)), dma((CHUNKS,)), dma((CHUNKS,)),
            dma((CHUNKS, 3)), dma((CHUNKS, 3)), dma((CHUNKS,)), dma((CHUNKS,)),
            dma((3,)), dma((BR,)), dma((2,)), dma((2,)), dma, dma, dma, dma,
        ],
        compiler_params=pltpu.CompilerParams(
            collective_id=0, has_side_effects=True, vmem_limit_bytes=56 << 20),
    )(send_rows.reshape(1, ROWS), seq_lengths, rollout, attn_gain, w_query[0], w_keyval[0], head_weight, head_attn)


def solution(mesh):
    return jax.shard_map(
        local,
        mesh=mesh,
        in_specs=(
            P(("branch", "segment"), None),
            P(("branch", "segment")),
            P("segment", None),
            P("branch", None),
            P("branch", "segment", "tp"),
            P("branch", "segment", "tp"),
            P("branch", "tp"),
            P("branch", "tp"),
        ),
        out_specs=P(None, ("branch", "segment")),
        check_vma=False,
    )
```

```python
import math

import jax
import jax.numpy as jnp
from jax import lax
from jax.experimental import pallas as pl
from jax.experimental.pallas import tpu as pltpu
from jax.sharding import PartitionSpec as P

EPS = 1e-05
MESH = pl.DeviceIdType.MESH

BR, SEG, TP = 4, 8, 16
NX = 4
ROWS = 72
PIECE = 9
PACK = 288
HALF = PACK // 2
D = 8192
KS = D // SEG
HK = KS // 2
LANES = 128
HEADS_HERE = 4
CHUNKS = HEADS_HERE + 1
MSG = 80
WIDTH = HEADS_HERE * LANES


def kernel(send_ref, len_ref, roll_hbm, gain_hbm, wq_hbm, wkv_hbm, hw_hbm, ha_hbm, out_ref,
           roll, gain_v, wA, hw_v, ha_v, y, X, N, pf, pbuf, rbuf, fown, ybuf, qf, kvb, hwf, hwb, bias, tb, rb, zo, zb,
           ld, lw, xo, xq, so, sd, fo, fq, zn, ws, wr, ps, pr, ys, yr, hs, hr, kvs, kvr, ts, tr, zs, zr, ra, rb4):
    f32, bf, i32 = jnp.float32, jnp.bfloat16, jnp.int32
    br = lax.axis_index("branch")
    seg = lax.axis_index("segment")
    z = lax.axis_index("tp")
    core, yh = lax.rem(br, 2), br // 2
    x, yl = lax.rem(seg, NX), seg // NX
    sib = br + 1 - 2 * core
    far = lax.rem(br + 2, BR)
    part_seg = lax.rem(seg + NX, SEG)
    quarter = lax.rem(z, NX)

    def xpeer(d):
        return yl * NX + lax.rem(x + d, NX)

    ld_roll = pltpu.make_async_copy(roll_hbm, roll, ld.at[0])
    ld_gain = pltpu.make_async_copy(gain_hbm, gain_v, ld.at[1])
    ld_hw = pltpu.make_async_copy(hw_hbm, hw_v, ld.at[2])
    ld_ha = pltpu.make_async_copy(ha_hbm, ha_v, ld.at[3])
    ld_w = [pltpu.make_async_copy(wkv_hbm, wA.at[yl, 0], lw.at[0])]
    for c in range(HEADS_HERE):
        ld_w.append(pltpu.make_async_copy(wq_hbm.at[:, pl.ds(c * LANES, LANES)], wA.at[yl, c + 1], lw.at[c + 1]))
    for c in [ld_roll, ld_hw, ld_gain] + ld_w + [ld_ha]:
        c.start()

    barrier = pltpu.get_barrier_semaphore()

    def greet(dev):
        pl.semaphore_signal(barrier, inc=1, device_id=dev, device_id_type=MESH)

    for d in range(1, NX):
        greet((br, xpeer(d), z))
    for d in range(NX):
        greet((far, xpeer(d), z))
    greet((br, part_seg, z))
    greet((sib, seg, z))
    greet((lax.rem(sib + 2, BR), seg, z))
    for d in (1, 2, TP - 2, TP - 1):
        greet((br, seg, lax.rem(z + d, TP)))

    drains = []

    def finish():
        for f in drains:
            f()

    sub = lax.broadcasted_iota(i32, (ROWS, LANES), 0)
    lane = lax.broadcasted_iota(i32, (ROWS, LANES), 1)
    diag = sub == lane
    src = jnp.where(sub < 64, (sub >> 3) * PIECE + (sub & 7), (sub - 64) * PIECE + 8)
    send = jnp.concatenate([send_ref[...].astype(f32), jnp.zeros((1, LANES - ROWS), f32)], axis=1)
    order = jnp.sum(jnp.where(lane == src, send, 0.0), axis=1, keepdims=True)
    order_i = order.astype(i32)
    order_row = jnp.sum(jnp.where(diag, order, 0.0), axis=0, keepdims=True).astype(i32)

    ld_roll.wait()
    xf = roll[...].astype(f32)
    r = lax.rsqrt(jnp.sum(xf * xf, axis=-1, keepdims=True) * (1.0 / D) + EPS)
    r_row = jnp.sum(jnp.where((order_row == sub) & (lane < ROWS), r, 0.0), axis=0, keepdims=True)
    hi = r_row.astype(bf).astype(f32)
    mid = (r_row - hi).astype(bf).astype(f32)
    lo = r_row - hi - mid
    s8 = lax.broadcasted_iota(i32, (8, LANES), 0)
    tail = jnp.where(s8 == 0, hi, jnp.where(s8 == 1, mid, jnp.where(s8 == 2, lo, 0.0)))
    tail = jnp.concatenate([tail] + [jnp.zeros((8, LANES), f32)] * (HK // LANES - 1), axis=1)
    perm = (order_i == lane[:, :ROWS]).astype(f32).astype(bf)
    for c in range(2 * SEG):
        yc = jnp.dot(perm, roll[:, c * HK:(c + 1) * HK], preferred_element_type=f32)
        y[c] = jnp.concatenate([yc, tail], axis=0).astype(bf)
    ld_hw.wait()
    hwf[...] = hw_v[...].astype(f32)
    for c in ld_w:
        c.wait()
    ld_gain.wait()
    ld_ha.wait()

    pl.semaphore_wait(barrier, 14)

    def spread(sem, d):
        for e in (d, TP - d):
            pl.semaphore_signal(sem, inc=1, device_id=(br, seg, lax.rem(z + e, TP)), device_id_type=MESH)

    spread(ra, 2)

    def dist(d):
        xd = lax.rem(x + d, NX)
        return pltpu.make_async_remote_copy(
            src_ref=y.at[(quarter // 2) * SEG + 2 * xd + lax.rem(quarter, 2)], dst_ref=X.at[yh, x * NX + quarter, core],
            send_sem=sd.at[d], recv_sem=xq.at[x, quarter, core], device_id=(far, yl * NX + xd, z), device_id_type=MESH)

    for d in range(NX):
        dist(d).start()

    def wsend(c):
        return pltpu.make_async_remote_copy(
            src_ref=wA.at[yl, c], dst_ref=wA.at[yl, c], send_sem=ws.at[c], recv_sem=wr.at[c],
            device_id=(br, part_seg, z), device_id_type=MESH)

    for c in range(CHUNKS):
        wsend(c).start()

    def row_send(d, q):
        xd = lax.rem(x + d, NX)
        return pltpu.make_async_remote_copy(
            src_ref=y.at[pl.ds(q * SEG + 2 * xd, 2)], dst_ref=X.at[yh, pl.ds(x * NX + 2 * q, 2), core],
            send_sem=so.at[d, q], recv_sem=xo.at[x, core, q], device_id=(br, yl * NX + xd, z), device_id_type=MESH)

    def row_keep(q):
        return pltpu.make_async_copy(
            y.at[pl.ds(q * SEG + 2 * x, 2)], X.at[yh, pl.ds(x * NX + 2 * q, 2), core], xo.at[x, core, q])

    def row_side(d, q, src_ref):
        xs = lax.rem(x + d, NX)
        dst = X.at[yh, pl.ds(xs * NX + 2 * q, 2), core]
        return pltpu.make_async_remote_copy(
            src_ref=dst if src_ref is None else src_ref, dst_ref=dst, send_sem=fo.at[d, q],
            recv_sem=xo.at[xs, core, q], device_id=(sib, seg, z), device_id_type=MESH)

    def row_wait(d, q, c):
        xs = lax.rem(x + d, NX)
        ref = X.at[yh, pl.ds(xs * NX + 2 * q, 2), c]
        pltpu.make_async_copy(ref, ref, xo.at[xs, c, q]).wait()

    for d in (1, 3, 2):
        for q in range(2):
            row_send(d, q).start()
    for q in range(2):
        row_keep(q).start()
        row_side(0, q, y.at[pl.ds(q * SEG + 2 * x, 2)]).start()

    def hw_send(o):
        return pltpu.make_async_remote_copy(
            src_ref=hwf, dst_ref=hwb.at[br], send_sem=hs.at[o - 1], recv_sem=hr.at[br],
            device_id=(lax.rem(br + o, BR), seg, z), device_id_type=MESH)

    for o in range(1, BR):
        hw_send(o).start()

    @drains.append
    def _():
        for d in range(NX):
            dist(d).wait_send()
        for c in range(CHUNKS):
            wsend(c).wait_send()
        for d in range(1, NX):
            for q in range(2):
                row_send(d, q).wait_send()
        for q in range(2):
            row_side(0, q, y.at[pl.ds(q * SEG + 2 * x, 2)]).wait_send()
        for o in range(1, BR):
            hw_send(o).wait_send()

    rq = lax.broadcasted_iota(i32, (PACK, PACK), 0)
    rk = lax.broadcasted_iota(i32, (PACK, PACK), 1)

    def position(p):
        low = (p >= HALF).astype(i32)
        u = p - low * HALF
        left = u >= 2 * BR * 16
        sh = jnp.where(left, u - 128, u >> 3)
        i = jnp.where(left, 8, u & 7)
        g = ((sh >> 3) * 2 + (sh & 1)) * SEG + low * NX + ((sh >> 1) & 3)
        return g * PIECE + i

    pq, pk = position(rq), position(rk)
    start = jnp.zeros((PACK, PACK), i32)
    end = jnp.int32(0)
    for e in range(len_ref.shape[1]):
        end = end + len_ref[0, e]
        start = jnp.where(pq >= end, end, start)
    bias[...] = jnp.where((pk >= start) & (pk <= pq), 0.0, -1e30)

    other = 1 - yh

    def block(xp, q, c):
        return X.at[other, xp * NX + q, c]

    def zshare(xp, k):
        dz = (1, TP - 1, jnp.where(lax.rem(xp, 2) == 0, 2, TP - 2))[k]
        ref = block(xp, quarter, core)
        return pltpu.make_async_remote_copy(
            src_ref=ref, dst_ref=ref, send_sem=zn.at[xp, k], recv_sem=xq.at[xp, quarter, core],
            device_id=(br, seg, lax.rem(z + dz, TP)), device_id_type=MESH)

    def to_sib(xp, q):
        ref = block(xp, q, core)
        return pltpu.make_async_remote_copy(
            src_ref=ref, dst_ref=ref, send_sem=fq.at[xp, q], recv_sem=xq.at[xp, q, core],
            device_id=(sib, seg, z), device_id_type=MESH)

    def block_wait(xp, q, c):
        ref = block(xp, q, c)
        pltpu.make_async_copy(ref, ref, xq.at[xp, q, c]).wait()

    for d in (0, 1, 3, 2):
        xp = lax.rem(x + d, NX)
        block_wait(xp, quarter, core)
        for k in range(3):
            zshare(xp, k).start()
        to_sib(xp, quarter).start()
    pl.semaphore_wait(ra, 2)
    spread(rb4, 4)

    for d in (1, 3, 2):
        for q in range(2):
            row_wait(d, q, core)
            row_side(d, q, None).start()
    for d in (0, 1, 3, 2):
        xp = lax.rem(x + d, NX)
        for k in (1, 3, 2):
            q = lax.rem(quarter + k, NX)
            block_wait(xp, q, core)
            to_sib(xp, q).start()

    @drains.append
    def _():
        for d in range(1, NX):
            for q in range(2):
                row_side(d, q, None).wait_send()
        for xp in range(NX):
            for k in range(3):
                zshare(xp, k).wait_send()
            for q in range(4):
                to_sib(xp, q).wait_send()

    for d in range(NX):
        for q in range(2):
            row_wait(d, q, 1 - core)
    for q in range(2):
        row_wait(0, q, core)
    for xp in range(NX):
        for q in range(4):
            block_wait(xp, q, 1 - core)

    def norm(g, _):
        gy, gx = g // NX, lax.rem(g, NX)
        scale = []
        for c in range(2):
            row = jnp.sum(X[gy, gx * NX, c][ROWS:, :LANES].astype(f32), axis=0, keepdims=True)
            scale.append(jnp.sum(jnp.where(diag, row, 0.0), axis=-1, keepdims=True))
        for q in range(4):
            g0 = pl.multiple_of(((q // 2) * NX + x) * KS + (q % 2) * HK, HK)
            gain = gain_v[:, pl.ds(g0, HK)].astype(f32)
            v = jnp.concatenate([X[gy, gx * NX + q, c].astype(f32)[:ROWS] * scale[c] for c in range(2)], axis=0)
            N[g, :, q * HK:(q + 1) * HK] = (v * gain).astype(bf)
        return 0

    lax.fori_loop(0, 2 * NX, norm, 0)

    def psend(c, d):
        return pltpu.make_async_remote_copy(
            src_ref=pbuf.at[c, d - 1], dst_ref=rbuf.at[c, d - 1], send_sem=ps.at[c, d - 1], recv_sem=pr.at[c, d - 1],
            device_id=(br, xpeer(d), z), device_id_type=MESH)

    def ysend(c):
        return pltpu.make_async_remote_copy(
            src_ref=ybuf.at[c], dst_ref=qf.at[c, yl], send_sem=ys.at[c], recv_sem=yr.at[c],
            device_id=(br, part_seg, z), device_id_type=MESH)

    def produce(c):
        wsend(c).wait_recv()
        lhs = N[...].reshape(8 * HALF, 2 * KS)
        acc = jnp.dot(lhs[:, :KS], wA[0, c], preferred_element_type=f32)
        acc = acc + jnp.dot(lhs[:, KS:], wA[1, c], preferred_element_type=f32)
        pf[...] = acc.reshape(16, PIECE, 8, LANES)
        left = pf[:, 8].reshape(128, LANES)
        lx = lax.broadcasted_iota(i32, (16, 8, LANES), 1)
        left = left.reshape(16, 8, LANES)
        for d in range(NX):
            xd = lax.rem(x + d, NX)
            for k in range(2):
                s = k * NX + xd
                main = pf[:, s].reshape(128, LANES)
                tail = jnp.sum(jnp.where(lx == s, left, 0.0), axis=1)
                v = jnp.concatenate([main, tail], axis=0)
                if d == 0:
                    fown[c, k] = v
                else:
                    pbuf[c, d - 1, k] = v.astype(bf)
            if d:
                psend(c, d).start()

    def consume(c):
        tot = fown[c]
        for d in range(1, NX):
            psend(c, d).wait_recv()
            tot = tot + rbuf[c, d - 1].astype(f32)
        fown[c] = tot
        ybuf[c] = fown[c, 1 - yl].astype(bf)
        ysend(c).start()
        qf[c, yl] = fown[c, yl].astype(bf)

    slot = z // 8

    def kv_send(e):
        return pltpu.make_async_remote_copy(
            src_ref=qf.at[0], dst_ref=kvb.at[slot], send_sem=kvs.at[e], recv_sem=kvr.at[slot],
            device_id=(br, seg, 2 * lax.rem(z, 8) + e), device_id_type=MESH)

    keep = pltpu.make_async_copy(qf.at[0], kvb.at[slot], kvr.at[slot])

    def kv_start():
        pl.semaphore_wait(rb4, 2)
        ysend(0).wait_recv()
        for e in range(2):
            here = 2 * lax.rem(z, 8) + e == z

            @pl.when(here)
            def _():
                keep.start()

            @pl.when(jnp.logical_not(here))
            def _():
                kv_send(e).start()

    def chunk(c, _):
        produce(c)

        @pl.when(c > 0)
        def _():
            consume(c - 1)

        @pl.when(c == 2)
        def _():
            kv_start()
        return 0

    lax.fori_loop(0, CHUNKS, chunk, 0)

    @drains.append
    def _():
        def drain(c, _):
            for d in range(1, NX):
                psend(c, d).wait_send()
            ysend(c).wait_send()
            return 0

        lax.fori_loop(0, CHUNKS, drain, 0)
        for e in range(2):
            @pl.when(2 * lax.rem(z, 8) + e != z)
            def _():
                kv_send(e).wait_send()

    for o in range(1, BR):
        frm = lax.rem(br + o, BR)
        pltpu.make_async_copy(hwb.at[frm], hwb.at[frm], hr.at[frm]).wait()
    hwb[br] = hwf[...]
    hw4 = jnp.concatenate([hwb[m] for m in range(BR)] + [jnp.zeros((4, WIDTH), f32)], axis=0).astype(bf)
    c0 = pl.multiple_of(z * WIDTH, WIDTH)
    direct = lax.dot_general(hw4, roll[:, pl.ds(c0, WIDTH)], (((1,), (1,)), ((), ())), preferred_element_type=f32)
    lanes16 = lax.broadcasted_iota(i32, (16, LANES), 1)
    table = jnp.concatenate(
        [jnp.concatenate([order_i[s * 8:(s + 1) * 8], order_i[64:72]], axis=0) == lanes16 for s in range(SEG)], axis=1)
    table = table.astype(f32).astype(bf)

    consume(CHUNKS - 1)
    for k in range(2):
        pltpu.make_async_copy(kvb.at[k], kvb.at[k], kvr.at[k]).wait()
    keys, values = kvb[0].reshape(PACK, LANES), kvb[1].reshape(PACK, LANES)
    acc = jnp.zeros((PACK, LANES), f32)
    for h in range(HEADS_HERE):
        ysend(h + 1).wait_recv()
        logits = lax.dot_general(qf[h + 1].reshape(PACK, LANES), keys, (((1,), (1,)), ((), ())),
                                 preferred_element_type=f32)
        logits = logits * (1.0 / math.sqrt(LANES)) + bias[...]
        expo = jnp.exp(logits - jnp.max(logits, axis=-1, keepdims=True))
        probs = (expo * (1.0 / jnp.sum(expo, axis=-1, keepdims=True))).astype(bf)
        att = jnp.dot(probs, values, preferred_element_type=f32)
        acc = acc + att * ha_v[:, h * LANES:(h + 1) * LANES].astype(f32)
    through = jnp.sum(acc, axis=-1, keepdims=True)
    sub = lax.broadcasted_iota(i32, (128, LANES), 0)
    lane = lax.broadcasted_iota(i32, (128, LANES), 1)
    for k in range(2):
        rows = through[k * HALF:(k + 1) * HALF]
        main = jnp.where((sub & 7) == lane, rows[:128], 0.0).reshape(16, 8, LANES).sum(axis=1)
        main = main + jnp.where(lane[:16] == 8 + seg, rows[128:], 0.0)
        tb[k * 16:(k + 1) * 16] = main.reshape(16, 1, LANES)

    def at(b2, s2):
        return (s2 // NX) * 16 + ((b2 // 2) * NX + lax.rem(s2, NX)) * 2 + lax.rem(b2, 2)

    def tsend(o, d):
        b2, s2 = lax.rem(br + o, BR), lax.rem(seg + d, SEG)
        return pltpu.make_async_remote_copy(
            src_ref=tb.at[at(b2, s2)], dst_ref=rb.at[br * SEG + seg], send_sem=ts, recv_sem=tr,
            device_id=(b2, s2, z), device_id_type=MESH)

    for o in range(BR):
        for d in range(SEG):
            if o or d:
                tsend(o, d).start()
    pltpu.make_async_copy(tb.at[at(br, seg)], rb.at[br * SEG + seg], tr).start()
    pltpu.make_async_copy(rb, rb, tr).wait()

    @drains.append
    def _():
        pltpu.make_async_copy(tb.at[pl.ds(0, 31)], tb.at[pl.ds(0, 31)], ts).wait()

    got = rb[...].reshape(32, LANES)[:, :16]
    g_hi = got.astype(bf)
    rest = got - g_hi.astype(f32)
    g_mid = rest.astype(bf)
    g_lo = (rest - g_mid.astype(f32)).astype(bf)
    routed = jnp.dot(g_hi, table, preferred_element_type=f32)
    routed = routed + jnp.dot(g_mid, table, preferred_element_type=f32)
    routed = routed + jnp.dot(g_lo, table, preferred_element_type=f32)
    pack_of = lax.broadcasted_iota(i32, (32, LANES), 0) & 7
    part = jnp.zeros((32, LANES), f32)
    for s in range(SEG):
        part = part + jnp.where(pack_of == s, routed[:, s * LANES:(s + 1) * LANES], 0.0)
    part = part.reshape(BR, SEG, LANES).sum(axis=1)
    zo[...] = jnp.zeros((BR, LANES), f32)
    zo[:, :ROWS] = part[:, :ROWS] + direct[:BR]

    def zsend(d):
        return pltpu.make_async_remote_copy(
            src_ref=zo, dst_ref=zb.at[z], send_sem=zs, recv_sem=zr,
            device_id=(br, seg, lax.rem(z + d, TP)), device_id_type=MESH)

    for d in range(1, TP):
        zsend(d).start()
    pltpu.make_async_copy(zo, zb.at[z], zr).start()
    pltpu.make_async_copy(zb, zb, zr).wait()

    @drains.append
    def _():
        pltpu.make_async_copy(zb.at[pl.ds(0, 15)], zb.at[pl.ds(0, 15)], zs).wait()

    total = zb[0, :, :ROWS]
    for k in range(1, TP):
        total = total + zb[k, :, :ROWS]
    out_ref[...] = total
    finish()


def local(rollout, send_rows, seq_lengths, attn_gain, w_query, w_keyval, head_weight, head_attn):
    vm = pl.BlockSpec(memory_space=pltpu.VMEM)
    sm = pl.BlockSpec(memory_space=pltpu.SMEM)
    hbm = pl.BlockSpec(memory_space=pltpu.HBM)
    bf, f32, dma = jnp.bfloat16, jnp.float32, pltpu.SemaphoreType.DMA
    return pl.pallas_call(
        kernel,
        name="scores",
        out_shape=jax.ShapeDtypeStruct((BR, ROWS), f32),
        in_specs=[vm, sm] + [hbm] * 6,
        out_specs=vm,
        scratch_shapes=[
            pltpu.VMEM((ROWS, D), bf), pltpu.VMEM((1, D), bf), pltpu.VMEM((2, CHUNKS, KS, LANES), bf),
            pltpu.VMEM((1, WIDTH), bf), pltpu.VMEM((1, WIDTH), bf),
            pltpu.VMEM((2 * SEG, MSG, HK), bf),
            pltpu.VMEM((2, TP, 2, MSG, HK), bf),
            pltpu.VMEM((8, HALF, 2 * KS), bf),
            pltpu.VMEM((16, PIECE, 8, LANES), f32),
            pltpu.VMEM((CHUNKS, 3, 2, HALF, LANES), bf),
            pltpu.VMEM((CHUNKS, 3, 2, HALF, LANES), bf),
            pltpu.VMEM((CHUNKS, 2, HALF, LANES), f32),
            pltpu.VMEM((CHUNKS, HALF, LANES), bf),
            pltpu.VMEM((CHUNKS, 2, HALF, LANES), bf),
            pltpu.VMEM((2, 2, HALF, LANES), bf),
            pltpu.VMEM((1, WIDTH), f32), pltpu.VMEM((BR, 1, WIDTH), f32),
            pltpu.VMEM((PACK, PACK), f32),
            pltpu.VMEM((32, 1, LANES), f32), pltpu.VMEM((32, 1, LANES), f32),
            pltpu.VMEM((BR, LANES), f32), pltpu.VMEM((TP, BR, LANES), f32),
            dma((4,)), dma((CHUNKS,)), dma((NX, 2, 2)), dma((NX, 4, 2)), dma((NX, 2)), dma((NX,)),
            dma((NX, 2)), dma((NX, 4)), dma((NX, 3)), dma((CHUNKS,)), dma((CHUNKS,)),
            dma((CHUNKS, 3)), dma((CHUNKS, 3)), dma((CHUNKS,)), dma((CHUNKS,)),
            dma((3,)), dma((BR,)), dma((2,)), dma((2,)), dma, dma, dma, dma,
            pltpu.SemaphoreType.REGULAR, pltpu.SemaphoreType.REGULAR,
        ],
        compiler_params=pltpu.CompilerParams(
            collective_id=0, has_side_effects=True, vmem_limit_bytes=56 << 20),
    )(send_rows.reshape(1, ROWS), seq_lengths, rollout, attn_gain, w_query[0], w_keyval[0], head_weight, head_attn)


def solution(mesh):
    return jax.shard_map(
        local,
        mesh=mesh,
        in_specs=(
            P(("branch", "segment"), None),
            P(("branch", "segment")),
            P("segment", None),
            P("branch", None),
            P("branch", "segment", "tp"),
            P("branch", "segment", "tp"),
            P("branch", "tp"),
            P("branch", "tp"),
        ),
        out_specs=P(None, ("branch", "segment")),
        check_vma=False,
    )
```

```python
import math

import jax
import jax.numpy as jnp
from jax import lax
from jax.experimental import pallas as pl
from jax.experimental.pallas import tpu as pltpu
from jax.sharding import PartitionSpec as P

EPS = 1e-05
MESH = pl.DeviceIdType.MESH

BR, SEG, TP = 4, 8, 16
NX = 4
ROWS = 72
PIECE = 9
PACK = 288
HALF = PACK // 2
D = 8192
KS = D // SEG
HK = KS // 2
LANES = 128
HEADS_HERE = 4
CHUNKS = HEADS_HERE + 1
MSG = 80
WIDTH = HEADS_HERE * LANES


def kernel(send_ref, len_ref, roll_hbm, gain_hbm, wq_hbm, wkv_hbm, hw_hbm, ha_hbm, out_ref,
           roll, gain_v, wA, hw_v, ha_v, y, X, N, pf, lsave, pbuf, rbuf, fown, ybuf, qf, kvb, hwf, hwb, bias, tb, rb, zo, zb,
           ld, lw, xo, xq, so, sd, fo, fq, zn, ws, wr, ps, pr, ys, yr, hs, hr, kvs, kvr, ts, tr, zs, zr, ra, rb4):
    f32, bf, i32 = jnp.float32, jnp.bfloat16, jnp.int32
    br = lax.axis_index("branch")
    seg = lax.axis_index("segment")
    z = lax.axis_index("tp")
    core, yh = lax.rem(br, 2), br // 2
    x, yl = lax.rem(seg, NX), seg // NX
    sib = br + 1 - 2 * core
    far = lax.rem(br + 2, BR)
    part_seg = lax.rem(seg + NX, SEG)
    quarter = lax.rem(z, NX)

    def xpeer(d):
        return yl * NX + lax.rem(x + d, NX)

    ld_roll = pltpu.make_async_copy(roll_hbm, roll, ld.at[0])
    ld_gain = pltpu.make_async_copy(gain_hbm, gain_v, ld.at[1])
    ld_hw = pltpu.make_async_copy(hw_hbm, hw_v, ld.at[2])
    ld_ha = pltpu.make_async_copy(ha_hbm, ha_v, ld.at[3])
    ld_w = [pltpu.make_async_copy(wkv_hbm, wA.at[yl, 0], lw.at[0])]
    for c in range(HEADS_HERE):
        ld_w.append(pltpu.make_async_copy(wq_hbm.at[:, pl.ds(c * LANES, LANES)], wA.at[yl, c + 1], lw.at[c + 1]))
    for c in [ld_roll, ld_hw, ld_gain] + ld_w + [ld_ha]:
        c.start()

    barrier = pltpu.get_barrier_semaphore()

    def greet(dev):
        pl.semaphore_signal(barrier, inc=1, device_id=dev, device_id_type=MESH)

    for d in range(1, NX):
        greet((br, xpeer(d), z))
    for d in range(NX):
        greet((far, xpeer(d), z))
    greet((br, part_seg, z))
    greet((sib, seg, z))
    greet((lax.rem(sib + 2, BR), seg, z))
    for d in (1, 2, TP - 2, TP - 1):
        greet((br, seg, lax.rem(z + d, TP)))

    drains = []

    def finish():
        for f in drains:
            f()
        drains.clear()

    sub = lax.broadcasted_iota(i32, (ROWS, LANES), 0)
    lane = lax.broadcasted_iota(i32, (ROWS, LANES), 1)
    diag = sub == lane
    src = jnp.where(sub < 64, (sub >> 3) * PIECE + (sub & 7), (sub - 64) * PIECE + 8)
    send = jnp.concatenate([send_ref[...].astype(f32), jnp.zeros((1, LANES - ROWS), f32)], axis=1)
    order = jnp.sum(jnp.where(lane == src, send, 0.0), axis=1, keepdims=True)
    order_i = order.astype(i32)
    order_row = jnp.sum(jnp.where(diag, order, 0.0), axis=0, keepdims=True).astype(i32)

    ld_roll.wait()
    xf = roll[...].astype(f32)
    r = lax.rsqrt(jnp.sum(xf * xf, axis=-1, keepdims=True) * (1.0 / D) + EPS)
    r_row = jnp.sum(jnp.where((order_row == sub) & (lane < ROWS), r, 0.0), axis=0, keepdims=True)
    hi = r_row.astype(bf).astype(f32)
    mid = (r_row - hi).astype(bf).astype(f32)
    lo = r_row - hi - mid
    s8 = lax.broadcasted_iota(i32, (8, LANES), 0)
    tail = jnp.where(s8 == 0, hi, jnp.where(s8 == 1, mid, jnp.where(s8 == 2, lo, 0.0)))
    tail = jnp.concatenate([tail] + [jnp.zeros((8, LANES), f32)] * (HK // LANES - 1), axis=1)
    perm = (order_i == lane[:, :ROWS]).astype(f32).astype(bf)
    for c in range(2 * SEG):
        yc = jnp.dot(perm, roll[:, c * HK:(c + 1) * HK], preferred_element_type=f32)
        y[c] = jnp.concatenate([yc, tail], axis=0).astype(bf)
    ld_hw.wait()
    hwf[...] = hw_v[...].astype(f32)
    for c in ld_w:
        c.wait()
    ld_gain.wait()
    ld_ha.wait()

    pl.semaphore_wait(barrier, 14)

    def spread(sem, d):
        for e in (d, TP - d):
            pl.semaphore_signal(sem, inc=1, device_id=(br, seg, lax.rem(z + e, TP)), device_id_type=MESH)

    spread(ra, 2)

    def dist(d):
        xd = lax.rem(x + d, NX)
        return pltpu.make_async_remote_copy(
            src_ref=y.at[(quarter // 2) * SEG + 2 * xd + lax.rem(quarter, 2)], dst_ref=X.at[yh, x * NX + quarter, core],
            send_sem=sd.at[d], recv_sem=xq.at[x, quarter, core], device_id=(far, yl * NX + xd, z), device_id_type=MESH)

    for d in range(NX):
        dist(d).start()

    def wsend(c):
        return pltpu.make_async_remote_copy(
            src_ref=wA.at[yl, c], dst_ref=wA.at[yl, c], send_sem=ws.at[c], recv_sem=wr.at[c],
            device_id=(br, part_seg, z), device_id_type=MESH)

    def w_next(c):
        wsend(c - 2).wait_send()
        wsend(c).start()

    for c in range(2):
        wsend(c).start()

    def row_send(d, q):
        xd = lax.rem(x + d, NX)
        return pltpu.make_async_remote_copy(
            src_ref=y.at[pl.ds(q * SEG + 2 * xd, 2)], dst_ref=X.at[yh, pl.ds(x * NX + 2 * q, 2), core],
            send_sem=so.at[d, q], recv_sem=xo.at[x, core, q], device_id=(br, yl * NX + xd, z), device_id_type=MESH)

    def row_keep(q):
        return pltpu.make_async_copy(
            y.at[pl.ds(q * SEG + 2 * x, 2)], X.at[yh, pl.ds(x * NX + 2 * q, 2), core], xo.at[x, core, q])

    def row_side(d, q, src_ref):
        xs = lax.rem(x + d, NX)
        dst = X.at[yh, pl.ds(xs * NX + 2 * q, 2), core]
        return pltpu.make_async_remote_copy(
            src_ref=dst if src_ref is None else src_ref, dst_ref=dst, send_sem=fo.at[d, q],
            recv_sem=xo.at[xs, core, q], device_id=(sib, seg, z), device_id_type=MESH)

    def row_wait(d, q, c):
        xs = lax.rem(x + d, NX)
        ref = X.at[yh, pl.ds(xs * NX + 2 * q, 2), c]
        pltpu.make_async_copy(ref, ref, xo.at[xs, c, q]).wait()

    for d in (1, 3, 2):
        for q in range(2):
            row_send(d, q).start()
    for q in range(2):
        row_keep(q).start()
        row_side(0, q, y.at[pl.ds(q * SEG + 2 * x, 2)]).start()

    def hw_send(o):
        return pltpu.make_async_remote_copy(
            src_ref=hwf, dst_ref=hwb.at[br], send_sem=hs.at[o - 1], recv_sem=hr.at[br],
            device_id=(lax.rem(br + o, BR), seg, z), device_id_type=MESH)

    for o in range(1, BR):
        hw_send(o).start()

    @drains.append
    def _():
        for d in range(NX):
            dist(d).wait_send()
        for c in range(CHUNKS - 2, CHUNKS):
            wsend(c).wait_send()
        for d in range(1, NX):
            for q in range(2):
                row_send(d, q).wait_send()
        for q in range(2):
            row_side(0, q, y.at[pl.ds(q * SEG + 2 * x, 2)]).wait_send()
        for o in range(1, BR):
            hw_send(o).wait_send()

    rq = lax.broadcasted_iota(i32, (PACK, PACK), 0)
    rk = lax.broadcasted_iota(i32, (PACK, PACK), 1)

    def position(p):
        low = (p >= HALF).astype(i32)
        u = p - low * HALF
        left = u >= 128
        sh = jnp.where(left, u - 128, u >> 3)
        i = jnp.where(left, 8, u & 7)
        hi_row = jnp.where(sh >= 8, 1 - yh, yh)
        g = (hi_row * 2 + (sh & 1)) * SEG + low * NX + ((sh >> 1) & 3)
        return g * PIECE + i

    pq, pk = position(rq), position(rk)
    start = jnp.zeros((PACK, PACK), i32)
    end = jnp.int32(0)
    for e in range(len_ref.shape[1]):
        end = end + len_ref[0, e]
        start = jnp.where(pq >= end, end, start)
    bias[...] = jnp.where((pk >= start) & (pk <= pq), 0.0, -1e30)

    other = 1 - yh

    def block(xp, q, c):
        return X.at[other, xp * NX + q, c]

    def zshare(xp, k):
        dz = (1, TP - 1, jnp.where(lax.rem(xp, 2) == 0, 2, TP - 2))[k]
        ref = block(xp, quarter, core)
        return pltpu.make_async_remote_copy(
            src_ref=ref, dst_ref=ref, send_sem=zn.at[xp, k], recv_sem=xq.at[xp, quarter, core],
            device_id=(br, seg, lax.rem(z + dz, TP)), device_id_type=MESH)

    def to_sib(xp, q):
        ref = block(xp, q, core)
        return pltpu.make_async_remote_copy(
            src_ref=ref, dst_ref=ref, send_sem=fq.at[xp, q], recv_sem=xq.at[xp, q, core],
            device_id=(sib, seg, z), device_id_type=MESH)

    def block_wait(xp, q, c):
        ref = block(xp, q, c)
        pltpu.make_async_copy(ref, ref, xq.at[xp, q, c]).wait()

    for d in (0, 1, 3, 2):
        xp = lax.rem(x + d, NX)
        block_wait(xp, quarter, core)
        for k in range(3):
            zshare(xp, k).start()
        to_sib(xp, quarter).start()
    pl.semaphore_wait(ra, 2)
    spread(rb4, 4)

    w_next(2)
    for d in (1, 3, 2):
        for q in range(2):
            row_wait(d, q, core)
            row_side(d, q, None).start()
    w_next(3)

    def norm(g, _):
        gy, gx = g // NX, lax.rem(g, NX)
        scale = []
        for c in range(2):
            row = jnp.sum(X[gy, gx * NX, c][ROWS:, :LANES].astype(f32), axis=0, keepdims=True)
            scale.append(jnp.sum(jnp.where(diag, row, 0.0), axis=-1, keepdims=True))
        for q in range(4):
            g0 = pl.multiple_of(((q // 2) * NX + x) * KS + (q % 2) * HK, HK)
            gain = gain_v[:, pl.ds(g0, HK)].astype(f32)
            v = jnp.concatenate([X[gy, gx * NX + q, c].astype(f32)[:ROWS] * scale[c] for c in range(2)], axis=0)
            N[g, :, q * HK:(q + 1) * HK] = (v * gain).astype(bf)
        return 0

    def psend(c, d, part):
        rows = pl.ds(64 * part, 64 + 16 * part)
        return pltpu.make_async_remote_copy(
            src_ref=pbuf.at[c, d - 1, :, rows], dst_ref=rbuf.at[c, d - 1, :, rows], send_sem=ps.at[c, d - 1, part],
            recv_sem=pr.at[c, d - 1, part], device_id=(br, xpeer(d), z), device_id_type=MESH)

    def ysend(c):
        return pltpu.make_async_remote_copy(
            src_ref=ybuf.at[c], dst_ref=qf.at[c, yl], send_sem=ys.at[c], recv_sem=yr.at[c],
            device_id=(br, part_seg, z), device_id_type=MESH)

    def produce(c, part):
        gy = yh if part == 0 else other
        lhs = N[pl.ds(gy * NX, NX)].reshape(NX * HALF, 2 * KS)
        acc = jnp.dot(lhs[:, :KS], wA[0, c], preferred_element_type=f32)
        acc = acc + jnp.dot(lhs[:, KS:], wA[1, c], preferred_element_type=f32)
        pf[part] = acc.reshape(8, PIECE, 8, LANES)
        left = pf[part, :, 8]
        if part == 0:
            lsave[c] = left
        else:
            left = jnp.concatenate([lsave[c], left], axis=0)
            lx = lax.broadcasted_iota(i32, (16, 8, LANES), 1)
        for d in range(NX):
            xd = lax.rem(x + d, NX)
            for k in range(2):
                s = k * NX + xd
                v = pf[part, :, s].reshape(64, LANES)
                if part:
                    v = jnp.concatenate([v, jnp.sum(jnp.where(lx == s, left, 0.0), axis=1)], axis=0)
                rows = pl.ds(64 * part, 64 + 16 * part)
                if d == 0:
                    fown[c, k, rows] = v
                else:
                    pbuf[c, d - 1, k, rows] = v.astype(bf)
            if d:
                psend(c, d, part).start()

    def consume(c):
        tot = fown[c]
        for d in range(1, NX):
            for part in range(2):
                psend(c, d, part).wait_recv()
            tot = tot + rbuf[c, d - 1].astype(f32)
        fown[c] = tot
        ybuf[c] = fown[c, 1 - yl].astype(bf)
        ysend(c).start()
        qf[c, yl] = fown[c, yl].astype(bf)

    for q in range(2):
        row_wait(0, q, core)
        for d in range(NX):
            row_wait(d, q, 1 - core)

    def norm_own(g, _):
        return norm(yh * NX + g, 0)

    lax.fori_loop(0, NX, norm_own, 0)

    def early(c, _):
        wsend(c).wait_recv()
        produce(c, 0)
        return 0

    lax.fori_loop(0, 2, early, 0)

    for d in (0, 1, 3, 2):
        xp = lax.rem(x + d, NX)
        for k in (1, 3, 2):
            q = lax.rem(quarter + k, NX)
            block_wait(xp, q, core)
            to_sib(xp, q).start()
        if d == 1:
            w_next(4)

    @drains.append
    def _():
        for d in range(1, NX):
            for q in range(2):
                row_side(d, q, None).wait_send()
        for xp in range(NX):
            for k in range(3):
                zshare(xp, k).wait_send()
            for q in range(4):
                to_sib(xp, q).wait_send()

    for xp in range(NX):
        for q in range(4):
            block_wait(xp, q, 1 - core)

    def norm_far(g, _):
        return norm(other * NX + g, 0)

    lax.fori_loop(0, NX, norm_far, 0)

    slot = z // 8

    def kv_send(e):
        return pltpu.make_async_remote_copy(
            src_ref=qf.at[0], dst_ref=kvb.at[slot], send_sem=kvs.at[e], recv_sem=kvr.at[slot],
            device_id=(br, seg, 2 * lax.rem(z, 8) + e), device_id_type=MESH)

    keep = pltpu.make_async_copy(qf.at[0], kvb.at[slot], kvr.at[slot])

    def kv_start():
        pl.semaphore_wait(rb4, 2)
        ysend(0).wait_recv()
        for e in range(2):
            here = 2 * lax.rem(z, 8) + e == z

            @pl.when(here)
            def _():
                keep.start()

            @pl.when(jnp.logical_not(here))
            def _():
                kv_send(e).start()

    def chunk(c, _):
        @pl.when(c >= 2)
        def _():
            wsend(c).wait_recv()
            produce(c, 0)

        produce(c, 1)

        @pl.when(c > 0)
        def _():
            consume(c - 1)

        @pl.when(c == 2)
        def _():
            kv_start()
        return 0

    lax.fori_loop(0, CHUNKS, chunk, 0)

    @drains.append
    def _():
        def drain(c, _):
            for d in range(1, NX):
                for part in range(2):
                    psend(c, d, part).wait_send()
            ysend(c).wait_send()
            return 0

        lax.fori_loop(0, CHUNKS, drain, 0)
        for e in range(2):
            @pl.when(2 * lax.rem(z, 8) + e != z)
            def _():
                kv_send(e).wait_send()

    for o in range(1, BR):
        frm = lax.rem(br + o, BR)
        pltpu.make_async_copy(hwb.at[frm], hwb.at[frm], hr.at[frm]).wait()
    hwb[br] = hwf[...]
    hw4 = jnp.concatenate([hwb[m] for m in range(BR)] + [jnp.zeros((4, WIDTH), f32)], axis=0).astype(bf)
    c0 = pl.multiple_of(z * WIDTH, WIDTH)
    direct = lax.dot_general(hw4, roll[:, pl.ds(c0, WIDTH)], (((1,), (1,)), ((), ())), preferred_element_type=f32)
    lanes16 = lax.broadcasted_iota(i32, (16, LANES), 1)
    table = jnp.concatenate(
        [jnp.concatenate([order_i[s * 8:(s + 1) * 8], order_i[64:72]], axis=0) == lanes16 for s in range(SEG)], axis=1)
    table = table.astype(f32).astype(bf)

    consume(CHUNKS - 1)
    for k in range(2):
        pltpu.make_async_copy(kvb.at[k], kvb.at[k], kvr.at[k]).wait()
    keys, values = kvb[0].reshape(PACK, LANES), kvb[1].reshape(PACK, LANES)
    acc = jnp.zeros((PACK, LANES), f32)
    for h in range(HEADS_HERE):
        ysend(h + 1).wait_recv()
        logits = lax.dot_general(qf[h + 1].reshape(PACK, LANES), keys, (((1,), (1,)), ((), ())),
                                 preferred_element_type=f32)
        logits = logits * (1.0 / math.sqrt(LANES)) + bias[...]
        expo = jnp.exp(logits - jnp.max(logits, axis=-1, keepdims=True))
        probs = (expo * (1.0 / jnp.sum(expo, axis=-1, keepdims=True))).astype(bf)
        att = jnp.dot(probs, values, preferred_element_type=f32)
        acc = acc + att * ha_v[:, h * LANES:(h + 1) * LANES].astype(f32)
    through = jnp.sum(acc, axis=-1, keepdims=True)
    sub = lax.broadcasted_iota(i32, (128, LANES), 0)
    lane = lax.broadcasted_iota(i32, (128, LANES), 1)
    for k in range(2):
        rows = through[k * HALF:(k + 1) * HALF]
        main = jnp.where((sub & 7) == lane, rows[:128], 0.0).reshape(16, 8, LANES).sum(axis=1)
        main = main + jnp.where(lane[:16] == 8 + seg, rows[128:], 0.0)
        tb[k * 16:(k + 1) * 16] = main.reshape(16, 1, LANES)

    def at(b2, s2):
        return (s2 // NX) * 16 + jnp.where(b2 // 2 == yh, 0, 8) + lax.rem(s2, NX) * 2 + lax.rem(b2, 2)

    def tsend(o, d):
        b2, s2 = lax.rem(br + o, BR), lax.rem(seg + d, SEG)
        return pltpu.make_async_remote_copy(
            src_ref=tb.at[at(b2, s2)], dst_ref=rb.at[br * SEG + seg], send_sem=ts, recv_sem=tr,
            device_id=(b2, s2, z), device_id_type=MESH)

    for o in range(BR):
        for d in range(SEG):
            if o or d:
                tsend(o, d).start()
    pltpu.make_async_copy(tb.at[at(br, seg)], rb.at[br * SEG + seg], tr).start()
    finish()
    pltpu.make_async_copy(rb, rb, tr).wait()

    @drains.append
    def _():
        pltpu.make_async_copy(tb.at[pl.ds(0, 31)], tb.at[pl.ds(0, 31)], ts).wait()

    got = rb[...].reshape(32, LANES)[:, :16]
    g_hi = got.astype(bf)
    rest = got - g_hi.astype(f32)
    g_mid = rest.astype(bf)
    g_lo = (rest - g_mid.astype(f32)).astype(bf)
    routed = jnp.dot(g_hi, table, preferred_element_type=f32)
    routed = routed + jnp.dot(g_mid, table, preferred_element_type=f32)
    routed = routed + jnp.dot(g_lo, table, preferred_element_type=f32)
    pack_of = lax.broadcasted_iota(i32, (32, LANES), 0) & 7
    part = jnp.zeros((32, LANES), f32)
    for s in range(SEG):
        part = part + jnp.where(pack_of == s, routed[:, s * LANES:(s + 1) * LANES], 0.0)
    part = part.reshape(BR, SEG, LANES).sum(axis=1)
    zo[...] = jnp.zeros((BR, LANES), f32)
    zo[:, :ROWS] = part[:, :ROWS] + direct[:BR]

    def zsend(d):
        return pltpu.make_async_remote_copy(
            src_ref=zo, dst_ref=zb.at[z], send_sem=zs, recv_sem=zr,
            device_id=(br, seg, lax.rem(z + d, TP)), device_id_type=MESH)

    for d in range(1, TP):
        zsend(d).start()
    pltpu.make_async_copy(zo, zb.at[z], zr).start()
    pltpu.make_async_copy(zb, zb, zr).wait()

    @drains.append
    def _():
        pltpu.make_async_copy(zb.at[pl.ds(0, 15)], zb.at[pl.ds(0, 15)], zs).wait()

    total = zb[0, :, :ROWS]
    for k in range(1, TP):
        total = total + zb[k, :, :ROWS]
    out_ref[...] = total
    finish()


def local(rollout, send_rows, seq_lengths, attn_gain, w_query, w_keyval, head_weight, head_attn):
    vm = pl.BlockSpec(memory_space=pltpu.VMEM)
    sm = pl.BlockSpec(memory_space=pltpu.SMEM)
    hbm = pl.BlockSpec(memory_space=pltpu.HBM)
    bf, f32, dma = jnp.bfloat16, jnp.float32, pltpu.SemaphoreType.DMA
    return pl.pallas_call(
        kernel,
        name="scores",
        out_shape=jax.ShapeDtypeStruct((BR, ROWS), f32),
        in_specs=[vm, sm] + [hbm] * 6,
        out_specs=vm,
        scratch_shapes=[
            pltpu.VMEM((ROWS, D), bf), pltpu.VMEM((1, D), bf), pltpu.VMEM((2, CHUNKS, KS, LANES), bf),
            pltpu.VMEM((1, WIDTH), bf), pltpu.VMEM((1, WIDTH), bf),
            pltpu.VMEM((2 * SEG, MSG, HK), bf),
            pltpu.VMEM((2, TP, 2, MSG, HK), bf),
            pltpu.VMEM((8, HALF, 2 * KS), bf),
            pltpu.VMEM((2, 8, PIECE, 8, LANES), f32),
            pltpu.VMEM((CHUNKS, 8, 8, LANES), f32),
            pltpu.VMEM((CHUNKS, 3, 2, HALF, LANES), bf),
            pltpu.VMEM((CHUNKS, 3, 2, HALF, LANES), bf),
            pltpu.VMEM((CHUNKS, 2, HALF, LANES), f32),
            pltpu.VMEM((CHUNKS, HALF, LANES), bf),
            pltpu.VMEM((CHUNKS, 2, HALF, LANES), bf),
            pltpu.VMEM((2, 2, HALF, LANES), bf),
            pltpu.VMEM((1, WIDTH), f32), pltpu.VMEM((BR, 1, WIDTH), f32),
            pltpu.VMEM((PACK, PACK), f32),
            pltpu.VMEM((32, 1, LANES), f32), pltpu.VMEM((32, 1, LANES), f32),
            pltpu.VMEM((BR, LANES), f32), pltpu.VMEM((TP, BR, LANES), f32),
            dma((4,)), dma((CHUNKS,)), dma((NX, 2, 2)), dma((NX, 4, 2)), dma((NX, 2)), dma((NX,)),
            dma((NX, 2)), dma((NX, 4)), dma((NX, 3)), dma((CHUNKS,)), dma((CHUNKS,)),
            dma((CHUNKS, 3, 2)), dma((CHUNKS, 3, 2)), dma((CHUNKS,)), dma((CHUNKS,)),
            dma((3,)), dma((BR,)), dma((2,)), dma((2,)), dma, dma, dma, dma,
            pltpu.SemaphoreType.REGULAR, pltpu.SemaphoreType.REGULAR,
        ],
        compiler_params=pltpu.CompilerParams(
            collective_id=0, has_side_effects=True, vmem_limit_bytes=56 << 20),
    )(send_rows.reshape(1, ROWS), seq_lengths, rollout, attn_gain, w_query[0], w_keyval[0], head_weight, head_attn)


def solution(mesh):
    return jax.shard_map(
        local,
        mesh=mesh,
        in_specs=(
            P(("branch", "segment"), None),
            P(("branch", "segment")),
            P("segment", None),
            P("branch", None),
            P("branch", "segment", "tp"),
            P("branch", "segment", "tp"),
            P("branch", "tp"),
            P("branch", "tp"),
        ),
        out_specs=P(None, ("branch", "segment")),
        check_vma=False,
    )
```

```python
import math

import jax
import jax.numpy as jnp
from jax import lax
from jax.experimental import pallas as pl
from jax.experimental.pallas import tpu as pltpu
from jax.sharding import PartitionSpec as P

EPS = 1e-05
MESH = pl.DeviceIdType.MESH

BR, SEG, TP = 4, 8, 16
NX = 4
ROWS = 72
PIECE = 9
PACK = 288
HALF = PACK // 2
D = 8192
KS = D // SEG
HK = KS // 2
LANES = 128
HEADS_HERE = 4
CHUNKS = HEADS_HERE + 1
MSG = 80
WIDTH = HEADS_HERE * LANES


def kernel(send_ref, len_ref, roll_hbm, gain_hbm, wq_hbm, wkv_hbm, hw_hbm, ha_hbm, out_ref,
           roll, gain_v, wA, hw_v, ha_v, y, X, N, pf, lsave, pbuf, rbuf, fown, ybuf, qf, kvst, kvb, hwf, hwb, bias, tb, rb, zo, zb,
           ld, lw, xo, xq, so, sd, fo, fq, zn, ws, wr, ps, pr, ys, yr, hs, hr, kvs, kvr, ts, tr, zs, zr, ra, rb4, rc):
    f32, bf, i32 = jnp.float32, jnp.bfloat16, jnp.int32
    br = lax.axis_index("branch")
    seg = lax.axis_index("segment")
    z = lax.axis_index("tp")
    core, yh = lax.rem(br, 2), br // 2
    x, yl = lax.rem(seg, NX), seg // NX
    sib = br + 1 - 2 * core
    far = lax.rem(br + 2, BR)
    part_seg = lax.rem(seg + NX, SEG)
    quarter = lax.rem(z, NX)

    def xpeer(d):
        return yl * NX + lax.rem(x + d, NX)

    ld_roll = pltpu.make_async_copy(roll_hbm, roll, ld.at[0])
    ld_gain = pltpu.make_async_copy(gain_hbm, gain_v, ld.at[1])
    ld_hw = pltpu.make_async_copy(hw_hbm, hw_v, ld.at[2])
    ld_ha = pltpu.make_async_copy(ha_hbm, ha_v, ld.at[3])
    ld_w = [pltpu.make_async_copy(wkv_hbm, wA.at[yl, 0], lw.at[0])]
    for c in range(HEADS_HERE):
        ld_w.append(pltpu.make_async_copy(wq_hbm.at[:, pl.ds(c * LANES, LANES)], wA.at[yl, c + 1], lw.at[c + 1]))
    for c in [ld_roll, ld_hw, ld_gain] + ld_w + [ld_ha]:
        c.start()

    barrier = pltpu.get_barrier_semaphore()

    def greet(dev):
        pl.semaphore_signal(barrier, inc=1, device_id=dev, device_id_type=MESH)

    for d in range(1, NX):
        greet((br, xpeer(d), z))
    for d in range(NX):
        greet((far, xpeer(d), z))
    greet((br, part_seg, z))
    greet((sib, seg, z))
    greet((lax.rem(sib + 2, BR), seg, z))
    for d in (1, 2, TP - 2, TP - 1):
        greet((br, seg, lax.rem(z + d, TP)))

    drains = []

    def finish():
        for f in drains:
            f()
        drains.clear()

    sub = lax.broadcasted_iota(i32, (ROWS, LANES), 0)
    lane = lax.broadcasted_iota(i32, (ROWS, LANES), 1)
    diag = sub == lane
    src = jnp.where(sub < 64, (sub >> 3) * PIECE + (sub & 7), (sub - 64) * PIECE + 8)
    send = jnp.concatenate([send_ref[...].astype(f32), jnp.zeros((1, LANES - ROWS), f32)], axis=1)
    order = jnp.sum(jnp.where(lane == src, send, 0.0), axis=1, keepdims=True)
    order_i = order.astype(i32)
    order_row = jnp.sum(jnp.where(diag, order, 0.0), axis=0, keepdims=True).astype(i32)

    ld_roll.wait()
    xf = roll[...].astype(f32)
    r = lax.rsqrt(jnp.sum(xf * xf, axis=-1, keepdims=True) * (1.0 / D) + EPS)
    r_row = jnp.sum(jnp.where((order_row == sub) & (lane < ROWS), r, 0.0), axis=0, keepdims=True)
    hi = r_row.astype(bf).astype(f32)
    mid = (r_row - hi).astype(bf).astype(f32)
    lo = r_row - hi - mid
    s8 = lax.broadcasted_iota(i32, (8, LANES), 0)
    tail = jnp.where(s8 == 0, hi, jnp.where(s8 == 1, mid, jnp.where(s8 == 2, lo, 0.0)))
    tail = jnp.concatenate([tail] + [jnp.zeros((8, LANES), f32)] * (HK // LANES - 1), axis=1)
    perm = (order_i == lane[:, :ROWS]).astype(f32).astype(bf)
    for c in range(2 * SEG):
        yc = jnp.dot(perm, roll[:, c * HK:(c + 1) * HK], preferred_element_type=f32)
        y[c] = jnp.concatenate([yc, tail], axis=0).astype(bf)
    ld_hw.wait()
    hwf[...] = hw_v[...].astype(f32)
    for c in ld_w:
        c.wait()
    ld_gain.wait()
    ld_ha.wait()

    pl.semaphore_wait(barrier, 14)

    def spread(sem, d):
        for e in (d, TP - d):
            pl.semaphore_signal(sem, inc=1, device_id=(br, seg, lax.rem(z + e, TP)), device_id_type=MESH)

    spread(ra, 2)

    def dist(d):
        xd = lax.rem(x + d, NX)
        return pltpu.make_async_remote_copy(
            src_ref=y.at[(quarter // 2) * SEG + 2 * xd + lax.rem(quarter, 2)], dst_ref=X.at[yh, x * NX + quarter, core],
            send_sem=sd.at[d], recv_sem=xq.at[x, quarter, core], device_id=(far, yl * NX + xd, z), device_id_type=MESH)

    for d in range(NX):
        dist(d).start()

    def wsend(c):
        return pltpu.make_async_remote_copy(
            src_ref=wA.at[yl, c], dst_ref=wA.at[yl, c], send_sem=ws.at[c], recv_sem=wr.at[c],
            device_id=(br, part_seg, z), device_id_type=MESH)

    def w_next(c):
        wsend(c - 2).wait_send()
        wsend(c).start()

    for c in range(2):
        wsend(c).start()

    def row_send(d, q):
        xd = lax.rem(x + d, NX)
        return pltpu.make_async_remote_copy(
            src_ref=y.at[pl.ds(q * SEG + 2 * xd, 2)], dst_ref=X.at[yh, pl.ds(x * NX + 2 * q, 2), core],
            send_sem=so.at[d, q], recv_sem=xo.at[x, core, q], device_id=(br, yl * NX + xd, z), device_id_type=MESH)

    def row_keep(q):
        return pltpu.make_async_copy(
            y.at[pl.ds(q * SEG + 2 * x, 2)], X.at[yh, pl.ds(x * NX + 2 * q, 2), core], xo.at[x, core, q])

    def row_side(d, q, src_ref):
        xs = lax.rem(x + d, NX)
        dst = X.at[yh, pl.ds(xs * NX + 2 * q, 2), core]
        return pltpu.make_async_remote_copy(
            src_ref=dst if src_ref is None else src_ref, dst_ref=dst, send_sem=fo.at[d, q],
            recv_sem=xo.at[xs, core, q], device_id=(sib, seg, z), device_id_type=MESH)

    def row_wait(d, q, c):
        xs = lax.rem(x + d, NX)
        ref = X.at[yh, pl.ds(xs * NX + 2 * q, 2), c]
        pltpu.make_async_copy(ref, ref, xo.at[xs, c, q]).wait()

    for d in (1, 3, 2):
        for q in range(2):
            row_send(d, q).start()
    for q in range(2):
        row_keep(q).start()
        row_side(0, q, y.at[pl.ds(q * SEG + 2 * x, 2)]).start()

    def hw_send(o):
        return pltpu.make_async_remote_copy(
            src_ref=hwf, dst_ref=hwb.at[br], send_sem=hs.at[o - 1], recv_sem=hr.at[br],
            device_id=(lax.rem(br + o, BR), seg, z), device_id_type=MESH)

    for o in range(1, BR):
        hw_send(o).start()

    @drains.append
    def _():
        for d in range(NX):
            dist(d).wait_send()
        for c in range(CHUNKS - 2, CHUNKS):
            wsend(c).wait_send()
        for d in range(1, NX):
            for q in range(2):
                row_send(d, q).wait_send()
        for q in range(2):
            row_side(0, q, y.at[pl.ds(q * SEG + 2 * x, 2)]).wait_send()
        for o in range(1, BR):
            hw_send(o).wait_send()

    rq = lax.broadcasted_iota(i32, (PACK, PACK), 0)
    rk = lax.broadcasted_iota(i32, (PACK, PACK), 1)

    def position(p):
        low = (p >= HALF).astype(i32)
        u = p - low * HALF
        left = u >= 128
        sh = jnp.where(left, u - 128, u >> 3)
        i = jnp.where(left, 8, u & 7)
        hi_row = jnp.where(sh >= 8, 1 - yh, yh)
        g = (hi_row * 2 + (sh & 1)) * SEG + low * NX + ((sh >> 1) & 3)
        return g * PIECE + i

    pq, pk = position(rq), position(rk)
    start = jnp.zeros((PACK, PACK), i32)
    end = jnp.int32(0)
    for e in range(len_ref.shape[1]):
        end = end + len_ref[0, e]
        start = jnp.where(pq >= end, end, start)
    bias[...] = jnp.where((pk >= start) & (pk <= pq), 0.0, -1e30)

    other = 1 - yh

    def block(xp, q, c):
        return X.at[other, xp * NX + q, c]

    def zshare(xp, k):
        dz = (1, TP - 1, jnp.where(lax.rem(xp, 2) == 0, 2, TP - 2))[k]
        ref = block(xp, quarter, core)
        return pltpu.make_async_remote_copy(
            src_ref=ref, dst_ref=ref, send_sem=zn.at[xp, k], recv_sem=xq.at[xp, quarter, core],
            device_id=(br, seg, lax.rem(z + dz, TP)), device_id_type=MESH)

    def to_sib(xp, q):
        ref = block(xp, q, core)
        return pltpu.make_async_remote_copy(
            src_ref=ref, dst_ref=ref, send_sem=fq.at[xp, q], recv_sem=xq.at[xp, q, core],
            device_id=(sib, seg, z), device_id_type=MESH)

    def block_wait(xp, q, c):
        ref = block(xp, q, c)
        pltpu.make_async_copy(ref, ref, xq.at[xp, q, c]).wait()

    for d in (0, 1, 3, 2):
        xp = lax.rem(x + d, NX)
        block_wait(xp, quarter, core)
        for k in range(3):
            zshare(xp, k).start()
        to_sib(xp, quarter).start()
    pl.semaphore_wait(ra, 2)
    spread(rb4, 4)

    w_next(2)
    for d in (1, 3, 2):
        for q in range(2):
            row_wait(d, q, core)
            row_side(d, q, None).start()
    w_next(3)

    def norm(g, _):
        gy, gx = g // NX, lax.rem(g, NX)
        scale = []
        for c in range(2):
            row = jnp.sum(X[gy, gx * NX, c][ROWS:, :LANES].astype(f32), axis=0, keepdims=True)
            scale.append(jnp.sum(jnp.where(diag, row, 0.0), axis=-1, keepdims=True))
        for q in range(4):
            g0 = pl.multiple_of(((q // 2) * NX + x) * KS + (q % 2) * HK, HK)
            gain = gain_v[:, pl.ds(g0, HK)].astype(f32)
            v = jnp.concatenate([X[gy, gx * NX + q, c].astype(f32)[:ROWS] * scale[c] for c in range(2)], axis=0)
            N[g, :, q * HK:(q + 1) * HK] = (v * gain).astype(bf)
        return 0

    def psend(c, d, part):
        rows = pl.ds(64 * part, 64 + 16 * part)
        return pltpu.make_async_remote_copy(
            src_ref=pbuf.at[c, d - 1, :, rows], dst_ref=rbuf.at[c, d - 1, :, rows], send_sem=ps.at[c, d - 1, part],
            recv_sem=pr.at[c, d - 1, part], device_id=(br, xpeer(d), z), device_id_type=MESH)

    def ysend(c):
        return pltpu.make_async_remote_copy(
            src_ref=ybuf.at[c], dst_ref=qf.at[c, yl], send_sem=ys.at[c], recv_sem=yr.at[c],
            device_id=(br, part_seg, z), device_id_type=MESH)

    def produce(c, part):
        gy = yh if part == 0 else other
        lhs = N[pl.ds(gy * NX, NX)].reshape(NX * HALF, 2 * KS)
        acc = jnp.dot(lhs[:, :KS], wA[0, c], preferred_element_type=f32)
        acc = acc + jnp.dot(lhs[:, KS:], wA[1, c], preferred_element_type=f32)
        pf[part] = acc.reshape(8, PIECE, 8, LANES)
        left = pf[part, :, 8]
        if part == 0:
            lsave[c] = left
        else:
            left = jnp.concatenate([lsave[c], left], axis=0)
            lx = lax.broadcasted_iota(i32, (16, 8, LANES), 1)
        for d in range(NX):
            xd = lax.rem(x + d, NX)
            for k in range(2):
                s = k * NX + xd
                v = pf[part, :, s].reshape(64, LANES)
                if part:
                    v = jnp.concatenate([v, jnp.sum(jnp.where(lx == s, left, 0.0), axis=1)], axis=0)
                rows = pl.ds(64 * part, 64 + 16 * part)
                if d == 0:
                    fown[c, k, rows] = v
                else:
                    pbuf[c, d - 1, k, rows] = v.astype(bf)
            if d:
                psend(c, d, part).start()

    def consume(c):
        tot = fown[c]
        for d in range(1, NX):
            for part in range(2):
                psend(c, d, part).wait_recv()
            tot = tot + rbuf[c, d - 1].astype(f32)
        fown[c] = tot
        ybuf[c] = fown[c, 1 - yl].astype(bf)
        ysend(c).start()
        qf[c, yl] = fown[c, yl].astype(bf)

    slot = z // 8

    def kv_rows(part):
        return pl.ds(64 * part, 64 + 16 * part)

    def kv_here(k, e):
        return jnp.logical_and(k == yl, 2 * lax.rem(z, 8) + e == z)

    def kv_send(k, e, part):
        return pltpu.make_async_remote_copy(
            src_ref=kvst.at[k, kv_rows(part)], dst_ref=kvb.at[slot, yl, kv_rows(part)], send_sem=kvs.at[k, e, part],
            recv_sem=kvr.at[slot, yl, part], device_id=(br, k * NX + x, 2 * lax.rem(z, 8) + e), device_id_type=MESH)

    def kv_keep(k, part):
        return pltpu.make_async_copy(
            kvst.at[k, kv_rows(part)], kvb.at[slot, yl, kv_rows(part)], kvr.at[slot, yl, part])

    def consume_kv(part):
        rows = kv_rows(part)
        tot = fown[0, :, rows]
        for d in range(1, NX):
            psend(0, d, part).wait_recv()
            tot = tot + rbuf[0, d - 1, :, rows].astype(f32)
        kvst[:, rows] = tot.astype(bf)
        for k in range(2):
            for e in range(2):
                @pl.when(kv_here(k, e))
                def _():
                    kv_keep(k, part).start()

                @pl.when(jnp.logical_not(kv_here(k, e)))
                def _():
                    kv_send(k, e, part).start()

    pl.semaphore_wait(rb4, 2)
    pl.semaphore_signal(rc, inc=1, device_id=(br, part_seg, z), device_id_type=MESH)

    for q in range(2):
        row_wait(0, q, core)
        for d in range(NX):
            row_wait(d, q, 1 - core)

    def norm_own(g, _):
        return norm(yh * NX + g, 0)

    lax.fori_loop(0, NX, norm_own, 0)

    def early(c, _):
        wsend(c).wait_recv()
        produce(c, 0)
        return 0

    lax.fori_loop(0, 2, early, 0)

    for d in (0, 1, 3, 2):
        xp = lax.rem(x + d, NX)
        for k in (1, 3, 2):
            q = lax.rem(quarter + k, NX)
            block_wait(xp, q, core)
            to_sib(xp, q).start()
        if d == 1:
            w_next(4)
            pl.semaphore_wait(rc, 1)
            consume_kv(0)

    @drains.append
    def _():
        for d in range(1, NX):
            for q in range(2):
                row_side(d, q, None).wait_send()
        for xp in range(NX):
            for k in range(3):
                zshare(xp, k).wait_send()
            for q in range(4):
                to_sib(xp, q).wait_send()

    for xp in range(NX):
        for q in range(4):
            block_wait(xp, q, 1 - core)

    def norm_far(g, _):
        return norm(other * NX + g, 0)

    lax.fori_loop(0, NX, norm_far, 0)

    def chunk(c, _):
        @pl.when(c >= 2)
        def _():
            wsend(c).wait_recv()
            produce(c, 0)

        produce(c, 1)

        @pl.when(c == 1)
        def _():
            consume_kv(1)

        @pl.when(c > 1)
        def _():
            consume(c - 1)
        return 0

    lax.fori_loop(0, CHUNKS, chunk, 0)

    @drains.append
    def _():
        def drain(c, _):
            for d in range(1, NX):
                for part in range(2):
                    psend(c, d, part).wait_send()

            @pl.when(c > 0)
            def _():
                ysend(c).wait_send()
            return 0

        lax.fori_loop(0, CHUNKS, drain, 0)
        for k in range(2):
            for e in range(2):
                @pl.when(jnp.logical_not(kv_here(k, e)))
                def _():
                    for part in range(2):
                        kv_send(k, e, part).wait_send()

    for o in range(1, BR):
        frm = lax.rem(br + o, BR)
        pltpu.make_async_copy(hwb.at[frm], hwb.at[frm], hr.at[frm]).wait()
    hwb[br] = hwf[...]
    hw4 = jnp.concatenate([hwb[m] for m in range(BR)] + [jnp.zeros((4, WIDTH), f32)], axis=0).astype(bf)
    c0 = pl.multiple_of(z * WIDTH, WIDTH)
    direct = lax.dot_general(hw4, roll[:, pl.ds(c0, WIDTH)], (((1,), (1,)), ((), ())), preferred_element_type=f32)
    lanes16 = lax.broadcasted_iota(i32, (16, LANES), 1)
    table = jnp.concatenate(
        [jnp.concatenate([order_i[s * 8:(s + 1) * 8], order_i[64:72]], axis=0) == lanes16 for s in range(SEG)], axis=1)
    table = table.astype(f32).astype(bf)

    consume(CHUNKS - 1)
    for k in range(2):
        for h in range(2):
            for part in range(2):
                ref = kvb.at[k, h, kv_rows(part)]
                pltpu.make_async_copy(ref, ref, kvr.at[k, h, part]).wait()
    keys, values = kvb[0].reshape(PACK, LANES), kvb[1].reshape(PACK, LANES)
    acc = jnp.zeros((PACK, LANES), f32)
    for h in range(HEADS_HERE):
        ysend(h + 1).wait_recv()
        logits = lax.dot_general(qf[h + 1].reshape(PACK, LANES), keys, (((1,), (1,)), ((), ())),
                                 preferred_element_type=f32)
        logits = logits * (1.0 / math.sqrt(LANES)) + bias[...]
        expo = jnp.exp(logits - jnp.max(logits, axis=-1, keepdims=True))
        probs = (expo * (1.0 / jnp.sum(expo, axis=-1, keepdims=True))).astype(bf)
        att = jnp.dot(probs, values, preferred_element_type=f32)
        acc = acc + att * ha_v[:, h * LANES:(h + 1) * LANES].astype(f32)
    through = jnp.sum(acc, axis=-1, keepdims=True)
    sub = lax.broadcasted_iota(i32, (128, LANES), 0)
    lane = lax.broadcasted_iota(i32, (128, LANES), 1)
    for k in range(2):
        rows = through[k * HALF:(k + 1) * HALF]
        main = jnp.where((sub & 7) == lane, rows[:128], 0.0).reshape(16, 8, LANES).sum(axis=1)
        main = main + jnp.where(lane[:16] == 8 + seg, rows[128:], 0.0)
        tb[k * 16:(k + 1) * 16] = main.reshape(16, 1, LANES)

    def at(b2, s2):
        return (s2 // NX) * 16 + jnp.where(b2 // 2 == yh, 0, 8) + lax.rem(s2, NX) * 2 + lax.rem(b2, 2)

    def tsend(o, d):
        b2, s2 = lax.rem(br + o, BR), lax.rem(seg + d, SEG)
        return pltpu.make_async_remote_copy(
            src_ref=tb.at[at(b2, s2)], dst_ref=rb.at[br * SEG + seg], send_sem=ts, recv_sem=tr,
            device_id=(b2, s2, z), device_id_type=MESH)

    for o in range(BR):
        for d in range(SEG):
            if o or d:
                tsend(o, d).start()
    pltpu.make_async_copy(tb.at[at(br, seg)], rb.at[br * SEG + seg], tr).start()
    finish()
    pltpu.make_async_copy(rb, rb, tr).wait()

    @drains.append
    def _():
        pltpu.make_async_copy(tb.at[pl.ds(0, 31)], tb.at[pl.ds(0, 31)], ts).wait()

    got = rb[...].reshape(32, LANES)[:, :16]
    g_hi = got.astype(bf)
    rest = got - g_hi.astype(f32)
    g_mid = rest.astype(bf)
    g_lo = (rest - g_mid.astype(f32)).astype(bf)
    routed = jnp.dot(g_hi, table, preferred_element_type=f32)
    routed = routed + jnp.dot(g_mid, table, preferred_element_type=f32)
    routed = routed + jnp.dot(g_lo, table, preferred_element_type=f32)
    pack_of = lax.broadcasted_iota(i32, (32, LANES), 0) & 7
    part = jnp.zeros((32, LANES), f32)
    for s in range(SEG):
        part = part + jnp.where(pack_of == s, routed[:, s * LANES:(s + 1) * LANES], 0.0)
    part = part.reshape(BR, SEG, LANES).sum(axis=1)
    zo[...] = jnp.zeros((BR, LANES), f32)
    zo[:, :ROWS] = part[:, :ROWS] + direct[:BR]

    def zsend(d):
        return pltpu.make_async_remote_copy(
            src_ref=zo, dst_ref=zb.at[z], send_sem=zs, recv_sem=zr,
            device_id=(br, seg, lax.rem(z + d, TP)), device_id_type=MESH)

    for d in range(1, TP):
        zsend(d).start()
    pltpu.make_async_copy(zo, zb.at[z], zr).start()
    pltpu.make_async_copy(zb, zb, zr).wait()

    @drains.append
    def _():
        pltpu.make_async_copy(zb.at[pl.ds(0, 15)], zb.at[pl.ds(0, 15)], zs).wait()

    total = zb[0, :, :ROWS]
    for k in range(1, TP):
        total = total + zb[k, :, :ROWS]
    out_ref[...] = total
    finish()


def local(rollout, send_rows, seq_lengths, attn_gain, w_query, w_keyval, head_weight, head_attn):
    vm = pl.BlockSpec(memory_space=pltpu.VMEM)
    sm = pl.BlockSpec(memory_space=pltpu.SMEM)
    hbm = pl.BlockSpec(memory_space=pltpu.HBM)
    bf, f32, dma = jnp.bfloat16, jnp.float32, pltpu.SemaphoreType.DMA
    return pl.pallas_call(
        kernel,
        name="scores",
        out_shape=jax.ShapeDtypeStruct((BR, ROWS), f32),
        in_specs=[vm, sm] + [hbm] * 6,
        out_specs=vm,
        scratch_shapes=[
            pltpu.VMEM((ROWS, D), bf), pltpu.VMEM((1, D), bf), pltpu.VMEM((2, CHUNKS, KS, LANES), bf),
            pltpu.VMEM((1, WIDTH), bf), pltpu.VMEM((1, WIDTH), bf),
            pltpu.VMEM((2 * SEG, MSG, HK), bf),
            pltpu.VMEM((2, TP, 2, MSG, HK), bf),
            pltpu.VMEM((8, HALF, 2 * KS), bf),
            pltpu.VMEM((2, 8, PIECE, 8, LANES), f32),
            pltpu.VMEM((CHUNKS, 8, 8, LANES), f32),
            pltpu.VMEM((CHUNKS, 3, 2, HALF, LANES), bf),
            pltpu.VMEM((CHUNKS, 3, 2, HALF, LANES), bf),
            pltpu.VMEM((CHUNKS, 2, HALF, LANES), f32),
            pltpu.VMEM((CHUNKS, HALF, LANES), bf),
            pltpu.VMEM((CHUNKS, 2, HALF, LANES), bf),
            pltpu.VMEM((2, HALF, LANES), bf), pltpu.VMEM((2, 2, HALF, LANES), bf),
            pltpu.VMEM((1, WIDTH), f32), pltpu.VMEM((BR, 1, WIDTH), f32),
            pltpu.VMEM((PACK, PACK), f32),
            pltpu.VMEM((32, 1, LANES), f32), pltpu.VMEM((32, 1, LANES), f32),
            pltpu.VMEM((BR, LANES), f32), pltpu.VMEM((TP, BR, LANES), f32),
            dma((4,)), dma((CHUNKS,)), dma((NX, 2, 2)), dma((NX, 4, 2)), dma((NX, 2)), dma((NX,)),
            dma((NX, 2)), dma((NX, 4)), dma((NX, 3)), dma((CHUNKS,)), dma((CHUNKS,)),
            dma((CHUNKS, 3, 2)), dma((CHUNKS, 3, 2)), dma((CHUNKS,)), dma((CHUNKS,)),
            dma((3,)), dma((BR,)), dma((2, 2, 2)), dma((2, 2, 2)), dma, dma, dma, dma,
            pltpu.SemaphoreType.REGULAR, pltpu.SemaphoreType.REGULAR, pltpu.SemaphoreType.REGULAR,
        ],
        compiler_params=pltpu.CompilerParams(
            collective_id=0, has_side_effects=True, vmem_limit_bytes=56 << 20),
    )(send_rows.reshape(1, ROWS), seq_lengths, rollout, attn_gain, w_query[0], w_keyval[0], head_weight, head_attn)


def solution(mesh):
    return jax.shard_map(
        local,
        mesh=mesh,
        in_specs=(
            P(("branch", "segment"), None),
            P(("branch", "segment")),
            P("segment", None),
            P("branch", None),
            P("branch", "segment", "tp"),
            P("branch", "segment", "tp"),
            P("branch", "tp"),
            P("branch", "tp"),
        ),
        out_specs=P(None, ("branch", "segment")),
        check_vma=False,
    )
```

```python
import math

import jax
import jax.numpy as jnp
from jax import lax
from jax.experimental import pallas as pl
from jax.experimental.pallas import tpu as pltpu
from jax.sharding import PartitionSpec as P

EPS = 1e-05
MESH = pl.DeviceIdType.MESH

BR, SEG, TP = 4, 8, 16
NX = 4
ROWS = 72
PIECE = 9
PACK = 288
HALF = PACK // 2
D = 8192
KS = D // SEG
HK = KS // 2
LANES = 128
HEADS_HERE = 4
CHUNKS = HEADS_HERE + 1
MSG = 80
WIDTH = HEADS_HERE * LANES


def kernel(send_ref, len_ref, roll_hbm, gain_hbm, wq_hbm, wkv_hbm, hw_hbm, ha_hbm, out_ref,
           roll, gain_v, wA, hw_v, ha_v, y, X, N, pf, lsave, pbuf, rbuf, fown, ybuf, qf, kvst, kvb, hwf, hwb, bias, tb, rb, zo, zb,
           ld, lw, xo, xq, so, sd, fo, fq, zn, ws, wr, ps, pr, ys, yr, hs, hr, kvs, kvr, ts, tr, zs, zr, ra, rb4, rc):
    f32, bf, i32 = jnp.float32, jnp.bfloat16, jnp.int32
    br = lax.axis_index("branch")
    seg = lax.axis_index("segment")
    z = lax.axis_index("tp")
    core, yh = lax.rem(br, 2), br // 2
    x, yl = lax.rem(seg, NX), seg // NX
    sib = br + 1 - 2 * core
    far = lax.rem(br + 2, BR)
    part_seg = lax.rem(seg + NX, SEG)
    quarter = lax.rem(z, NX)

    def xpeer(d):
        return yl * NX + lax.rem(x + d, NX)

    ld_roll = pltpu.make_async_copy(roll_hbm, roll, ld.at[0])
    ld_gain = pltpu.make_async_copy(gain_hbm, gain_v, ld.at[1])
    ld_hw = pltpu.make_async_copy(hw_hbm, hw_v, ld.at[2])
    ld_ha = pltpu.make_async_copy(ha_hbm, ha_v, ld.at[3])
    ld_w = [pltpu.make_async_copy(wkv_hbm, wA.at[yl, 0], lw.at[0])]
    for c in range(HEADS_HERE):
        ld_w.append(pltpu.make_async_copy(wq_hbm.at[:, pl.ds(c * LANES, LANES)], wA.at[yl, c + 1], lw.at[c + 1]))
    for c in [ld_roll, ld_hw, ld_gain] + ld_w + [ld_ha]:
        c.start()

    barrier = pltpu.get_barrier_semaphore()

    def greet(dev):
        pl.semaphore_signal(barrier, inc=1, device_id=dev, device_id_type=MESH)

    for d in range(1, NX):
        greet((br, xpeer(d), z))
    for d in range(NX):
        greet((far, xpeer(d), z))
    greet((br, part_seg, z))
    greet((sib, seg, z))
    greet((lax.rem(sib + 2, BR), seg, z))
    for d in (1, 2, TP - 2, TP - 1):
        greet((br, seg, lax.rem(z + d, TP)))

    drains = []

    def finish():
        for f in drains:
            f()
        drains.clear()

    sub = lax.broadcasted_iota(i32, (ROWS, LANES), 0)
    lane = lax.broadcasted_iota(i32, (ROWS, LANES), 1)
    diag = sub == lane
    src = jnp.where(sub < 64, (sub >> 3) * PIECE + (sub & 7), (sub - 64) * PIECE + 8)
    send = jnp.concatenate([send_ref[...].astype(f32), jnp.zeros((1, LANES - ROWS), f32)], axis=1)
    order = jnp.sum(jnp.where(lane == src, send, 0.0), axis=1, keepdims=True)
    order_i = order.astype(i32)
    order_row = jnp.sum(jnp.where(diag, order, 0.0), axis=0, keepdims=True).astype(i32)

    ld_roll.wait()
    xf = roll[...].astype(f32)
    r = lax.rsqrt(jnp.sum(xf * xf, axis=-1, keepdims=True) * (1.0 / D) + EPS)
    r_row = jnp.sum(jnp.where((order_row == sub) & (lane < ROWS), r, 0.0), axis=0, keepdims=True)
    hi = r_row.astype(bf).astype(f32)
    mid = (r_row - hi).astype(bf).astype(f32)
    lo = r_row - hi - mid
    s8 = lax.broadcasted_iota(i32, (8, LANES), 0)
    tail = jnp.where(s8 == 0, hi, jnp.where(s8 == 1, mid, jnp.where(s8 == 2, lo, 0.0)))
    tail = jnp.concatenate([tail] + [jnp.zeros((8, LANES), f32)] * (HK // LANES - 1), axis=1)
    perm = (order_i == lane[:, :ROWS]).astype(f32).astype(bf)
    for c in range(2 * SEG):
        yc = jnp.dot(perm, roll[:, c * HK:(c + 1) * HK], preferred_element_type=f32)
        y[c] = jnp.concatenate([yc, tail], axis=0).astype(bf)
    ld_hw.wait()
    hwf[...] = hw_v[...].astype(f32)
    for c in ld_w:
        c.wait()
    ld_gain.wait()
    ld_ha.wait()

    pl.semaphore_wait(barrier, 14)

    def spread(sem, d):
        for e in (d, TP - d):
            pl.semaphore_signal(sem, inc=1, device_id=(br, seg, lax.rem(z + e, TP)), device_id_type=MESH)

    spread(ra, 2)

    def dist(d):
        xd = lax.rem(x + d, NX)
        return pltpu.make_async_remote_copy(
            src_ref=y.at[(quarter // 2) * SEG + 2 * xd + lax.rem(quarter, 2)], dst_ref=X.at[yh, x * NX + quarter, core],
            send_sem=sd.at[d], recv_sem=xq.at[x, quarter, core], device_id=(far, yl * NX + xd, z), device_id_type=MESH)

    for d in range(NX):
        dist(d).start()

    def wsend(c):
        return pltpu.make_async_remote_copy(
            src_ref=wA.at[yl, c], dst_ref=wA.at[yl, c], send_sem=ws.at[c], recv_sem=wr.at[c],
            device_id=(br, part_seg, z), device_id_type=MESH)

    def w_next(c):
        wsend(c - 2).wait_send()
        wsend(c).start()

    wsend(0).start()

    def row_send(d, q):
        xd = lax.rem(x + d, NX)
        return pltpu.make_async_remote_copy(
            src_ref=y.at[pl.ds(q * SEG + 2 * xd, 2)], dst_ref=X.at[yh, pl.ds(x * NX + 2 * q, 2), core],
            send_sem=so.at[d, q], recv_sem=xo.at[x, core, q], device_id=(br, yl * NX + xd, z), device_id_type=MESH)

    def row_keep(q):
        return pltpu.make_async_copy(
            y.at[pl.ds(q * SEG + 2 * x, 2)], X.at[yh, pl.ds(x * NX + 2 * q, 2), core], xo.at[x, core, q])

    def row_side(d, q, src_ref):
        xs = lax.rem(x + d, NX)
        dst = X.at[yh, pl.ds(xs * NX + 2 * q, 2), core]
        return pltpu.make_async_remote_copy(
            src_ref=dst if src_ref is None else src_ref, dst_ref=dst, send_sem=fo.at[d, q],
            recv_sem=xo.at[xs, core, q], device_id=(sib, seg, z), device_id_type=MESH)

    def row_wait(d, q, c):
        xs = lax.rem(x + d, NX)
        ref = X.at[yh, pl.ds(xs * NX + 2 * q, 2), c]
        pltpu.make_async_copy(ref, ref, xo.at[xs, c, q]).wait()

    for d in (1, 3, 2):
        row_send(d, 0).start()
    for q in range(2):
        row_keep(q).start()
        row_side(0, q, y.at[pl.ds(q * SEG + 2 * x, 2)]).start()

    def hw_send(o):
        return pltpu.make_async_remote_copy(
            src_ref=hwf, dst_ref=hwb.at[br], send_sem=hs.at[o - 1], recv_sem=hr.at[br],
            device_id=(lax.rem(br + o, BR), seg, z), device_id_type=MESH)

    for o in range(1, BR):
        hw_send(o).start()

    @drains.append
    def _():
        for c in range(CHUNKS - 2, CHUNKS):
            wsend(c).wait_send()
        for d in range(1, NX):
            for q in range(2):
                row_send(d, q).wait_send()
        for q in range(2):
            row_side(0, q, y.at[pl.ds(q * SEG + 2 * x, 2)]).wait_send()
        for o in range(1, BR):
            hw_send(o).wait_send()

    rq = lax.broadcasted_iota(i32, (PACK, PACK), 0)
    rk = lax.broadcasted_iota(i32, (PACK, PACK), 1)

    def position(p):
        low = (p >= HALF).astype(i32)
        u = p - low * HALF
        left = u >= 128
        sh = jnp.where(left, u - 128, u >> 3)
        i = jnp.where(left, 8, u & 7)
        hi_row = jnp.where(sh >= 8, 1 - yh, yh)
        g = (hi_row * 2 + (sh & 1)) * SEG + low * NX + ((sh >> 1) & 3)
        return g * PIECE + i

    pq, pk = position(rq), position(rk)
    start = jnp.zeros((PACK, PACK), i32)
    end = jnp.int32(0)
    for e in range(len_ref.shape[1]):
        end = end + len_ref[0, e]
        start = jnp.where(pq >= end, end, start)
    bias[...] = jnp.where((pk >= start) & (pk <= pq), 0.0, -1e30)

    for d in range(NX):
        dist(d).wait_send()
    wsend(1).start()
    for d in (1, 3, 2):
        row_send(d, 1).start()

    other = 1 - yh

    def block(xp, q, c):
        return X.at[other, xp * NX + q, c]

    def zshare(xp, k):
        dz = (1, TP - 1, jnp.where(lax.rem(xp, 2) == 0, 2, TP - 2))[k]
        ref = block(xp, quarter, core)
        return pltpu.make_async_remote_copy(
            src_ref=ref, dst_ref=ref, send_sem=zn.at[xp, k], recv_sem=xq.at[xp, quarter, core],
            device_id=(br, seg, lax.rem(z + dz, TP)), device_id_type=MESH)

    def to_sib(xp, q):
        ref = block(xp, q, core)
        return pltpu.make_async_remote_copy(
            src_ref=ref, dst_ref=ref, send_sem=fq.at[xp, q], recv_sem=xq.at[xp, q, core],
            device_id=(sib, seg, z), device_id_type=MESH)

    def block_wait(xp, q, c):
        ref = block(xp, q, c)
        pltpu.make_async_copy(ref, ref, xq.at[xp, q, c]).wait()

    for d in (0, 1, 3, 2):
        xp = lax.rem(x + d, NX)
        block_wait(xp, quarter, core)
        for k in range(3):
            zshare(xp, k).start()
        to_sib(xp, quarter).start()
    pl.semaphore_wait(ra, 2)
    spread(rb4, 4)

    w_next(2)
    for q in range(2):
        for d in (1, 3, 2):
            row_wait(d, q, core)
            row_side(d, q, None).start()
    w_next(3)

    def norm(g, _):
        gy, gx = g // NX, lax.rem(g, NX)
        scale = []
        for c in range(2):
            row = jnp.sum(X[gy, gx * NX, c][ROWS:, :LANES].astype(f32), axis=0, keepdims=True)
            scale.append(jnp.sum(jnp.where(diag, row, 0.0), axis=-1, keepdims=True))
        for q in range(4):
            g0 = pl.multiple_of(((q // 2) * NX + x) * KS + (q % 2) * HK, HK)
            gain = gain_v[:, pl.ds(g0, HK)].astype(f32)
            v = jnp.concatenate([X[gy, gx * NX + q, c].astype(f32)[:ROWS] * scale[c] for c in range(2)], axis=0)
            N[g, :, q * HK:(q + 1) * HK] = (v * gain).astype(bf)
        return 0

    def psend(c, d, part):
        rows = pl.ds(64 * part, 64 + 16 * part)
        return pltpu.make_async_remote_copy(
            src_ref=pbuf.at[c, d - 1, :, rows], dst_ref=rbuf.at[c, d - 1, :, rows], send_sem=ps.at[c, d - 1, part],
            recv_sem=pr.at[c, d - 1, part], device_id=(br, xpeer(d), z), device_id_type=MESH)

    def ysend(c):
        return pltpu.make_async_remote_copy(
            src_ref=ybuf.at[c], dst_ref=qf.at[c, yl], send_sem=ys.at[c], recv_sem=yr.at[c],
            device_id=(br, part_seg, z), device_id_type=MESH)

    def produce(c, part):
        gy = yh if part == 0 else other
        lhs = N[pl.ds(gy * NX, NX)].reshape(NX * HALF, 2 * KS)
        acc = jnp.dot(lhs[:, :KS], wA[0, c], preferred_element_type=f32)
        acc = acc + jnp.dot(lhs[:, KS:], wA[1, c], preferred_element_type=f32)
        pf[part] = acc.reshape(8, PIECE, 8, LANES)
        left = pf[part, :, 8]
        if part == 0:
            lsave[c] = left
        else:
            left = jnp.concatenate([lsave[c], left], axis=0)
            lx = lax.broadcasted_iota(i32, (16, 8, LANES), 1)
        for d in range(NX):
            xd = lax.rem(x + d, NX)
            for k in range(2):
                s = k * NX + xd
                v = pf[part, :, s].reshape(64, LANES)
                if part:
                    v = jnp.concatenate([v, jnp.sum(jnp.where(lx == s, left, 0.0), axis=1)], axis=0)
                rows = pl.ds(64 * part, 64 + 16 * part)
                if d == 0:
                    fown[c, k, rows] = v
                else:
                    pbuf[c, d - 1, k, rows] = v.astype(bf)
            if d:
                psend(c, d, part).start()

    def consume(c):
        tot = fown[c]
        for d in range(1, NX):
            for part in range(2):
                psend(c, d, part).wait_recv()
            tot = tot + rbuf[c, d - 1].astype(f32)
        fown[c] = tot
        ybuf[c] = fown[c, 1 - yl].astype(bf)
        ysend(c).start()
        qf[c, yl] = fown[c, yl].astype(bf)

    slot = z // 8

    def kv_rows(part):
        return pl.ds(64 * part, 64 + 16 * part)

    def kv_here(k, e):
        return jnp.logical_and(k == yl, 2 * lax.rem(z, 8) + e == z)

    def kv_send(k, e, part):
        return pltpu.make_async_remote_copy(
            src_ref=kvst.at[k, kv_rows(part)], dst_ref=kvb.at[slot, yl, kv_rows(part)], send_sem=kvs.at[k, e, part],
            recv_sem=kvr.at[slot, yl, part], device_id=(br, k * NX + x, 2 * lax.rem(z, 8) + e), device_id_type=MESH)

    def kv_keep(k, part):
        return pltpu.make_async_copy(
            kvst.at[k, kv_rows(part)], kvb.at[slot, yl, kv_rows(part)], kvr.at[slot, yl, part])

    def consume_kv(part):
        rows = kv_rows(part)
        tot = fown[0, :, rows]
        for d in range(1, NX):
            psend(0, d, part).wait_recv()
            tot = tot + rbuf[0, d - 1, :, rows].astype(f32)
        kvst[:, rows] = tot.astype(bf)
        for k in range(2):
            for e in range(2):
                @pl.when(kv_here(k, e))
                def _():
                    kv_keep(k, part).start()

                @pl.when(jnp.logical_not(kv_here(k, e)))
                def _():
                    kv_send(k, e, part).start()

    pl.semaphore_wait(rb4, 2)
    pl.semaphore_signal(rc, inc=1, device_id=(br, part_seg, z), device_id_type=MESH)

    for q in range(2):
        row_wait(0, q, core)
        for d in range(NX):
            row_wait(d, q, 1 - core)

    def norm_own(g, _):
        return norm(yh * NX + g, 0)

    lax.fori_loop(0, NX, norm_own, 0)

    def early(c, _):
        wsend(c).wait_recv()
        produce(c, 0)
        return 0

    lax.fori_loop(0, 2, early, 0)

    for d in (0, 1, 3, 2):
        xp = lax.rem(x + d, NX)
        for k in (1, 3, 2):
            q = lax.rem(quarter + k, NX)
            block_wait(xp, q, core)
            to_sib(xp, q).start()
        if d == 1:
            w_next(4)
            pl.semaphore_wait(rc, 1)
            consume_kv(0)

    @drains.append
    def _():
        for d in range(1, NX):
            for q in range(2):
                row_side(d, q, None).wait_send()
        for xp in range(NX):
            for k in range(3):
                zshare(xp, k).wait_send()
            for q in range(4):
                to_sib(xp, q).wait_send()

    for xp in range(NX):
        for q in range(4):
            block_wait(xp, q, 1 - core)

    def norm_far(g, _):
        return norm(other * NX + g, 0)

    lax.fori_loop(0, NX, norm_far, 0)

    def chunk(c, _):
        @pl.when(c >= 2)
        def _():
            wsend(c).wait_recv()
            produce(c, 0)

        produce(c, 1)

        @pl.when(c == 1)
        def _():
            consume_kv(1)

        @pl.when(c > 1)
        def _():
            consume(c - 1)
        return 0

    lax.fori_loop(0, CHUNKS, chunk, 0)
    finish()

    @drains.append
    def _():
        def drain(c, _):
            for d in range(1, NX):
                for part in range(2):
                    psend(c, d, part).wait_send()

            @pl.when(c > 0)
            def _():
                ysend(c).wait_send()
            return 0

        lax.fori_loop(0, CHUNKS, drain, 0)
        for k in range(2):
            for e in range(2):
                @pl.when(jnp.logical_not(kv_here(k, e)))
                def _():
                    for part in range(2):
                        kv_send(k, e, part).wait_send()

    for o in range(1, BR):
        frm = lax.rem(br + o, BR)
        pltpu.make_async_copy(hwb.at[frm], hwb.at[frm], hr.at[frm]).wait()
    hwb[br] = hwf[...]
    hw4 = jnp.concatenate([hwb[m] for m in range(BR)] + [jnp.zeros((4, WIDTH), f32)], axis=0).astype(bf)
    c0 = pl.multiple_of(z * WIDTH, WIDTH)
    direct = lax.dot_general(hw4, roll[:, pl.ds(c0, WIDTH)], (((1,), (1,)), ((), ())), preferred_element_type=f32)
    lanes16 = lax.broadcasted_iota(i32, (16, LANES), 1)
    table = jnp.concatenate(
        [jnp.concatenate([order_i[s * 8:(s + 1) * 8], order_i[64:72]], axis=0) == lanes16 for s in range(SEG)], axis=1)
    table = table.astype(f32).astype(bf)

    consume(CHUNKS - 1)
    for k in range(2):
        for h in range(2):
            for part in range(2):
                ref = kvb.at[k, h, kv_rows(part)]
                pltpu.make_async_copy(ref, ref, kvr.at[k, h, part]).wait()
    keys, values = kvb[0].reshape(PACK, LANES), kvb[1].reshape(PACK, LANES)
    acc = jnp.zeros((PACK, LANES), f32)
    for h in range(HEADS_HERE):
        ysend(h + 1).wait_recv()
        logits = lax.dot_general(qf[h + 1].reshape(PACK, LANES), keys, (((1,), (1,)), ((), ())),
                                 preferred_element_type=f32)
        logits = logits * (1.0 / math.sqrt(LANES)) + bias[...]
        expo = jnp.exp(logits - jnp.max(logits, axis=-1, keepdims=True))
        probs = (expo * (1.0 / jnp.sum(expo, axis=-1, keepdims=True))).astype(bf)
        att = jnp.dot(probs, values, preferred_element_type=f32)
        acc = acc + att * ha_v[:, h * LANES:(h + 1) * LANES].astype(f32)
    through = jnp.sum(acc, axis=-1, keepdims=True)
    sub = lax.broadcasted_iota(i32, (128, LANES), 0)
    lane = lax.broadcasted_iota(i32, (128, LANES), 1)
    for k in range(2):
        rows = through[k * HALF:(k + 1) * HALF]
        main = jnp.where((sub & 7) == lane, rows[:128], 0.0).reshape(16, 8, LANES).sum(axis=1)
        main = main + jnp.where(lane[:16] == 8 + seg, rows[128:], 0.0)
        tb[k * 16:(k + 1) * 16] = main.reshape(16, 1, LANES)

    def at(b2, s2):
        return (s2 // NX) * 16 + jnp.where(b2 // 2 == yh, 0, 8) + lax.rem(s2, NX) * 2 + lax.rem(b2, 2)

    def tsend(o, d):
        b2, s2 = lax.rem(br + o, BR), lax.rem(seg + d, SEG)
        return pltpu.make_async_remote_copy(
            src_ref=tb.at[at(b2, s2)], dst_ref=rb.at[br * SEG + seg], send_sem=ts, recv_sem=tr,
            device_id=(b2, s2, z), device_id_type=MESH)

    for o in range(BR):
        for d in range(SEG):
            if o or d:
                tsend(o, d).start()
    pltpu.make_async_copy(tb.at[at(br, seg)], rb.at[br * SEG + seg], tr).start()
    finish()
    pltpu.make_async_copy(rb, rb, tr).wait()

    @drains.append
    def _():
        pltpu.make_async_copy(tb.at[pl.ds(0, 31)], tb.at[pl.ds(0, 31)], ts).wait()

    got = rb[...].reshape(32, LANES)[:, :16]
    g_hi = got.astype(bf)
    rest = got - g_hi.astype(f32)
    g_mid = rest.astype(bf)
    g_lo = (rest - g_mid.astype(f32)).astype(bf)
    routed = jnp.dot(g_hi, table, preferred_element_type=f32)
    routed = routed + jnp.dot(g_mid, table, preferred_element_type=f32)
    routed = routed + jnp.dot(g_lo, table, preferred_element_type=f32)
    pack_of = lax.broadcasted_iota(i32, (32, LANES), 0) & 7
    part = jnp.zeros((32, LANES), f32)
    for s in range(SEG):
        part = part + jnp.where(pack_of == s, routed[:, s * LANES:(s + 1) * LANES], 0.0)
    part = part.reshape(BR, SEG, LANES).sum(axis=1)
    zo[...] = jnp.zeros((BR, LANES), f32)
    zo[:, :ROWS] = part[:, :ROWS] + direct[:BR]

    def zsend(d):
        return pltpu.make_async_remote_copy(
            src_ref=zo, dst_ref=zb.at[z], send_sem=zs, recv_sem=zr,
            device_id=(br, seg, lax.rem(z + d, TP)), device_id_type=MESH)

    for d in range(1, TP):
        zsend(d).start()
    pltpu.make_async_copy(zo, zb.at[z], zr).start()
    pltpu.make_async_copy(zb, zb, zr).wait()

    @drains.append
    def _():
        pltpu.make_async_copy(zb.at[pl.ds(0, 15)], zb.at[pl.ds(0, 15)], zs).wait()

    total = zb[0, :, :ROWS]
    for k in range(1, TP):
        total = total + zb[k, :, :ROWS]
    out_ref[...] = total
    finish()


def local(rollout, send_rows, seq_lengths, attn_gain, w_query, w_keyval, head_weight, head_attn):
    vm = pl.BlockSpec(memory_space=pltpu.VMEM)
    sm = pl.BlockSpec(memory_space=pltpu.SMEM)
    hbm = pl.BlockSpec(memory_space=pltpu.HBM)
    bf, f32, dma = jnp.bfloat16, jnp.float32, pltpu.SemaphoreType.DMA
    return pl.pallas_call(
        kernel,
        name="scores",
        out_shape=jax.ShapeDtypeStruct((BR, ROWS), f32),
        in_specs=[vm, sm] + [hbm] * 6,
        out_specs=vm,
        scratch_shapes=[
            pltpu.VMEM((ROWS, D), bf), pltpu.VMEM((1, D), bf), pltpu.VMEM((2, CHUNKS, KS, LANES), bf),
            pltpu.VMEM((1, WIDTH), bf), pltpu.VMEM((1, WIDTH), bf),
            pltpu.VMEM((2 * SEG, MSG, HK), bf),
            pltpu.VMEM((2, TP, 2, MSG, HK), bf),
            pltpu.VMEM((8, HALF, 2 * KS), bf),
            pltpu.VMEM((2, 8, PIECE, 8, LANES), f32),
            pltpu.VMEM((CHUNKS, 8, 8, LANES), f32),
            pltpu.VMEM((CHUNKS, 3, 2, HALF, LANES), bf),
            pltpu.VMEM((CHUNKS, 3, 2, HALF, LANES), bf),
            pltpu.VMEM((CHUNKS, 2, HALF, LANES), f32),
            pltpu.VMEM((CHUNKS, HALF, LANES), bf),
            pltpu.VMEM((CHUNKS, 2, HALF, LANES), bf),
            pltpu.VMEM((2, HALF, LANES), bf), pltpu.VMEM((2, 2, HALF, LANES), bf),
            pltpu.VMEM((1, WIDTH), f32), pltpu.VMEM((BR, 1, WIDTH), f32),
            pltpu.VMEM((PACK, PACK), f32),
            pltpu.VMEM((32, 1, LANES), f32), pltpu.VMEM((32, 1, LANES), f32),
            pltpu.VMEM((BR, LANES), f32), pltpu.VMEM((TP, BR, LANES), f32),
            dma((4,)), dma((CHUNKS,)), dma((NX, 2, 2)), dma((NX, 4, 2)), dma((NX, 2)), dma((NX,)),
            dma((NX, 2)), dma((NX, 4)), dma((NX, 3)), dma((CHUNKS,)), dma((CHUNKS,)),
            dma((CHUNKS, 3, 2)), dma((CHUNKS, 3, 2)), dma((CHUNKS,)), dma((CHUNKS,)),
            dma((3,)), dma((BR,)), dma((2, 2, 2)), dma((2, 2, 2)), dma, dma, dma, dma,
            pltpu.SemaphoreType.REGULAR, pltpu.SemaphoreType.REGULAR, pltpu.SemaphoreType.REGULAR,
        ],
        compiler_params=pltpu.CompilerParams(
            collective_id=0, has_side_effects=True, vmem_limit_bytes=56 << 20),
    )(send_rows.reshape(1, ROWS), seq_lengths, rollout, attn_gain, w_query[0], w_keyval[0], head_weight, head_attn)


def solution(mesh):
    return jax.shard_map(
        local,
        mesh=mesh,
        in_specs=(
            P(("branch", "segment"), None),
            P(("branch", "segment")),
            P("segment", None),
            P("branch", None),
            P("branch", "segment", "tp"),
            P("branch", "segment", "tp"),
            P("branch", "tp"),
            P("branch", "tp"),
        ),
        out_specs=P(None, ("branch", "segment")),
        check_vma=False,
    )
```

```python
import math

import jax
import jax.numpy as jnp
from jax import lax
from jax.experimental import pallas as pl
from jax.experimental.pallas import tpu as pltpu
from jax.sharding import PartitionSpec as P

EPS = 1e-05
MESH = pl.DeviceIdType.MESH

BR, SEG, TP = 4, 8, 16
NX = 4
ROWS = 72
PIECE = 9
PACK = 288
HALF = PACK // 2
D = 8192
KS = D // SEG
HK = KS // 2
LANES = 128
HEADS_HERE = 4
CHUNKS = HEADS_HERE + 1
MSG = 80
WIDTH = HEADS_HERE * LANES


def kernel(send_ref, len_ref, roll_hbm, gain_hbm, wq_hbm, wkv_hbm, hw_hbm, ha_hbm, out_ref,
           roll, gain_v, wA, hw_v, ha_v, y, X, N, pf, lsave, pbuf, rbuf, fown, ybuf, qf, kvst, kvb, hwf, hwb, bias, tb, rb, zo, zb,
           ld, lw, xo, xq, so, sd, fo, fq, zn, ws, wr, ps, pr, ys, yr, hs, hr, kvs, kvr, ts, tr, zs, zr, ra, rb4, rc):
    f32, bf, i32 = jnp.float32, jnp.bfloat16, jnp.int32
    br = lax.axis_index("branch")
    seg = lax.axis_index("segment")
    z = lax.axis_index("tp")
    core, yh = lax.rem(br, 2), br // 2
    x, yl = lax.rem(seg, NX), seg // NX
    sib = br + 1 - 2 * core
    far = lax.rem(br + 2, BR)
    part_seg = lax.rem(seg + NX, SEG)
    quarter = lax.rem(z, NX)

    def xpeer(d):
        return yl * NX + lax.rem(x + d, NX)

    ld_roll = pltpu.make_async_copy(roll_hbm, roll, ld.at[0])
    ld_gain = pltpu.make_async_copy(gain_hbm, gain_v, ld.at[1])
    ld_hw = pltpu.make_async_copy(hw_hbm, hw_v, ld.at[2])
    ld_ha = pltpu.make_async_copy(ha_hbm, ha_v, ld.at[3])
    ld_w = [pltpu.make_async_copy(wkv_hbm, wA.at[yl, 0], lw.at[0])]
    for c in range(HEADS_HERE):
        ld_w.append(pltpu.make_async_copy(wq_hbm.at[:, pl.ds(c * LANES, LANES)], wA.at[yl, c + 1], lw.at[c + 1]))
    for c in [ld_roll, ld_hw, ld_gain] + ld_w + [ld_ha]:
        c.start()

    barrier = pltpu.get_barrier_semaphore()

    def greet(dev):
        pl.semaphore_signal(barrier, inc=1, device_id=dev, device_id_type=MESH)

    for d in range(1, NX):
        greet((br, xpeer(d), z))
    for d in range(NX):
        greet((far, xpeer(d), z))
    greet((br, part_seg, z))
    greet((sib, seg, z))
    greet((lax.rem(sib + 2, BR), seg, z))
    for d in (1, 2, TP - 2, TP - 1):
        greet((br, seg, lax.rem(z + d, TP)))

    drains = []

    def finish():
        for f in drains:
            f()
        drains.clear()

    sub = lax.broadcasted_iota(i32, (ROWS, LANES), 0)
    lane = lax.broadcasted_iota(i32, (ROWS, LANES), 1)
    diag = sub == lane
    src = jnp.where(sub < 64, (sub >> 3) * PIECE + (sub & 7), (sub - 64) * PIECE + 8)
    send = jnp.concatenate([send_ref[...].astype(f32), jnp.zeros((1, LANES - ROWS), f32)], axis=1)
    order = jnp.sum(jnp.where(lane == src, send, 0.0), axis=1, keepdims=True)
    order_i = order.astype(i32)
    order_row = jnp.sum(jnp.where(diag, order, 0.0), axis=0, keepdims=True).astype(i32)

    ld_roll.wait()
    xf = roll[...].astype(f32)
    r = lax.rsqrt(jnp.sum(xf * xf, axis=-1, keepdims=True) * (1.0 / D) + EPS)
    r_row = jnp.sum(jnp.where((order_row == sub) & (lane < ROWS), r, 0.0), axis=0, keepdims=True)
    hi = r_row.astype(bf).astype(f32)
    mid = (r_row - hi).astype(bf).astype(f32)
    lo = r_row - hi - mid
    s8 = lax.broadcasted_iota(i32, (8, LANES), 0)
    tail = jnp.where(s8 == 0, hi, jnp.where(s8 == 1, mid, jnp.where(s8 == 2, lo, 0.0)))
    tail = jnp.concatenate([tail] + [jnp.zeros((8, LANES), f32)] * (HK // LANES - 1), axis=1)
    perm = (order_i == lane[:, :ROWS]).astype(f32).astype(bf)
    for c in range(2 * SEG):
        yc = jnp.dot(perm, roll[:, c * HK:(c + 1) * HK], preferred_element_type=f32)
        y[c] = jnp.concatenate([yc, tail], axis=0).astype(bf)
    ld_hw.wait()
    hwf[...] = hw_v[...].astype(f32)
    for c in ld_w:
        c.wait()
    ld_gain.wait()
    ld_ha.wait()

    pl.semaphore_wait(barrier, 14)

    def spread(sem, d):
        for e in (d, TP - d):
            pl.semaphore_signal(sem, inc=1, device_id=(br, seg, lax.rem(z + e, TP)), device_id_type=MESH)

    spread(ra, 2)

    def dist(d):
        xd = lax.rem(x + d, NX)
        return pltpu.make_async_remote_copy(
            src_ref=y.at[(quarter // 2) * SEG + 2 * xd + lax.rem(quarter, 2)], dst_ref=X.at[yh, x * NX + quarter, core],
            send_sem=sd.at[d], recv_sem=xq.at[x, quarter, core], device_id=(far, yl * NX + xd, z), device_id_type=MESH)

    for d in range(NX):
        dist(d).start()

    def wsend(c):
        return pltpu.make_async_remote_copy(
            src_ref=wA.at[yl, c], dst_ref=wA.at[yl, c], send_sem=ws.at[c], recv_sem=wr.at[c],
            device_id=(br, part_seg, z), device_id_type=MESH)

    def w_next(c):
        wsend(c - 2).wait_send()
        wsend(c).start()

    wsend(0).start()

    def row_send(d, q):
        xd = lax.rem(x + d, NX)
        return pltpu.make_async_remote_copy(
            src_ref=y.at[pl.ds(q * SEG + 2 * xd, 2)], dst_ref=X.at[yh, pl.ds(x * NX + 2 * q, 2), core],
            send_sem=so.at[d, q], recv_sem=xo.at[x, core, q], device_id=(br, yl * NX + xd, z), device_id_type=MESH)

    def row_keep(q):
        return pltpu.make_async_copy(
            y.at[pl.ds(q * SEG + 2 * x, 2)], X.at[yh, pl.ds(x * NX + 2 * q, 2), core], xo.at[x, core, q])

    def row_side(d, q, src_ref):
        xs = lax.rem(x + d, NX)
        dst = X.at[yh, pl.ds(xs * NX + 2 * q, 2), core]
        return pltpu.make_async_remote_copy(
            src_ref=dst if src_ref is None else src_ref, dst_ref=dst, send_sem=fo.at[d, q],
            recv_sem=xo.at[xs, core, q], device_id=(sib, seg, z), device_id_type=MESH)

    def row_wait(d, q, c):
        xs = lax.rem(x + d, NX)
        ref = X.at[yh, pl.ds(xs * NX + 2 * q, 2), c]
        pltpu.make_async_copy(ref, ref, xo.at[xs, c, q]).wait()

    for d in (1, 3, 2):
        row_send(d, 0).start()
    for q in range(2):
        row_keep(q).start()
        row_side(0, q, y.at[pl.ds(q * SEG + 2 * x, 2)]).start()

    def hw_send(o):
        return pltpu.make_async_remote_copy(
            src_ref=hwf, dst_ref=hwb.at[br], send_sem=hs.at[o - 1], recv_sem=hr.at[br],
            device_id=(lax.rem(br + o, BR), seg, z), device_id_type=MESH)

    for o in range(1, BR):
        hw_send(o).start()

    @drains.append
    def _():
        for c in range(CHUNKS - 2, CHUNKS):
            wsend(c).wait_send()
        for d in range(1, NX):
            for q in range(2):
                row_send(d, q).wait_send()
        for q in range(2):
            row_side(0, q, y.at[pl.ds(q * SEG + 2 * x, 2)]).wait_send()
        for o in range(1, BR):
            hw_send(o).wait_send()

    rq = lax.broadcasted_iota(i32, (PACK, PACK), 0)
    rk = lax.broadcasted_iota(i32, (PACK, PACK), 1)

    def position(p):
        low = (p >= HALF).astype(i32)
        u = p - low * HALF
        left = u >= 128
        sh = jnp.where(left, u - 128, u >> 3)
        i = jnp.where(left, 8, u & 7)
        hi_row = jnp.where(sh >= 8, 1 - yh, yh)
        g = (hi_row * 2 + (sh & 1)) * SEG + low * NX + ((sh >> 1) & 3)
        return g * PIECE + i

    pq, pk = position(rq), position(rk)
    start = jnp.zeros((PACK, PACK), i32)
    end = jnp.int32(0)
    for e in range(len_ref.shape[1]):
        end = end + len_ref[0, e]
        start = jnp.where(pq >= end, end, start)
    bias[...] = jnp.where((pk >= start) & (pk <= pq), 0.0, -1e30)

    for d in range(NX):
        dist(d).wait_send()
    wsend(1).start()
    for d in (1, 3, 2):
        row_send(d, 1).start()

    other = 1 - yh

    def block(xp, q, c):
        return X.at[other, xp * NX + q, c]

    def zshare(xp, k):
        dz = (1, TP - 1, jnp.where(lax.rem(xp, 2) == 0, 2, TP - 2))[k]
        ref = block(xp, quarter, core)
        return pltpu.make_async_remote_copy(
            src_ref=ref, dst_ref=ref, send_sem=zn.at[xp, k], recv_sem=xq.at[xp, quarter, core],
            device_id=(br, seg, lax.rem(z + dz, TP)), device_id_type=MESH)

    def to_sib(xp, q):
        ref = block(xp, q, core)
        return pltpu.make_async_remote_copy(
            src_ref=ref, dst_ref=ref, send_sem=fq.at[xp, q], recv_sem=xq.at[xp, q, core],
            device_id=(sib, seg, z), device_id_type=MESH)

    def block_wait(xp, q, c):
        ref = block(xp, q, c)
        pltpu.make_async_copy(ref, ref, xq.at[xp, q, c]).wait()

    for d in (0, 1, 3, 2):
        xp = lax.rem(x + d, NX)
        block_wait(xp, quarter, core)
        for k in range(3):
            zshare(xp, k).start()
        to_sib(xp, quarter).start()
    pl.semaphore_wait(ra, 2)
    spread(rb4, 4)

    w_next(2)
    for q in range(2):
        for d in (1, 3, 2):
            row_wait(d, q, core)
            row_side(d, q, None).start()
    w_next(3)

    def norm(g, _):
        gy, gx = g // NX, lax.rem(g, NX)
        scale = []
        for c in range(2):
            row = jnp.sum(X[gy, gx * NX, c][ROWS:, :LANES].astype(f32), axis=0, keepdims=True)
            scale.append(jnp.sum(jnp.where(diag, row, 0.0), axis=-1, keepdims=True))
        for q in range(4):
            g0 = pl.multiple_of(((q // 2) * NX + x) * KS + (q % 2) * HK, HK)
            gain = gain_v[:, pl.ds(g0, HK)].astype(f32)
            v = jnp.concatenate([X[gy, gx * NX + q, c].astype(f32)[:ROWS] * scale[c] for c in range(2)], axis=0)
            N[g, :, q * HK:(q + 1) * HK] = (v * gain).astype(bf)
        return 0

    def psend(c, d, part):
        rows = pl.ds(64 * part, 64 + 16 * part)
        return pltpu.make_async_remote_copy(
            src_ref=pbuf.at[c, d - 1, :, rows], dst_ref=rbuf.at[c, d - 1, :, rows], send_sem=ps.at[c, d - 1, part],
            recv_sem=pr.at[c, d - 1, part], device_id=(br, xpeer(d), z), device_id_type=MESH)

    def ysend(c):
        return pltpu.make_async_remote_copy(
            src_ref=ybuf.at[c], dst_ref=qf.at[c, yl], send_sem=ys.at[c], recv_sem=yr.at[c],
            device_id=(br, part_seg, z), device_id_type=MESH)

    def produce(c, part):
        gy = yh if part == 0 else other
        lhs = N[pl.ds(gy * NX, NX)].reshape(NX * HALF, 2 * KS)
        acc = jnp.dot(lhs[:, :KS], wA[0, c], preferred_element_type=f32)
        acc = acc + jnp.dot(lhs[:, KS:], wA[1, c], preferred_element_type=f32)
        pf[part] = acc.reshape(8, PIECE, 8, LANES)
        left = pf[part, :, 8]
        if part == 0:
            lsave[c] = left
        else:
            left = jnp.concatenate([lsave[c], left], axis=0)
            lx = lax.broadcasted_iota(i32, (16, 8, LANES), 1)
        for d in range(NX):
            xd = lax.rem(x + d, NX)
            for k in range(2):
                s = k * NX + xd
                v = pf[part, :, s].reshape(64, LANES)
                if part:
                    v = jnp.concatenate([v, jnp.sum(jnp.where(lx == s, left, 0.0), axis=1)], axis=0)
                rows = pl.ds(64 * part, 64 + 16 * part)
                if d == 0:
                    fown[c, k, rows] = v
                else:
                    pbuf[c, d - 1, k, rows] = v.astype(bf)
            if d:
                psend(c, d, part).start()

    def consume(c):
        tot = fown[c]
        for d in range(1, NX):
            for part in range(2):
                psend(c, d, part).wait_recv()
            tot = tot + rbuf[c, d - 1].astype(f32)
        fown[c] = tot
        ybuf[c] = fown[c, 1 - yl].astype(bf)
        ysend(c).start()
        qf[c, yl] = fown[c, yl].astype(bf)

    slot = z // 8

    def kv_rows(part):
        return pl.ds(64 * part, 64 + 16 * part)

    def kv_here(k, e):
        return jnp.logical_and(k == yl, 2 * lax.rem(z, 8) + e == z)

    def kv_send(k, e, part):
        return pltpu.make_async_remote_copy(
            src_ref=kvst.at[k, kv_rows(part)], dst_ref=kvb.at[slot, yl, kv_rows(part)], send_sem=kvs.at[k, e, part],
            recv_sem=kvr.at[slot, yl, part], device_id=(br, k * NX + x, 2 * lax.rem(z, 8) + e), device_id_type=MESH)

    def kv_keep(k, part):
        return pltpu.make_async_copy(
            kvst.at[k, kv_rows(part)], kvb.at[slot, yl, kv_rows(part)], kvr.at[slot, yl, part])

    def consume_kv(part):
        rows = kv_rows(part)
        tot = fown[0, :, rows]
        for d in range(1, NX):
            psend(0, d, part).wait_recv()
            tot = tot + rbuf[0, d - 1, :, rows].astype(f32)
        kvst[:, rows] = tot.astype(bf)
        for k in range(2):
            for e in range(2):
                @pl.when(kv_here(k, e))
                def _():
                    kv_keep(k, part).start()

                @pl.when(jnp.logical_not(kv_here(k, e)))
                def _():
                    kv_send(k, e, part).start()

    pl.semaphore_wait(rb4, 2)
    pl.semaphore_signal(rc, inc=1, device_id=(br, part_seg, z), device_id_type=MESH)

    for q in range(2):
        row_wait(0, q, core)
        for d in range(NX):
            row_wait(d, q, 1 - core)

    def norm_own(g, _):
        return norm(yh * NX + g, 0)

    lax.fori_loop(0, NX, norm_own, 0)

    def early(c, _):
        wsend(c).wait_recv()
        produce(c, 0)
        return 0

    lax.fori_loop(0, 2, early, 0)

    for d in (0, 1, 3, 2):
        xp = lax.rem(x + d, NX)
        for k in (1, 3, 2):
            q = lax.rem(quarter + k, NX)
            block_wait(xp, q, core)
            to_sib(xp, q).start()
        if d == 1:
            w_next(4)
            pl.semaphore_wait(rc, 1)
            consume_kv(0)
        if d == 3:
            lax.fori_loop(2, 3, early, 0)

    @drains.append
    def _():
        for d in range(1, NX):
            for q in range(2):
                row_side(d, q, None).wait_send()
        for xp in range(NX):
            for k in range(3):
                zshare(xp, k).wait_send()
            for q in range(4):
                to_sib(xp, q).wait_send()

    for xp in range(NX):
        for q in range(4):
            block_wait(xp, q, 1 - core)

    def norm_far(g, _):
        return norm(other * NX + g, 0)

    lax.fori_loop(0, NX, norm_far, 0)

    def chunk(c, _):
        @pl.when(c >= 3)
        def _():
            wsend(c).wait_recv()
            produce(c, 0)

        produce(c, 1)

        @pl.when(c == 2)
        def _():
            consume_kv(1)

        @pl.when(c > 3)
        def _():
            consume(c - 3)
        return 0

    lax.fori_loop(0, CHUNKS, chunk, 0)

    @drains.append
    def _():
        def drain(c, _):
            for d in range(1, NX):
                for part in range(2):
                    psend(c, d, part).wait_send()

            @pl.when(c > 0)
            def _():
                ysend(c).wait_send()
            return 0

        lax.fori_loop(0, CHUNKS, drain, 0)
        for k in range(2):
            for e in range(2):
                @pl.when(jnp.logical_not(kv_here(k, e)))
                def _():
                    for part in range(2):
                        kv_send(k, e, part).wait_send()

    for o in range(1, BR):
        frm = lax.rem(br + o, BR)
        pltpu.make_async_copy(hwb.at[frm], hwb.at[frm], hr.at[frm]).wait()
    hwb[br] = hwf[...]
    hw4 = jnp.concatenate([hwb[m] for m in range(BR)] + [jnp.zeros((4, WIDTH), f32)], axis=0).astype(bf)
    c0 = pl.multiple_of(z * WIDTH, WIDTH)
    direct = lax.dot_general(hw4, roll[:, pl.ds(c0, WIDTH)], (((1,), (1,)), ((), ())), preferred_element_type=f32)
    lanes16 = lax.broadcasted_iota(i32, (16, LANES), 1)
    table = jnp.concatenate(
        [jnp.concatenate([order_i[s * 8:(s + 1) * 8], order_i[64:72]], axis=0) == lanes16 for s in range(SEG)], axis=1)
    table = table.astype(f32).astype(bf)

    consume(CHUNKS - 3)
    consume(CHUNKS - 2)
    consume(CHUNKS - 1)
    for k in range(2):
        for h in range(2):
            for part in range(2):
                ref = kvb.at[k, h, kv_rows(part)]
                pltpu.make_async_copy(ref, ref, kvr.at[k, h, part]).wait()
    keys, values = kvb[0].reshape(PACK, LANES), kvb[1].reshape(PACK, LANES)
    acc = jnp.zeros((PACK, LANES), f32)
    for h in range(HEADS_HERE):
        ysend(h + 1).wait_recv()
        logits = lax.dot_general(qf[h + 1].reshape(PACK, LANES), keys, (((1,), (1,)), ((), ())),
                                 preferred_element_type=f32)
        logits = logits * (1.0 / math.sqrt(LANES)) + bias[...]
        expo = jnp.exp(logits - jnp.max(logits, axis=-1, keepdims=True))
        probs = (expo * (1.0 / jnp.sum(expo, axis=-1, keepdims=True))).astype(bf)
        att = jnp.dot(probs, values, preferred_element_type=f32)
        acc = acc + att * ha_v[:, h * LANES:(h + 1) * LANES].astype(f32)
    through = jnp.sum(acc, axis=-1, keepdims=True)
    sub = lax.broadcasted_iota(i32, (128, LANES), 0)
    lane = lax.broadcasted_iota(i32, (128, LANES), 1)
    for k in range(2):
        rows = through[k * HALF:(k + 1) * HALF]
        main = jnp.where((sub & 7) == lane, rows[:128], 0.0).reshape(16, 8, LANES).sum(axis=1)
        main = main + jnp.where(lane[:16] == 8 + seg, rows[128:], 0.0)
        tb[k * 16:(k + 1) * 16] = main.reshape(16, 1, LANES)

    def at(b2, s2):
        return (s2 // NX) * 16 + jnp.where(b2 // 2 == yh, 0, 8) + lax.rem(s2, NX) * 2 + lax.rem(b2, 2)

    def tsend(o, d):
        b2, s2 = lax.rem(br + o, BR), lax.rem(seg + d, SEG)
        return pltpu.make_async_remote_copy(
            src_ref=tb.at[at(b2, s2)], dst_ref=rb.at[br * SEG + seg], send_sem=ts, recv_sem=tr,
            device_id=(b2, s2, z), device_id_type=MESH)

    for o in range(BR):
        for d in range(SEG):
            if o or d:
                tsend(o, d).start()
    pltpu.make_async_copy(tb.at[at(br, seg)], rb.at[br * SEG + seg], tr).start()
    finish()
    pltpu.make_async_copy(rb, rb, tr).wait()

    @drains.append
    def _():
        pltpu.make_async_copy(tb.at[pl.ds(0, 31)], tb.at[pl.ds(0, 31)], ts).wait()

    got = rb[...].reshape(32, LANES)[:, :16]
    g_hi = got.astype(bf)
    rest = got - g_hi.astype(f32)
    g_mid = rest.astype(bf)
    g_lo = (rest - g_mid.astype(f32)).astype(bf)
    routed = jnp.dot(g_hi, table, preferred_element_type=f32)
    routed = routed + jnp.dot(g_mid, table, preferred_element_type=f32)
    routed = routed + jnp.dot(g_lo, table, preferred_element_type=f32)
    pack_of = lax.broadcasted_iota(i32, (32, LANES), 0) & 7
    part = jnp.zeros((32, LANES), f32)
    for s in range(SEG):
        part = part + jnp.where(pack_of == s, routed[:, s * LANES:(s + 1) * LANES], 0.0)
    part = part.reshape(BR, SEG, LANES).sum(axis=1)
    zo[...] = jnp.zeros((BR, LANES), f32)
    zo[:, :ROWS] = part[:, :ROWS] + direct[:BR]

    def zsend(d):
        return pltpu.make_async_remote_copy(
            src_ref=zo, dst_ref=zb.at[z], send_sem=zs, recv_sem=zr,
            device_id=(br, seg, lax.rem(z + d, TP)), device_id_type=MESH)

    for d in range(1, TP):
        zsend(d).start()
    pltpu.make_async_copy(zo, zb.at[z], zr).start()
    pltpu.make_async_copy(zb, zb, zr).wait()

    @drains.append
    def _():
        pltpu.make_async_copy(zb.at[pl.ds(0, 15)], zb.at[pl.ds(0, 15)], zs).wait()

    total = zb[0, :, :ROWS]
    for k in range(1, TP):
        total = total + zb[k, :, :ROWS]
    out_ref[...] = total
    finish()


def local(rollout, send_rows, seq_lengths, attn_gain, w_query, w_keyval, head_weight, head_attn):
    vm = pl.BlockSpec(memory_space=pltpu.VMEM)
    sm = pl.BlockSpec(memory_space=pltpu.SMEM)
    hbm = pl.BlockSpec(memory_space=pltpu.HBM)
    bf, f32, dma = jnp.bfloat16, jnp.float32, pltpu.SemaphoreType.DMA
    return pl.pallas_call(
        kernel,
        name="scores",
        out_shape=jax.ShapeDtypeStruct((BR, ROWS), f32),
        in_specs=[vm, sm] + [hbm] * 6,
        out_specs=vm,
        scratch_shapes=[
            pltpu.VMEM((ROWS, D), bf), pltpu.VMEM((1, D), bf), pltpu.VMEM((2, CHUNKS, KS, LANES), bf),
            pltpu.VMEM((1, WIDTH), bf), pltpu.VMEM((1, WIDTH), bf),
            pltpu.VMEM((2 * SEG, MSG, HK), bf),
            pltpu.VMEM((2, TP, 2, MSG, HK), bf),
            pltpu.VMEM((8, HALF, 2 * KS), bf),
            pltpu.VMEM((2, 8, PIECE, 8, LANES), f32),
            pltpu.VMEM((CHUNKS, 8, 8, LANES), f32),
            pltpu.VMEM((CHUNKS, 3, 2, HALF, LANES), bf),
            pltpu.VMEM((CHUNKS, 3, 2, HALF, LANES), bf),
            pltpu.VMEM((CHUNKS, 2, HALF, LANES), f32),
            pltpu.VMEM((CHUNKS, HALF, LANES), bf),
            pltpu.VMEM((CHUNKS, 2, HALF, LANES), bf),
            pltpu.VMEM((2, HALF, LANES), bf), pltpu.VMEM((2, 2, HALF, LANES), bf),
            pltpu.VMEM((1, WIDTH), f32), pltpu.VMEM((BR, 1, WIDTH), f32),
            pltpu.VMEM((PACK, PACK), f32),
            pltpu.VMEM((32, 1, LANES), f32), pltpu.VMEM((32, 1, LANES), f32),
            pltpu.VMEM((BR, LANES), f32), pltpu.VMEM((TP, BR, LANES), f32),
            dma((4,)), dma((CHUNKS,)), dma((NX, 2, 2)), dma((NX, 4, 2)), dma((NX, 2)), dma((NX,)),
            dma((NX, 2)), dma((NX, 4)), dma((NX, 3)), dma((CHUNKS,)), dma((CHUNKS,)),
            dma((CHUNKS, 3, 2)), dma((CHUNKS, 3, 2)), dma((CHUNKS,)), dma((CHUNKS,)),
            dma((3,)), dma((BR,)), dma((2, 2, 2)), dma((2, 2, 2)), dma, dma, dma, dma,
            pltpu.SemaphoreType.REGULAR, pltpu.SemaphoreType.REGULAR, pltpu.SemaphoreType.REGULAR,
        ],
        compiler_params=pltpu.CompilerParams(
            collective_id=0, has_side_effects=True, vmem_limit_bytes=56 << 20),
    )(send_rows.reshape(1, ROWS), seq_lengths, rollout, attn_gain, w_query[0], w_keyval[0], head_weight, head_attn)


def solution(mesh):
    return jax.shard_map(
        local,
        mesh=mesh,
        in_specs=(
            P(("branch", "segment"), None),
            P(("branch", "segment")),
            P("segment", None),
            P("branch", None),
            P("branch", "segment", "tp"),
            P("branch", "segment", "tp"),
            P("branch", "tp"),
            P("branch", "tp"),
        ),
        out_specs=P(None, ("branch", "segment")),
        check_vma=False,
    )
```

```python
import math

import jax
import jax.numpy as jnp
from jax import lax
from jax.experimental import pallas as pl
from jax.experimental.pallas import tpu as pltpu
from jax.sharding import PartitionSpec as P

EPS = 1e-05
MESH = pl.DeviceIdType.MESH

BR, SEG, TP = 4, 8, 16
NX = 4
ROWS = 72
PIECE = 9
PACK = 288
HALF = PACK // 2
D = 8192
KS = D // SEG
HK = KS // 2
LANES = 128
HEADS_HERE = 4
CHUNKS = HEADS_HERE + 1
MSG = 80
WIDTH = HEADS_HERE * LANES


def kernel(send_ref, len_ref, roll_hbm, gain_hbm, wq_hbm, wkv_hbm, hw_hbm, ha_hbm, out_ref,
           roll, gain_v, wA, hw_v, ha_v, y, X, N, pf, lsave, pbuf, rbuf, fown, ybuf, qf, kvst, kvb, hwf, hwb, bias, tb, rb, zo, zb,
           ld, lw, xo, xq, so, sd, fo, fq, zn, ws, wr, ps, pr, ys, yr, hs, hr, kvs, kvr, ts, tr, zs, zr, ra, rb4, rc):
    f32, bf, i32 = jnp.float32, jnp.bfloat16, jnp.int32
    br = lax.axis_index("branch")
    seg = lax.axis_index("segment")
    z = lax.axis_index("tp")
    core, yh = lax.rem(br, 2), br // 2
    x, yl = lax.rem(seg, NX), seg // NX
    sib = br + 1 - 2 * core
    far = lax.rem(br + 2, BR)
    part_seg = lax.rem(seg + NX, SEG)
    quarter = lax.rem(z, NX)

    def xpeer(d):
        return yl * NX + lax.rem(x + d, NX)

    ld_roll = pltpu.make_async_copy(roll_hbm, roll, ld.at[0])
    ld_gain = pltpu.make_async_copy(gain_hbm, gain_v, ld.at[1])
    ld_hw = pltpu.make_async_copy(hw_hbm, hw_v, ld.at[2])
    ld_ha = pltpu.make_async_copy(ha_hbm, ha_v, ld.at[3])
    ld_w = [pltpu.make_async_copy(wkv_hbm, wA.at[yl, 0], lw.at[0])]
    for c in range(HEADS_HERE):
        ld_w.append(pltpu.make_async_copy(wq_hbm.at[:, pl.ds(c * LANES, LANES)], wA.at[yl, c + 1], lw.at[c + 1]))
    for c in [ld_roll, ld_hw, ld_gain] + ld_w + [ld_ha]:
        c.start()

    barrier = pltpu.get_barrier_semaphore()

    def greet(dev):
        pl.semaphore_signal(barrier, inc=1, device_id=dev, device_id_type=MESH)

    for d in range(1, NX):
        greet((br, xpeer(d), z))
    for d in range(NX):
        greet((far, xpeer(d), z))
    greet((br, part_seg, z))
    greet((sib, seg, z))
    greet((lax.rem(sib + 2, BR), seg, z))
    for d in (1, 2, TP - 2, TP - 1):
        greet((br, seg, lax.rem(z + d, TP)))

    drains = []

    def finish():
        for f in drains:
            f()
        drains.clear()

    sub = lax.broadcasted_iota(i32, (ROWS, LANES), 0)
    lane = lax.broadcasted_iota(i32, (ROWS, LANES), 1)
    diag = sub == lane
    src = jnp.where(sub < 64, (sub >> 3) * PIECE + (sub & 7), (sub - 64) * PIECE + 8)
    send = jnp.concatenate([send_ref[...].astype(f32), jnp.zeros((1, LANES - ROWS), f32)], axis=1)
    order = jnp.sum(jnp.where(lane == src, send, 0.0), axis=1, keepdims=True)
    order_i = order.astype(i32)
    order_row = jnp.sum(jnp.where(diag, order, 0.0), axis=0, keepdims=True).astype(i32)

    ld_roll.wait()
    xf = roll[...].astype(f32)
    r = lax.rsqrt(jnp.sum(xf * xf, axis=-1, keepdims=True) * (1.0 / D) + EPS)
    r_row = jnp.sum(jnp.where((order_row == sub) & (lane < ROWS), r, 0.0), axis=0, keepdims=True)
    hi = r_row.astype(bf).astype(f32)
    mid = (r_row - hi).astype(bf).astype(f32)
    lo = r_row - hi - mid
    s8 = lax.broadcasted_iota(i32, (8, LANES), 0)
    tail = jnp.where(s8 == 0, hi, jnp.where(s8 == 1, mid, jnp.where(s8 == 2, lo, 0.0)))
    tail = jnp.concatenate([tail] + [jnp.zeros((8, LANES), f32)] * (HK // LANES - 1), axis=1)
    perm = (order_i == lane[:, :ROWS]).astype(f32).astype(bf)
    for c in range(2 * SEG):
        yc = jnp.dot(perm, roll[:, c * HK:(c + 1) * HK], preferred_element_type=f32)
        y[c] = jnp.concatenate([yc, tail], axis=0).astype(bf)
    ld_hw.wait()
    hwf[...] = hw_v[...].astype(f32)
    for c in ld_w:
        c.wait()
    ld_gain.wait()
    ld_ha.wait()

    pl.semaphore_wait(barrier, 14)

    def spread(sem, d):
        for e in (d, TP - d):
            pl.semaphore_signal(sem, inc=1, device_id=(br, seg, lax.rem(z + e, TP)), device_id_type=MESH)

    spread(ra, 2)

    def dist(d):
        xd = lax.rem(x + d, NX)
        return pltpu.make_async_remote_copy(
            src_ref=y.at[(quarter // 2) * SEG + 2 * xd + lax.rem(quarter, 2)], dst_ref=X.at[yh, x * NX + quarter, core],
            send_sem=sd.at[d], recv_sem=xq.at[x, quarter, core], device_id=(far, yl * NX + xd, z), device_id_type=MESH)

    for d in range(NX):
        dist(d).start()

    def wsend(c):
        return pltpu.make_async_remote_copy(
            src_ref=wA.at[yl, c], dst_ref=wA.at[yl, c], send_sem=ws.at[c], recv_sem=wr.at[c],
            device_id=(br, part_seg, z), device_id_type=MESH)

    def w_next(c):
        wsend(c - 2).wait_send()
        wsend(c).start()

    wsend(0).start()

    def row_send(d, q):
        xd = lax.rem(x + d, NX)
        return pltpu.make_async_remote_copy(
            src_ref=y.at[pl.ds(q * SEG + 2 * xd, 2)], dst_ref=X.at[yh, pl.ds(x * NX + 2 * q, 2), core],
            send_sem=so.at[d, q], recv_sem=xo.at[x, core, q], device_id=(br, yl * NX + xd, z), device_id_type=MESH)

    def row_keep(q):
        return pltpu.make_async_copy(
            y.at[pl.ds(q * SEG + 2 * x, 2)], X.at[yh, pl.ds(x * NX + 2 * q, 2), core], xo.at[x, core, q])

    def row_side(d, q, src_ref):
        xs = lax.rem(x + d, NX)
        dst = X.at[yh, pl.ds(xs * NX + 2 * q, 2), core]
        return pltpu.make_async_remote_copy(
            src_ref=dst if src_ref is None else src_ref, dst_ref=dst, send_sem=fo.at[d, q],
            recv_sem=xo.at[xs, core, q], device_id=(sib, seg, z), device_id_type=MESH)

    def row_wait(d, q, c):
        xs = lax.rem(x + d, NX)
        ref = X.at[yh, pl.ds(xs * NX + 2 * q, 2), c]
        pltpu.make_async_copy(ref, ref, xo.at[xs, c, q]).wait()

    for d in (1, 3, 2):
        row_send(d, 0).start()
    for q in range(2):
        row_keep(q).start()
        row_side(0, q, y.at[pl.ds(q * SEG + 2 * x, 2)]).start()

    def hw_send(o):
        return pltpu.make_async_remote_copy(
            src_ref=hwf, dst_ref=hwb.at[br], send_sem=hs.at[o - 1], recv_sem=hr.at[br],
            device_id=(lax.rem(br + o, BR), seg, z), device_id_type=MESH)

    for o in range(1, BR):
        hw_send(o).start()

    @drains.append
    def _():
        for c in range(CHUNKS - 2, CHUNKS):
            wsend(c).wait_send()
        for d in range(1, NX):
            for q in range(2):
                row_send(d, q).wait_send()
        for q in range(2):
            row_side(0, q, y.at[pl.ds(q * SEG + 2 * x, 2)]).wait_send()
        for o in range(1, BR):
            hw_send(o).wait_send()

    rq = lax.broadcasted_iota(i32, (PACK, PACK), 0)
    rk = lax.broadcasted_iota(i32, (PACK, PACK), 1)

    def position(p):
        low = (p >= HALF).astype(i32)
        u = p - low * HALF
        left = u >= 128
        sh = jnp.where(left, u - 128, u >> 3)
        i = jnp.where(left, 8, u & 7)
        hi_row = jnp.where(sh >= 8, 1 - yh, yh)
        g = (hi_row * 2 + (sh & 1)) * SEG + low * NX + ((sh >> 1) & 3)
        return g * PIECE + i

    pq, pk = position(rq), position(rk)
    start = jnp.zeros((PACK, PACK), i32)
    end = jnp.int32(0)
    for e in range(len_ref.shape[1]):
        end = end + len_ref[0, e]
        start = jnp.where(pq >= end, end, start)
    bias[...] = jnp.where((pk >= start) & (pk <= pq), 0.0, -1e30)

    for d in range(NX):
        dist(d).wait_send()
    wsend(1).start()
    for d in (1, 3, 2):
        row_send(d, 1).start()

    other = 1 - yh

    def block(xp, q, c):
        return X.at[other, xp * NX + q, c]

    def zshare(xp, k):
        dz = (1, TP - 1, jnp.where(lax.rem(xp, 2) == 0, 2, TP - 2))[k]
        ref = block(xp, quarter, core)
        return pltpu.make_async_remote_copy(
            src_ref=ref, dst_ref=ref, send_sem=zn.at[xp, k], recv_sem=xq.at[xp, quarter, core],
            device_id=(br, seg, lax.rem(z + dz, TP)), device_id_type=MESH)

    def to_sib(xp, q):
        ref = block(xp, q, core)
        return pltpu.make_async_remote_copy(
            src_ref=ref, dst_ref=ref, send_sem=fq.at[xp, q], recv_sem=xq.at[xp, q, core],
            device_id=(sib, seg, z), device_id_type=MESH)

    def block_wait(xp, q, c):
        ref = block(xp, q, c)
        pltpu.make_async_copy(ref, ref, xq.at[xp, q, c]).wait()

    for d in (0, 1, 3, 2):
        xp = lax.rem(x + d, NX)
        block_wait(xp, quarter, core)
        for k in range(3):
            zshare(xp, k).start()
        to_sib(xp, quarter).start()
    pl.semaphore_wait(ra, 2)
    spread(rb4, 4)

    w_next(2)
    for q in range(2):
        for d in (1, 3, 2):
            row_wait(d, q, core)
            row_side(d, q, None).start()
    w_next(3)

    def norm(g, _):
        gy, gx = g // NX, lax.rem(g, NX)
        scale = []
        for c in range(2):
            row = jnp.sum(X[gy, gx * NX, c][ROWS:, :LANES].astype(f32), axis=0, keepdims=True)
            scale.append(jnp.sum(jnp.where(diag, row, 0.0), axis=-1, keepdims=True))
        for q in range(4):
            g0 = pl.multiple_of(((q // 2) * NX + x) * KS + (q % 2) * HK, HK)
            gain = gain_v[:, pl.ds(g0, HK)].astype(f32)
            v = jnp.concatenate([X[gy, gx * NX + q, c].astype(f32)[:ROWS] * scale[c] for c in range(2)], axis=0)
            N[g, :, q * HK:(q + 1) * HK] = (v * gain).astype(bf)
        return 0

    def psend(c, d, part):
        rows = pl.ds(64 * part, 64 + 16 * part)
        return pltpu.make_async_remote_copy(
            src_ref=pbuf.at[c, d - 1, :, rows], dst_ref=rbuf.at[c, d - 1, :, rows], send_sem=ps.at[c, d - 1, part],
            recv_sem=pr.at[c, d - 1, part], device_id=(br, xpeer(d), z), device_id_type=MESH)

    def ysend(c):
        return pltpu.make_async_remote_copy(
            src_ref=ybuf.at[c], dst_ref=qf.at[c, yl], send_sem=ys.at[c], recv_sem=yr.at[c],
            device_id=(br, part_seg, z), device_id_type=MESH)

    def produce(c, part):
        gy = yh if part == 0 else other
        lhs = N[pl.ds(gy * NX, NX)].reshape(NX * HALF, 2 * KS)
        acc = jnp.dot(lhs[:, :KS], wA[0, c], preferred_element_type=f32)
        acc = acc + jnp.dot(lhs[:, KS:], wA[1, c], preferred_element_type=f32)
        pf[part] = acc.reshape(8, PIECE, 8, LANES)
        left = pf[part, :, 8]
        if part == 0:
            lsave[c] = left
        else:
            left = jnp.concatenate([lsave[c], left], axis=0)
            lx = lax.broadcasted_iota(i32, (16, 8, LANES), 1)
        for d in range(NX):
            xd = lax.rem(x + d, NX)
            for k in range(2):
                s = k * NX + xd
                v = pf[part, :, s].reshape(64, LANES)
                if part:
                    v = jnp.concatenate([v, jnp.sum(jnp.where(lx == s, left, 0.0), axis=1)], axis=0)
                rows = pl.ds(64 * part, 64 + 16 * part)
                if d == 0:
                    fown[c, k, rows] = v
                else:
                    pbuf[c, d - 1, k, rows] = v.astype(bf)
            if d:
                psend(c, d, part).start()

    def consume(c):
        tot = fown[c]
        for d in range(1, NX):
            for part in range(2):
                psend(c, d, part).wait_recv()
            tot = tot + rbuf[c, d - 1].astype(f32)
        fown[c] = tot
        ybuf[c] = fown[c, 1 - yl].astype(bf)
        ysend(c).start()
        qf[c, yl] = fown[c, yl].astype(bf)

    slot = z // 8

    def kv_rows(part):
        return pl.ds(64 * part, 64 + 16 * part)

    def kv_here(k, e):
        return jnp.logical_and(k == yl, 2 * lax.rem(z, 8) + e == z)

    def kv_send(k, e, part):
        return pltpu.make_async_remote_copy(
            src_ref=kvst.at[k, kv_rows(part)], dst_ref=kvb.at[slot, yl, kv_rows(part)], send_sem=kvs.at[k, e, part],
            recv_sem=kvr.at[slot, yl, part], device_id=(br, k * NX + x, 2 * lax.rem(z, 8) + e), device_id_type=MESH)

    def kv_keep(k, part):
        return pltpu.make_async_copy(
            kvst.at[k, kv_rows(part)], kvb.at[slot, yl, kv_rows(part)], kvr.at[slot, yl, part])

    def consume_kv(part):
        rows = kv_rows(part)
        tot = fown[0, :, rows]
        for d in range(1, NX):
            psend(0, d, part).wait_recv()
            tot = tot + rbuf[0, d - 1, :, rows].astype(f32)
        kvst[:, rows] = tot.astype(bf)
        for k in range(2):
            for e in range(2):
                @pl.when(kv_here(k, e))
                def _():
                    kv_keep(k, part).start()

                @pl.when(jnp.logical_not(kv_here(k, e)))
                def _():
                    kv_send(k, e, part).start()

    pl.semaphore_wait(rb4, 2)
    pl.semaphore_signal(rc, inc=1, device_id=(br, part_seg, z), device_id_type=MESH)

    for q in range(2):
        row_wait(0, q, core)
        for d in range(NX):
            row_wait(d, q, 1 - core)

    def norm_own(g, _):
        return norm(yh * NX + g, 0)

    lax.fori_loop(0, NX, norm_own, 0)

    def early(c, _):
        wsend(c).wait_recv()
        produce(c, 0)
        return 0

    lax.fori_loop(0, 2, early, 0)

    for d in (0, 1, 3, 2):
        xp = lax.rem(x + d, NX)
        for k in (1, 3, 2):
            q = lax.rem(quarter + k, NX)
            block_wait(xp, q, core)
            to_sib(xp, q).start()
        if d == 1:
            w_next(4)
            pl.semaphore_wait(rc, 1)
            consume_kv(0)
        if d == 3:
            lax.fori_loop(2, 3, early, 0)

    @drains.append
    def _():
        for d in range(1, NX):
            for q in range(2):
                row_side(d, q, None).wait_send()
        for xp in range(NX):
            for k in range(3):
                zshare(xp, k).wait_send()
            for q in range(4):
                to_sib(xp, q).wait_send()

    for xp in range(NX):
        for q in range(4):
            block_wait(xp, q, 1 - core)

    def norm_far(g, _):
        return norm(other * NX + g, 0)

    lax.fori_loop(0, NX, norm_far, 0)

    def chunk(c, _):
        @pl.when(c >= 3)
        def _():
            wsend(c).wait_recv()
            produce(c, 0)

        produce(c, 1)

        @pl.when(c == 2)
        def _():
            consume_kv(1)

        @pl.when(c > 3)
        def _():
            consume(c - 3)
        return 0

    lax.fori_loop(0, CHUNKS, chunk, 0)

    @drains.append
    def _():
        def drain(c, _):
            for d in range(1, NX):
                for part in range(2):
                    psend(c, d, part).wait_send()

            @pl.when(c > 0)
            def _():
                ysend(c).wait_send()
            return 0

        lax.fori_loop(0, CHUNKS, drain, 0)
        for k in range(2):
            for e in range(2):
                @pl.when(jnp.logical_not(kv_here(k, e)))
                def _():
                    for part in range(2):
                        kv_send(k, e, part).wait_send()

    consume(CHUNKS - 3)
    consume(CHUNKS - 2)
    consume(CHUNKS - 1)

    for o in range(1, BR):
        frm = lax.rem(br + o, BR)
        pltpu.make_async_copy(hwb.at[frm], hwb.at[frm], hr.at[frm]).wait()
    hwb[br] = hwf[...]
    hw4 = jnp.concatenate([hwb[m] for m in range(BR)] + [jnp.zeros((4, WIDTH), f32)], axis=0).astype(bf)
    c0 = pl.multiple_of(z * WIDTH, WIDTH)
    direct = lax.dot_general(hw4, roll[:, pl.ds(c0, WIDTH)], (((1,), (1,)), ((), ())), preferred_element_type=f32)
    lanes16 = lax.broadcasted_iota(i32, (16, LANES), 1)
    table = jnp.concatenate(
        [jnp.concatenate([order_i[s * 8:(s + 1) * 8], order_i[64:72]], axis=0) == lanes16 for s in range(SEG)], axis=1)
    table = table.astype(f32).astype(bf)

    finish()
    for k in range(2):
        for h in range(2):
            for part in range(2):
                ref = kvb.at[k, h, kv_rows(part)]
                pltpu.make_async_copy(ref, ref, kvr.at[k, h, part]).wait()
    keys, values = kvb[0].reshape(PACK, LANES), kvb[1].reshape(PACK, LANES)
    acc = jnp.zeros((PACK, LANES), f32)
    for h in range(HEADS_HERE):
        ysend(h + 1).wait_recv()
        logits = lax.dot_general(qf[h + 1].reshape(PACK, LANES), keys, (((1,), (1,)), ((), ())),
                                 preferred_element_type=f32)
        logits = logits * (1.0 / math.sqrt(LANES)) + bias[...]
        expo = jnp.exp(logits - jnp.max(logits, axis=-1, keepdims=True))
        probs = (expo * (1.0 / jnp.sum(expo, axis=-1, keepdims=True))).astype(bf)
        att = jnp.dot(probs, values, preferred_element_type=f32)
        acc = acc + att * ha_v[:, h * LANES:(h + 1) * LANES].astype(f32)
    through = jnp.sum(acc, axis=-1, keepdims=True)
    sub = lax.broadcasted_iota(i32, (128, LANES), 0)
    lane = lax.broadcasted_iota(i32, (128, LANES), 1)
    for k in range(2):
        rows = through[k * HALF:(k + 1) * HALF]
        main = jnp.where((sub & 7) == lane, rows[:128], 0.0).reshape(16, 8, LANES).sum(axis=1)
        main = main + jnp.where(lane[:16] == 8 + seg, rows[128:], 0.0)
        tb[k * 16:(k + 1) * 16] = main.reshape(16, 1, LANES)

    def at(b2, s2):
        return (s2 // NX) * 16 + jnp.where(b2 // 2 == yh, 0, 8) + lax.rem(s2, NX) * 2 + lax.rem(b2, 2)

    def tsend(o, d):
        b2, s2 = lax.rem(br + o, BR), lax.rem(seg + d, SEG)
        return pltpu.make_async_remote_copy(
            src_ref=tb.at[at(b2, s2)], dst_ref=rb.at[br * SEG + seg], send_sem=ts, recv_sem=tr,
            device_id=(b2, s2, z), device_id_type=MESH)

    for o in range(BR):
        for d in range(SEG):
            if o or d:
                tsend(o, d).start()
    pltpu.make_async_copy(tb.at[at(br, seg)], rb.at[br * SEG + seg], tr).start()
    finish()
    pltpu.make_async_copy(rb, rb, tr).wait()

    @drains.append
    def _():
        pltpu.make_async_copy(tb.at[pl.ds(0, 31)], tb.at[pl.ds(0, 31)], ts).wait()

    got = rb[...].reshape(32, LANES)[:, :16]
    g_hi = got.astype(bf)
    rest = got - g_hi.astype(f32)
    g_mid = rest.astype(bf)
    g_lo = (rest - g_mid.astype(f32)).astype(bf)
    routed = jnp.dot(g_hi, table, preferred_element_type=f32)
    routed = routed + jnp.dot(g_mid, table, preferred_element_type=f32)
    routed = routed + jnp.dot(g_lo, table, preferred_element_type=f32)
    pack_of = lax.broadcasted_iota(i32, (32, LANES), 0) & 7
    part = jnp.zeros((32, LANES), f32)
    for s in range(SEG):
        part = part + jnp.where(pack_of == s, routed[:, s * LANES:(s + 1) * LANES], 0.0)
    part = part.reshape(BR, SEG, LANES).sum(axis=1)
    zo[...] = jnp.zeros((BR, LANES), f32)
    zo[:, :ROWS] = part[:, :ROWS] + direct[:BR]

    def zsend(d):
        return pltpu.make_async_remote_copy(
            src_ref=zo, dst_ref=zb.at[z], send_sem=zs, recv_sem=zr,
            device_id=(br, seg, lax.rem(z + d, TP)), device_id_type=MESH)

    for d in range(1, TP):
        zsend(d).start()
    pltpu.make_async_copy(zo, zb.at[z], zr).start()
    pltpu.make_async_copy(zb, zb, zr).wait()

    @drains.append
    def _():
        pltpu.make_async_copy(zb.at[pl.ds(0, 15)], zb.at[pl.ds(0, 15)], zs).wait()

    total = zb[0, :, :ROWS]
    for k in range(1, TP):
        total = total + zb[k, :, :ROWS]
    out_ref[...] = total
    finish()


def local(rollout, send_rows, seq_lengths, attn_gain, w_query, w_keyval, head_weight, head_attn):
    vm = pl.BlockSpec(memory_space=pltpu.VMEM)
    sm = pl.BlockSpec(memory_space=pltpu.SMEM)
    hbm = pl.BlockSpec(memory_space=pltpu.HBM)
    bf, f32, dma = jnp.bfloat16, jnp.float32, pltpu.SemaphoreType.DMA
    return pl.pallas_call(
        kernel,
        name="scores",
        out_shape=jax.ShapeDtypeStruct((BR, ROWS), f32),
        in_specs=[vm, sm] + [hbm] * 6,
        out_specs=vm,
        scratch_shapes=[
            pltpu.VMEM((ROWS, D), bf), pltpu.VMEM((1, D), bf), pltpu.VMEM((2, CHUNKS, KS, LANES), bf),
            pltpu.VMEM((1, WIDTH), bf), pltpu.VMEM((1, WIDTH), bf),
            pltpu.VMEM((2 * SEG, MSG, HK), bf),
            pltpu.VMEM((2, TP, 2, MSG, HK), bf),
            pltpu.VMEM((8, HALF, 2 * KS), bf),
            pltpu.VMEM((2, 8, PIECE, 8, LANES), f32),
            pltpu.VMEM((CHUNKS, 8, 8, LANES), f32),
            pltpu.VMEM((CHUNKS, 3, 2, HALF, LANES), bf),
            pltpu.VMEM((CHUNKS, 3, 2, HALF, LANES), bf),
            pltpu.VMEM((CHUNKS, 2, HALF, LANES), f32),
            pltpu.VMEM((CHUNKS, HALF, LANES), bf),
            pltpu.VMEM((CHUNKS, 2, HALF, LANES), bf),
            pltpu.VMEM((2, HALF, LANES), bf), pltpu.VMEM((2, 2, HALF, LANES), bf),
            pltpu.VMEM((1, WIDTH), f32), pltpu.VMEM((BR, 1, WIDTH), f32),
            pltpu.VMEM((PACK, PACK), f32),
            pltpu.VMEM((32, 1, LANES), f32), pltpu.VMEM((32, 1, LANES), f32),
            pltpu.VMEM((BR, LANES), f32), pltpu.VMEM((TP, BR, LANES), f32),
            dma((4,)), dma((CHUNKS,)), dma((NX, 2, 2)), dma((NX, 4, 2)), dma((NX, 2)), dma((NX,)),
            dma((NX, 2)), dma((NX, 4)), dma((NX, 3)), dma((CHUNKS,)), dma((CHUNKS,)),
            dma((CHUNKS, 3, 2)), dma((CHUNKS, 3, 2)), dma((CHUNKS,)), dma((CHUNKS,)),
            dma((3,)), dma((BR,)), dma((2, 2, 2)), dma((2, 2, 2)), dma, dma, dma, dma,
            pltpu.SemaphoreType.REGULAR, pltpu.SemaphoreType.REGULAR, pltpu.SemaphoreType.REGULAR,
        ],
        compiler_params=pltpu.CompilerParams(
            collective_id=0, has_side_effects=True, vmem_limit_bytes=56 << 20),
    )(send_rows.reshape(1, ROWS), seq_lengths, rollout, attn_gain, w_query[0], w_keyval[0], head_weight, head_attn)


def solution(mesh):
    return jax.shard_map(
        local,
        mesh=mesh,
        in_specs=(
            P(("branch", "segment"), None),
            P(("branch", "segment")),
            P("segment", None),
            P("branch", None),
            P("branch", "segment", "tp"),
            P("branch", "segment", "tp"),
            P("branch", "tp"),
            P("branch", "tp"),
        ),
        out_specs=P(None, ("branch", "segment")),
        check_vma=False,
    )
```
